32 devices in a mesh: groups: 2 (over x), req: 4 (over y, core), fsdp: 4 (over z).
Axes of the slice: x: 2, y: 2, z: 4, core: 2. Of those that a mesh axis runs over, the one named last changes fastest.
Arguments:
- tokens: bfloat16 [2, 128, 8, 2048], P(None, ('groups', 'req', 'fsdp')), parts along dimension 1, may hold values from -6 to 6
- in_weight: bfloat16 [2048, 4224], P(('req', 'fsdp')), may hold values from -0.125 to 0.125
- dt_weight: bfloat16 [2048, 64], P(('req', 'fsdp')), may hold values from -0.125 to 0.125
- conv_weight: float32 [4, 4224], replicated, may hold values from -3 to 3
- conv_bias: float32 [4224], replicated, may hold values from -3 to 3
- dt_bias: float32 [64], replicated, may hold values from -2 to 1
- decay_rate: float32 [64], replicated, may hold values from 0.004 to 0.3
- skip_gain: float32 [64], replicated, may hold values from 0.5 to 1.5
- norm_gain: float32 [4096], replicated, may hold values from 0.5 to 1.5
- state_cache: bfloat16 [256, 64, 4096], P(('groups', 'req', 'fsdp')), parts along dimension 0, may hold values from -6 to 6
- conv_cache: bfloat16 [256, 3, 4224], P(('groups', 'req', 'fsdp')), parts along dimension 0, may hold values from -6 to 6
- hash_owner: int32 [128], P(('groups', 'req', 'fsdp')), parts along dimension 0, may hold values from 0 to 3, as said below
- cache_slot: int32 [128], P(('groups', 'req', 'fsdp')), parts along dimension 0, may hold values from 0 to 7, as said below
- event_counts: int32 [2, 128], P(None, ('groups', 'req', 'fsdp')), parts along dimension 1, may hold values from 1 to 8
Outputs:
- user_vectors: bfloat16 [2, 128, 4096], P(None, ('groups', 'req', 'fsdp')), parts along dimension 1
- new_states: bfloat16 [256, 64, 4096], P(('groups', 'req', 'fsdp')), parts along dimension 0
- new_windows: bfloat16 [256, 3, 4224], P(('groups', 'req', 'fsdp')), parts along dimension 0
The draws below stay inside these ranges and needn't reach their ends.
There are 2 independent parts, one for each index of `groups`. The reference program is written for one: setup_inputs(seed, part) draws one part's arguments, and reference() takes and returns one part's arrays. A program takes and returns all parts, laid end to end along the dimension named above; an argument that names none is the same for every part. Nothing has to cross between parts.
Inputs may be any that keep to these rules, and one draw needn't show every extreme that they name: `hash_owner`: among the users of one device at most 2 have the same owner, and some device has exactly 2 users of one owner. Among the users of all devices with one fsdp index at most 8 have the same owner, and some owner has exactly 8. `cache_slot`: users of one fsdp index with the same owner have distinct rows.
All inputs are finite; a program needn't handle non-finite values.
Results may differ from the reference program's by a relative error of at most 0.006.
Values may be sent and summed in bfloat16 or wider, within the bound.
A program may use at most 192 MiB of HBM per device.

```python
import math
import jax
import jax.numpy as jnp
from jax import lax

D = 2048
HEADS = 64
HEAD_DIM = 64
STATE = 64
KCONV = 4
STEPS = 2
USERS_DEV = 4
EV = 8
INNER = 4096
CONV_CH = 4224
CACHE = 8
USERS = 64
SLOTS = 128
N_REQ = 4
N_FSDP = 4


def owner_table(key):
    owners = N_REQ
    columns = N_FSDP
    per_device = USERS_DEV
    base_key = jax.random.fold_in(key, 7)
    key_perm, key_shift, key_order, key_slot = jax.random.split(base_key, 4)
    base_hot = 2 * per_device // owners
    extra_hot = 2 * per_device % owners
    req_index = jnp.arange(owners, dtype=jnp.int32)
    hot_count = base_hot + (req_index < extra_hot).astype(jnp.int32)
    position = jnp.arange(per_device, dtype=jnp.int32)
    shift = jax.random.randint(key_shift, (columns,), 0, max(owners - 1, 1)).astype(jnp.int32)
    remainder = position[None, None, :] - hot_count[:, None, None]
    label_rest = 1 + (req_index[:, None, None] + shift[None, :, None] + jnp.maximum(remainder, 0) // 2) % (owners - 1)
    label = jnp.where(remainder < 0, 0, label_rest)
    relabel = jax.vmap(lambda one_key: jax.random.permutation(one_key, owners))(jax.random.split(key_perm, columns)).astype(jnp.int32)
    column_index = jnp.arange(columns, dtype=jnp.int32)
    owner_grid = relabel[column_index[None, :, None], label]
    order = jax.vmap(lambda one_key: jax.random.permutation(one_key, per_device))(jax.random.split(key_order, owners * columns)).astype(jnp.int32)
    order = order.reshape(owners, columns, per_device)
    owner_grid = jnp.take_along_axis(owner_grid, order, axis=2)
    column_major = owner_grid.transpose(1, 0, 2).reshape(columns, owners * per_device)
    matches = (column_major[:, :, None] == jnp.arange(owners, dtype=jnp.int32)[None, None, :]).astype(jnp.int32)
    earlier = jnp.cumsum(matches, axis=1) - matches
    ranking = jnp.sum(earlier * matches, axis=2)
    slot_perm = jax.vmap(lambda one_key: jax.random.permutation(one_key, CACHE))(jax.random.split(key_slot, columns * owners)).astype(jnp.int32)
    slot_perm = slot_perm.reshape(columns, owners, CACHE)
    slot_column = slot_perm[column_index[:, None], column_major, ranking]
    slot_grid = slot_column.reshape(columns, owners, per_device).transpose(1, 0, 2)
    return (owner_grid.reshape(-1).astype(jnp.int32), slot_grid.reshape(-1).astype(jnp.int32))


def draw_hash_owner(key, part):
    return owner_table(key)[0]


def draw_cache_slot(key, part):
    return owner_table(key)[1]


def with_ends(drawn, rng, smallest, largest):
    extent = drawn.shape
    index_at = [jax.random.randint(jax.random.fold_in(rng, axis), (), 0, extent[axis]) for axis in range(len(extent))]
    drawn = drawn.at[tuple(index_at)].set(smallest)
    longest = extent.index(max(extent))
    index_at[longest] = (index_at[longest] + 1) % extent[longest]
    return drawn.at[tuple(index_at)].set(largest)


def level_of(rng, dims, cuts, smallest, high):
    level, own = 1.0, jax.random.fold_in(rng, 6)
    for axis_at, blocks in cuts:
        draws = jnp.exp(jax.random.uniform(jax.random.fold_in(own, axis_at), (blocks,), jnp.float32, smallest / len(cuts), high / len(cuts)))
        level = level * jnp.repeat(draws, dims[axis_at] // blocks).reshape([-1 if axis == axis_at else 1 for axis in range(len(dims))])
    return level


def gaussian(own_key, shape, deviation, reach, shards=(), kind=jnp.bfloat16):
    array = jax.random.normal(own_key, shape, jnp.float32) * deviation
    if len(shards) > 0:
        array = level_of(own_key, shape, shards, -0.22, 0.18) * array
    return jnp.clip(array, min=-reach, max=reach).astype(kind)


def setup_inputs(seed: int = 0, part: int = 0) -> dict:
    streams_of = jax.random.split(jax.random.key(seed), 15)
    part_keys = jax.random.split(jax.random.fold_in(streams_of[14], part), 15)
    tokens = gaussian(part_keys[0], (STEPS, USERS, EV, D), 1.0, 6.0, ((1, 16),))
    in_weight = gaussian(streams_of[1], (D, CONV_CH), D ** -0.5, 0.125, ((0, 16),))
    dt_weight = gaussian(streams_of[2], (D, HEADS), D ** -0.5, 0.125, ((0, 16),))
    conv_weight = gaussian(streams_of[3], (KCONV, CONV_CH), KCONV ** -0.5, 3.0, (), jnp.float32)
    conv_bias = gaussian(streams_of[4], (CONV_CH,), 0.5, 3.0, (), jnp.float32)
    dt_bias = jnp.clip(jax.random.uniform(streams_of[5], (HEADS,), jnp.float32, -2.0, 1.0), -2.0, 1.0)
    decay_rate = jnp.clip(jnp.exp(jax.random.uniform(streams_of[6], (HEADS,), jnp.float32, math.log(0.004), math.log(0.3))), 0.004, 0.3)
    skip_gain = jnp.clip(jax.random.uniform(streams_of[7], (HEADS,), jnp.float32, 0.5, 1.5), 0.5, 1.5)
    norm_gain = jnp.clip(1.0 + 0.1 * jax.random.normal(streams_of[8], (INNER,), jnp.float32), 0.5, 1.5)
    state_cache = gaussian(part_keys[9], (SLOTS, HEADS, HEAD_DIM * STATE), 1.0, 6.0, ((0, 16),))
    conv_cache = gaussian(part_keys[10], (SLOTS, KCONV - 1, CONV_CH), 1.0, 6.0, ((0, 16),))
    hash_owner = draw_hash_owner(jax.random.fold_in(jax.random.fold_in(streams_of[14], part), 71), part)
    cache_slot = draw_cache_slot(jax.random.fold_in(jax.random.fold_in(streams_of[14], part), 71), part)
    event_counts = with_ends(jax.random.randint(part_keys[13], (STEPS, USERS), 1, EV + 1), jax.random.fold_in(part_keys[13], 1), 1, EV).astype(jnp.int32)
    return {"tokens": tokens, "in_weight": in_weight, "dt_weight": dt_weight, "conv_weight": conv_weight, "conv_bias": conv_bias, "dt_bias": dt_bias, "decay_rate": decay_rate, "skip_gain": skip_gain, "norm_gain": norm_gain, "state_cache": state_cache, "conv_cache": conv_cache, "hash_owner": hash_owner, "cache_slot": cache_slot, "event_counts": event_counts}


def advance(projected, dt_raw, counts, state, window, conv_weight, conv_bias, dt_bias, decay_rate, skip_gain, norm_gain):
    users = projected.shape[0]
    length = projected.shape[1]
    kernel = conv_weight.shape[0]
    extended = jnp.concatenate([window, projected], axis=1)
    ext_float = extended.astype(jnp.float32)
    conv_sum = conv_bias + conv_weight[0] * ext_float[:, 0:length]
    for tap in range(1, kernel):
        conv_sum = conv_sum + conv_weight[tap] * ext_float[:, tap:tap + length]
    active = jax.nn.silu(conv_sum)
    inner = active.shape[-1] - 2 * STATE
    inputs = active[..., :inner].reshape(users, length, HEADS, HEAD_DIM)
    write_vec = active[..., inner:inner + STATE]
    read_vec = active[..., inner + STATE:]
    positions = jnp.arange(length, dtype=jnp.int32)
    valid = (positions[None, :] < counts[:, None]).astype(jnp.float32)
    step_size = jax.nn.softplus(dt_raw.astype(jnp.float32) + dt_bias) * valid[:, :, None]
    cumulative = jnp.cumsum(-decay_rate * step_size, axis=1)
    total_log = cumulative[:, -1]
    weighting = jnp.exp(total_log[:, None, :] - cumulative) * step_size
    weighted = weighting[..., None] * inputs
    update = jnp.einsum('uthp,utn->uhpn', weighted, write_vec, precision=lax.Precision.HIGHEST)
    new_state = jnp.exp(total_log)[:, :, None, None] * state + update
    last_pick = (positions[None, :] == counts[:, None] - 1).astype(jnp.float32)
    last_input = jnp.einsum('ut,uthp->uhp', last_pick, inputs, precision=lax.Precision.HIGHEST)
    last_read = jnp.einsum('ut,utn->un', last_pick, read_vec, precision=lax.Precision.HIGHEST)
    mixed = lax.optimization_barrier(jnp.sum(new_state * last_read[:, None, None, :], axis=-1))
    mixed = (mixed + skip_gain[:, None] * last_input).reshape(users, -1)
    inv_rms = lax.rsqrt(lax.optimization_barrier(jnp.mean(mixed * mixed, axis=-1, keepdims=True)) + 1e-05)
    result = (mixed * inv_rms * norm_gain).astype(jnp.bfloat16)
    window_rows = counts[:, None] + jnp.arange(kernel - 1, dtype=jnp.int32)[None, :]
    new_window = jnp.take_along_axis(extended, window_rows[:, :, None], axis=1)
    return (result, new_state, new_window)

def reference(tokens, in_weight, dt_weight, conv_weight, conv_bias, dt_bias, decay_rate, skip_gain, norm_gain, state_cache, conv_cache, hash_owner, cache_slot, event_counts):
    blocks = N_REQ * N_FSDP
    user_index = jnp.arange(USERS, dtype=jnp.int32)
    column = user_index // USERS_DEV % N_FSDP
    cache_row = ((hash_owner * N_FSDP + column) * CACHE + cache_slot).astype(jnp.int32)
    width = in_weight.shape[1]

    def one_device(block):
        start = (block * USERS_DEV).astype(jnp.int32)
        tok_block = lax.dynamic_slice_in_dim(tokens, start, USERS_DEV, 1)
        count_block = lax.dynamic_slice_in_dim(event_counts, start, USERS_DEV, 1)
        rows_block = lax.dynamic_slice_in_dim(cache_row, start, USERS_DEV, 0)
        flat_tokens = tok_block.reshape(-1, D)
        proj_in = jnp.dot(flat_tokens, in_weight, preferred_element_type=jnp.float32).astype(jnp.bfloat16)
        proj_in = proj_in.reshape(STEPS, USERS_DEV, EV, width)
        proj_dt = jnp.dot(flat_tokens, dt_weight, preferred_element_type=jnp.float32).astype(jnp.bfloat16)
        proj_dt = proj_dt.reshape(STEPS, USERS_DEV, EV, HEADS)
        state = state_cache[rows_block].astype(jnp.float32).reshape(USERS_DEV, HEADS, HEAD_DIM, STATE)
        window = conv_cache[rows_block]
        results = []
        for step in range(STEPS):
            result, state, window = advance(proj_in[step], proj_dt[step], count_block[step], state, window, conv_weight, conv_bias, dt_bias, decay_rate, skip_gain, norm_gain)
            results.append(result)
        final_state = state.reshape(USERS_DEV, HEADS, HEAD_DIM * STATE).astype(jnp.bfloat16)
        return (jnp.stack(results), final_state, window)
    outputs, states, windows = lax.map(one_device, jnp.arange(blocks, dtype=jnp.int32))
    user_vectors = outputs.transpose(1, 0, 2, 3).reshape(STEPS, USERS, -1)
    new_states = state_cache.at[cache_row].set(states.reshape(USERS, HEADS, HEAD_DIM * STATE))
    new_windows = conv_cache.at[cache_row].set(windows.reshape(USERS, KCONV - 1, width))
    return (user_vectors, new_states, new_windows)
```

```python
import functools

import jax
import jax.numpy as jnp
import numpy as np
from jax import lax
from jax.experimental import pallas as pl
from jax.experimental.pallas import tpu as pltpu
from jax.sharding import PartitionSpec as P

HEADS = 64
HEAD_DIM = 64
STATE = 64
STEPS = 2
EV = 8
EVENTS = STEPS * EV
INNER = HEADS * HEAD_DIM
LANES = 128
GROUP = 8
SLOTS_PER_PAIR = 2


def order_matrix():
    out = np.zeros((EVENTS * HEAD_DIM, EVENTS * HEAD_DIM), np.float32)
    t, p = np.meshgrid(np.arange(EVENTS), np.arange(HEAD_DIM), indexing="ij")
    out[t * HEAD_DIM + p, p * EVENTS + t] = 1.0
    return jnp.asarray(out, jnp.bfloat16)


def serve_kernel(
    channels,
    meta_ref,
    proj_ref,
    state_hbm,
    window_ref,
    cw_ref,
    cb_ref,
    head_ref,
    gain_ref,
    order_ref,
    new_state_hbm,
    new_window_ref,
    y_ref,
    state_buf,
    ext,
    stacked,
    table,
    columns,
    a_rows,
    a_sorted,
    y_part,
    b_save,
    row_item,
    in_sems,
    out_sems,
):
    cached = state_buf.shape[0]
    items = proj_ref.shape[0]
    f32, bf16 = jnp.float32, jnp.bfloat16

    def state_in(u):
        return pltpu.make_async_copy(state_hbm.at[u], state_buf.at[u], in_sems.at[u])

    def state_out(u):
        return pltpu.make_async_copy(state_buf.at[u], new_state_hbm.at[u], out_sems.at[u])

    for u in range(cached):
        state_in(u).start()
    for u in range(cached):
        found = jnp.int32(-1)
        for i in range(items):
            found = jnp.where(meta_ref[i // SLOTS_PER_PAIR, i % SLOTS_PER_PAIR, 0] == u, i, found)
        row_item[u] = found

    left = lax.broadcasted_iota(jnp.int32, (1, LANES), 1) < 64
    row8 = lax.broadcasted_iota(jnp.int32, (EV, 1), 0)
    y_ref[...] = jnp.zeros(y_ref.shape, y_ref.dtype)
    table[...] = jnp.zeros(table.shape, f32)

    def lift(u, carry):
        item = row_item[u]

        @pl.when(item < 0)
        def _():
            new_window_ref[u] = window_ref[u]
            a_rows[pl.ds(pl.multiple_of(u * HEADS, HEADS), HEADS), :] = jnp.zeros(
                (HEADS, EVENTS * HEAD_DIM), bf16
            )

        @pl.when(item >= 0)
        def _():
            pair, place = item // SLOTS_PER_PAIR, item % SLOTS_PER_PAIR
            counts = [meta_ref[pair, place, 1], meta_ref[pair, place, 2]]
            ext[0, 5:8, :] = window_ref[u].astype(f32)
            proj = proj_ref[item].astype(f32)
            actives = []
            for s in range(STEPS):
                ext[s, 8:16, :] = proj[s * EV : (s + 1) * EV, :channels]
                conv = cb_ref[...] + cw_ref[0:1, :] * ext[s, 5:13, :]
                for tap in range(1, 4):
                    conv = conv + cw_ref[tap : tap + 1, :] * ext[s, 5 + tap : 13 + tap, :]
                actives.append(conv * (1.0 / (1.0 + jnp.exp(-conv))))
                rolled = pltpu.roll(ext[s], 16 - counts[s], 0)
                if s + 1 < STEPS:
                    ext[s + 1, 0:8, :] = rolled[0:8]
                else:
                    new_window_ref[u] = rolled[5:8].astype(bf16)
            dt_bias, decay, skip = head_ref[0:1, :], head_ref[1:2, :], head_ref[2:3, :]
            weights, totals, reads, writes, picks = [], [], [], [], []
            for s in range(STEPS):
                raw = proj[s * EV : (s + 1) * EV, channels : channels + HEADS] + dt_bias
                size = jnp.maximum(raw, 0.0) + jnp.log1p(jnp.exp(-jnp.abs(raw)))
                size = jnp.where(row8 < counts[s], size, 0.0)
                cum = -decay * size
                for shift in (1, 2, 4):
                    cum = cum + jnp.where(row8 >= shift, pltpu.roll(cum, shift, 0), 0.0)
                total = cum[EV - 1 : EV, :]
                totals.append(total)
                weights.append(jnp.exp(total - cum) * size)
                picks.append((row8 == counts[s] - 1).astype(f32))
                writes.append(actives[s][:, INNER : INNER + STATE])
                reads.append(
                    jnp.sum(
                        picks[s] * actives[s][:, INNER + STATE : INNER + 2 * STATE],
                        axis=0,
                        keepdims=True,
                    )
                )
            carried = weights[0] * jnp.exp(totals[1])

            def gram(s, e):
                return jnp.sum(writes[e] * reads[s], axis=1, keepdims=True)

            table[0:8, 0:64] = weights[0] * gram(0, 0) + picks[0] * skip
            table[8:16, 0:64] = carried * gram(1, 0)
            table[16:24, 0:64] = weights[1] * gram(1, 1) + picks[1] * skip
            table[24:32, 0:64] = carried
            table[32:40, 0:64] = weights[1]
            table[40:41, 0:64] = jnp.exp(totals[0])
            table[41:42, 0:64] = jnp.exp(totals[0] + totals[1])
            table[42:43, 0:64] = reads[0]
            table[43:44, 0:64] = reads[1]
            cols = table[...].T[0:64]
            columns[u] = cols
            for s in range(STEPS):
                b_save[u, s * EV : (s + 1) * EV, :] = jnp.concatenate([writes[s], writes[s]], axis=1)
                for j in range(INNER // LANES):
                    x = actives[s][:, j * LANES : (j + 1) * LANES]
                    turned = pltpu.roll(x, 64, 1)
                    at = 2 * j * EVENTS + s * EV
                    stacked[at : at + EV, :] = jnp.where(left, x, turned)
                    stacked[at + EVENTS : at + EVENTS + EV, :] = jnp.where(left, turned, x)
            rows = pl.ds(pl.multiple_of(u * HEADS, HEADS), HEADS)
            part = jnp.zeros((HEADS, LANES), f32)
            for t in range(0, EVENTS, 2):
                pieces = []
                for e in (t, t + 1):
                    z = stacked[pl.ds(e, HEADS, stride=EVENTS), :]
                    second = cols[:, 8 + e : 9 + e]
                    if e < EV:
                        coef = jnp.where(left, cols[:, e : e + 1], second)
                    else:
                        coef = jnp.where(left, 0.0, second)
                    part = part + coef * z
                    pieces.append(cols[:, 24 + e : 25 + e] * z)
                a_rows[rows, t * HEAD_DIM : (t + 2) * HEAD_DIM] = jnp.where(
                    left, pieces[0], pieces[1]
                ).astype(bf16)
            y_part[u] = part

        return carry

    lax.fori_loop(0, cached, lift, 0)

    def arrange(q, carry):
        at = pl.ds(pl.multiple_of(q * LANES, LANES), LANES)
        a_sorted[q] = jnp.dot(
            a_rows[...], order_ref[:, at], preferred_element_type=f32
        ).astype(bf16)
        return carry

    lax.fori_loop(0, GROUP, arrange, 0)

    wide = GROUP * STATE
    block = lax.broadcasted_iota(jnp.int32, (GROUP * EVENTS, wide), 0) // EVENTS == (
        lax.broadcasted_iota(jnp.int32, (GROUP * EVENTS, wide), 1) // STATE
    )
    lane64 = lax.broadcasted_iota(jnp.int32, (1, LANES), 1) % 64

    def finish(u, carry):
        item = row_item[u]
        state_in(u).wait()

        @pl.when(item >= 0)
        def _():
            cols = columns[u]
            b = b_save[u]
            b_wide = jnp.concatenate([b] * (wide // LANES), axis=1)
            b_block = jnp.where(block, jnp.concatenate([b_wide] * GROUP, axis=0), 0.0).astype(bf16)
            lhs = a_sorted[:, pl.ds(pl.multiple_of(u * HEADS, HEADS), HEADS), :].reshape(
                GROUP * HEADS, LANES
            )
            update = jnp.dot(lhs, b_block, preferred_element_type=f32)
            read = jnp.where(left, cols[:, 42:43], cols[:, 43:44])
            decay = cols[:, 41:42]
            from_old = jnp.where(left, cols[:, 40:41], decay)
            total = jnp.zeros((HEADS, LANES), f32)
            for q in range(HEAD_DIM // GROUP):
                old = state_buf[u, :, q * wide : (q + 1) * wide]
                read_block = jnp.concatenate(
                    [jnp.where(lane64 == q * GROUP + i, read, 0.0) for i in range(GROUP)], axis=0
                ).astype(bf16)
                total = total + jnp.dot(old, read_block, preferred_element_type=f32)
                state_buf[u, :, q * wide : (q + 1) * wide] = (
                    decay * old.astype(f32) + update[q * HEADS : (q + 1) * HEADS]
                ).astype(bf16)
            y = from_old * total + y_part[u]
            square = jnp.sum(y * y, axis=0, keepdims=True)
            first = jnp.sum(jnp.where(left, square, 0.0), axis=1, keepdims=True)
            second = jnp.sum(jnp.where(left, 0.0, square), axis=1, keepdims=True)
            inverse = lax.rsqrt(jnp.where(left, first, second) * (1.0 / INNER) + 1e-05)
            y_ref[item] = (y * inverse * gain_ref[...]).astype(bf16)

        state_out(u).start()
        return carry

    lax.fori_loop(0, cached, finish, 0)
    for u in range(cached):
        state_out(u).wait()


def serve(meta, proj, state, window, conv_weight, conv_bias, dt_bias, decay_rate, skip_gain, norm_gain):
    cached = state.shape[0]
    items, _, width = proj.shape
    channels = window.shape[2]
    heads = jnp.stack([dt_bias, decay_rate, skip_gain])
    gain = norm_gain.reshape(HEADS, HEAD_DIM)
    gain = jnp.concatenate([gain, gain], axis=1)
    vmem = pl.BlockSpec(memory_space=pltpu.VMEM)
    hbm = pl.BlockSpec(memory_space=pl.ANY)
    return pl.pallas_call(
        functools.partial(serve_kernel, channels),
        in_specs=[pl.BlockSpec(memory_space=pltpu.SMEM), vmem, hbm] + [vmem] * 6,
        out_specs=[hbm, vmem, vmem],
        out_shape=[
            jax.ShapeDtypeStruct(state.shape, jnp.bfloat16),
            jax.ShapeDtypeStruct(window.shape, jnp.bfloat16),
            jax.ShapeDtypeStruct((items, HEADS, LANES), jnp.bfloat16),
        ],
        scratch_shapes=[
            pltpu.VMEM(state.shape, jnp.bfloat16),
            pltpu.VMEM((STEPS, 16, channels), jnp.float32),
            pltpu.VMEM((HEADS * EVENTS, LANES), jnp.float32),
            pltpu.VMEM((LANES, LANES), jnp.float32),
            pltpu.VMEM((cached, HEADS, LANES), jnp.float32),
            pltpu.VMEM((cached * HEADS, EVENTS * HEAD_DIM), jnp.bfloat16),
            pltpu.VMEM((GROUP, cached * HEADS, LANES), jnp.bfloat16),
            pltpu.VMEM((cached, HEADS, LANES), jnp.float32),
            pltpu.VMEM((cached, EVENTS, LANES), jnp.float32),
            pltpu.SMEM((cached,), jnp.int32),
            pltpu.SemaphoreType.DMA((cached,)),
            pltpu.SemaphoreType.DMA((cached,)),
        ],
        compiler_params=pltpu.CompilerParams(vmem_limit_bytes=48 * 2**20),
        cost_estimate=pl.CostEstimate(flops=6 * 10**9, bytes_accessed=10**7, transcendentals=10**6),
        name="serve",
    )(meta, proj, state, window, conv_weight, conv_bias[None], heads, gain, order_matrix())


def user_places(hash_owner, owners):
    users = hash_owner.shape[0]
    index = jnp.arange(users, dtype=jnp.int32)
    same = (hash_owner[:, None] == hash_owner[None, :]) & (index[None, :] < index[:, None])
    rank = jnp.sum(same.astype(jnp.int32), axis=1)
    return (hash_owner[None, None, :] == jnp.arange(owners, dtype=jnp.int32)[:, None, None]) & (
        rank[None, None, :] == jnp.arange(SLOTS_PER_PAIR, dtype=jnp.int32)[None, :, None]
    )


def on_device(
    tokens,
    in_weight,
    dt_weight,
    conv_weight,
    conv_bias,
    dt_bias,
    decay_rate,
    skip_gain,
    norm_gain,
    state_cache,
    conv_cache,
    hash_owner,
    cache_slot,
    event_counts,
):
    owners = lax.axis_size("req")
    users = tokens.shape[1]
    model = tokens.shape[3]
    pad = jnp.zeros((in_weight.shape[0], LANES - HEADS), jnp.bfloat16)
    both = jnp.concatenate([in_weight, dt_weight, pad], axis=1)
    full = lax.all_gather(both, ("req", "fsdp"), axis=0, tiled=True)
    places = user_places(hash_owner, owners)
    orders = jnp.stack([cache_slot + 1, event_counts[0], event_counts[1]], axis=1)
    meta = jnp.sum(jnp.where(places[..., None], orders[None, None], 0), axis=2)
    meta = meta - jnp.array([1, 0, 0], jnp.int32)
    arrived = lax.all_to_all(meta, "req", split_axis=0, concat_axis=0, tiled=True)
    rows = tokens.transpose(1, 0, 2, 3).reshape(users, EVENTS * model)
    picked = jnp.dot(
        places.reshape(-1, users).astype(jnp.bfloat16), rows, preferred_element_type=jnp.float32
    ).astype(jnp.bfloat16)
    picked = picked.reshape(owners, SLOTS_PER_PAIR * EVENTS, model)
    came = lax.all_to_all(picked, "req", split_axis=0, concat_axis=0, tiled=True)
    proj = jnp.dot(came.reshape(-1, model), full, preferred_element_type=jnp.float32).astype(
        jnp.bfloat16
    )
    proj = proj.reshape(owners * SLOTS_PER_PAIR, EVENTS, -1)
    new_state, new_window, y = serve(
        arrived,
        proj,
        state_cache,
        conv_cache,
        conv_weight,
        conv_bias,
        dt_bias,
        decay_rate,
        skip_gain,
        norm_gain,
    )
    y = y.reshape(owners, SLOTS_PER_PAIR, HEADS * LANES)
    back = lax.all_to_all(y, "req", split_axis=0, concat_axis=0, tiled=True)
    chosen = jnp.max(
        jnp.where(places[..., None], back[:, :, None, :].astype(jnp.float32), -jnp.inf), axis=(0, 1)
    ).astype(jnp.bfloat16)
    chosen = chosen.reshape(users, HEADS, STEPS, HEAD_DIM)
    user_vectors = chosen.transpose(2, 0, 1, 3).reshape(STEPS, users, INNER)
    return (user_vectors, new_state, new_window)


def solution(mesh):
    split = ("groups", "req", "fsdp")
    in_specs = (
        P(None, split, None, None),
        P(("req", "fsdp"), None),
        P(("req", "fsdp"), None),
        P(),
        P(),
        P(),
        P(),
        P(),
        P(),
        P(split, None, None),
        P(split, None, None),
        P(split),
        P(split),
        P(None, split),
    )
    out_specs = (P(None, split, None), P(split, None, None), P(split, None, None))
    return jax.shard_map(
        on_device, mesh=mesh, in_specs=in_specs, out_specs=out_specs, check_vma=False
    )
```

```python
import functools

import jax
import jax.numpy as jnp
import numpy as np
from jax import lax
from jax.experimental import pallas as pl
from jax.experimental.pallas import tpu as pltpu
from jax.sharding import PartitionSpec as P

HEADS = 64
HEAD_DIM = 64
STATE = 64
STEPS = 2
EV = 8
EVENTS = STEPS * EV
INNER = HEADS * HEAD_DIM
LANES = 128
GROUP = 8
SLOTS_PER_PAIR = 2


def order_matrix():
    out = np.zeros((EVENTS * HEAD_DIM, EVENTS * HEAD_DIM), np.float32)
    t, p = np.meshgrid(np.arange(EVENTS), np.arange(HEAD_DIM), indexing="ij")
    out[t * HEAD_DIM + p, p * EVENTS + t] = 1.0
    return jnp.asarray(out, jnp.bfloat16)


def serve_kernel(
    channels,
    meta_ref,
    proj_ref,
    state_hbm,
    window_ref,
    cw_ref,
    cb_ref,
    head_ref,
    gain_ref,
    order_ref,
    new_state_hbm,
    new_window_ref,
    y_ref,
    state_buf,
    ext,
    stacked,
    table,
    columns,
    a_rows,
    a_sorted,
    y_part,
    b_save,
    row_item,
    in_sems,
    out_sems,
):
    cached = state_buf.shape[0]
    items = proj_ref.shape[0]
    f32, bf16 = jnp.float32, jnp.bfloat16

    def state_in(u):
        return pltpu.make_async_copy(state_hbm.at[u], state_buf.at[u], in_sems.at[u])

    def state_out(u):
        return pltpu.make_async_copy(state_buf.at[u], new_state_hbm.at[u], out_sems.at[u])

    for u in range(cached):
        state_in(u).start()
    for u in range(cached):
        found = jnp.int32(-1)
        for i in range(items):
            found = jnp.where(meta_ref[i // SLOTS_PER_PAIR, i % SLOTS_PER_PAIR, 0] == u + 1, i, found)
        row_item[u] = found

    left = lax.broadcasted_iota(jnp.int32, (1, LANES), 1) < 64
    row8 = lax.broadcasted_iota(jnp.int32, (EV, 1), 0)
    y_ref[...] = jnp.zeros(y_ref.shape, y_ref.dtype)
    table[...] = jnp.zeros(table.shape, f32)

    def lift(u, carry):
        item = row_item[u]

        @pl.when(item < 0)
        def _():
            new_window_ref[u] = window_ref[u]
            a_rows[pl.ds(pl.multiple_of(u * HEADS, HEADS), HEADS), :] = jnp.zeros(
                (HEADS, EVENTS * HEAD_DIM), bf16
            )

        @pl.when(item >= 0)
        def _():
            pair, place = item // SLOTS_PER_PAIR, item % SLOTS_PER_PAIR
            counts = [meta_ref[pair, place, 1], meta_ref[pair, place, 2]]
            ext[0, 5:8, :] = window_ref[u].astype(f32)
            proj = proj_ref[item].astype(f32)
            actives = []
            for s in range(STEPS):
                ext[s, 8:16, :] = proj[s * EV : (s + 1) * EV, :channels]
                conv = cb_ref[...] + cw_ref[0:1, :] * ext[s, 5:13, :]
                for tap in range(1, 4):
                    conv = conv + cw_ref[tap : tap + 1, :] * ext[s, 5 + tap : 13 + tap, :]
                actives.append(conv * (1.0 / (1.0 + jnp.exp(-conv))))
                rolled = pltpu.roll(ext[s], 16 - counts[s], 0)
                if s + 1 < STEPS:
                    ext[s + 1, 0:8, :] = rolled[0:8]
                else:
                    new_window_ref[u] = rolled[5:8].astype(bf16)
            dt_bias, decay, skip = head_ref[0:1, :], head_ref[1:2, :], head_ref[2:3, :]
            weights, totals, reads, writes, picks = [], [], [], [], []
            for s in range(STEPS):
                raw = proj[s * EV : (s + 1) * EV, channels : channels + HEADS] + dt_bias
                size = jnp.maximum(raw, 0.0) + jnp.log1p(jnp.exp(-jnp.abs(raw)))
                size = jnp.where(row8 < counts[s], size, 0.0)
                cum = -decay * size
                for shift in (1, 2, 4):
                    cum = cum + jnp.where(row8 >= shift, pltpu.roll(cum, shift, 0), 0.0)
                total = cum[EV - 1 : EV, :]
                totals.append(total)
                weights.append(jnp.exp(total - cum) * size)
                picks.append((row8 == counts[s] - 1).astype(f32))
                writes.append(actives[s][:, INNER : INNER + STATE])
                reads.append(
                    jnp.sum(
                        picks[s] * actives[s][:, INNER + STATE : INNER + 2 * STATE],
                        axis=0,
                        keepdims=True,
                    )
                )
            carried = weights[0] * jnp.exp(totals[1])

            def gram(s, e):
                return jnp.sum(writes[e] * reads[s], axis=1, keepdims=True)

            table[0:8, 0:64] = weights[0] * gram(0, 0) + picks[0] * skip
            table[8:16, 0:64] = carried * gram(1, 0)
            table[16:24, 0:64] = weights[1] * gram(1, 1) + picks[1] * skip
            table[24:32, 0:64] = carried
            table[32:40, 0:64] = weights[1]
            table[40:41, 0:64] = jnp.exp(totals[0])
            table[41:42, 0:64] = jnp.exp(totals[0] + totals[1])
            table[42:43, 0:64] = reads[0]
            table[43:44, 0:64] = reads[1]
            cols = table[...].T[0:64]
            columns[u] = cols
            for s in range(STEPS):
                b_save[u, s * EV : (s + 1) * EV, :] = jnp.concatenate([writes[s], writes[s]], axis=1)
                for j in range(INNER // LANES):
                    x = actives[s][:, j * LANES : (j + 1) * LANES]
                    turned = pltpu.roll(x, 64, 1)
                    at = 2 * j * EVENTS + s * EV
                    stacked[at : at + EV, :] = jnp.where(left, x, turned)
                    stacked[at + EVENTS : at + EVENTS + EV, :] = jnp.where(left, turned, x)
            rows = pl.ds(pl.multiple_of(u * HEADS, HEADS), HEADS)
            part = jnp.zeros((HEADS, LANES), f32)
            for t in range(0, EVENTS, 2):
                pieces = []
                for e in (t, t + 1):
                    z = stacked[pl.ds(e, HEADS, stride=EVENTS), :]
                    second = cols[:, 8 + e : 9 + e]
                    if e < EV:
                        coef = jnp.where(left, cols[:, e : e + 1], second)
                    else:
                        coef = jnp.where(left, 0.0, second)
                    part = part + coef * z
                    pieces.append(cols[:, 24 + e : 25 + e] * z)
                a_rows[rows, t * HEAD_DIM : (t + 2) * HEAD_DIM] = jnp.where(
                    left, pieces[0], pieces[1]
                ).astype(bf16)
            y_part[u] = part

        return carry

    lax.fori_loop(0, cached, lift, 0)

    def arrange(q, carry):
        at = pl.ds(pl.multiple_of(q * LANES, LANES), LANES)
        a_sorted[q] = jnp.dot(
            a_rows[...], order_ref[:, at], preferred_element_type=f32
        ).astype(bf16)
        return carry

    lax.fori_loop(0, GROUP, arrange, 0)

    wide = GROUP * STATE
    block = lax.broadcasted_iota(jnp.int32, (GROUP * EVENTS, wide), 0) // EVENTS == (
        lax.broadcasted_iota(jnp.int32, (GROUP * EVENTS, wide), 1) // STATE
    )
    lane64 = lax.broadcasted_iota(jnp.int32, (1, LANES), 1) % 64

    def finish(u, carry):
        item = row_item[u]
        state_in(u).wait()

        @pl.when(item >= 0)
        def _():
            cols = columns[u]
            b = b_save[u]
            b_wide = jnp.concatenate([b] * (wide // LANES), axis=1)
            b_block = jnp.where(block, jnp.concatenate([b_wide] * GROUP, axis=0), 0.0).astype(bf16)
            lhs = a_sorted[:, pl.ds(pl.multiple_of(u * HEADS, HEADS), HEADS), :].reshape(
                GROUP * HEADS, LANES
            )
            update = jnp.dot(lhs, b_block, preferred_element_type=f32)
            read = jnp.where(left, cols[:, 42:43], cols[:, 43:44])
            decay = cols[:, 41:42]
            from_old = jnp.where(left, cols[:, 40:41], decay)
            total = jnp.zeros((HEADS, LANES), f32)
            for q in range(HEAD_DIM // GROUP):
                old = state_buf[u, :, q * wide : (q + 1) * wide]
                read_block = jnp.concatenate(
                    [jnp.where(lane64 == q * GROUP + i, read, 0.0) for i in range(GROUP)], axis=0
                ).astype(bf16)
                total = total + jnp.dot(old, read_block, preferred_element_type=f32)
                state_buf[u, :, q * wide : (q + 1) * wide] = (
                    decay * old.astype(f32) + update[q * HEADS : (q + 1) * HEADS]
                ).astype(bf16)
            y = from_old * total + y_part[u]
            square = jnp.sum(y * y, axis=0, keepdims=True)
            first = jnp.sum(jnp.where(left, square, 0.0), axis=1, keepdims=True)
            second = jnp.sum(jnp.where(left, 0.0, square), axis=1, keepdims=True)
            inverse = lax.rsqrt(jnp.where(left, first, second) * (1.0 / INNER) + 1e-05)
            y_ref[item] = (y * inverse * gain_ref[...]).astype(bf16)

        state_out(u).start()
        return carry

    lax.fori_loop(0, cached, finish, 0)
    for u in range(cached):
        state_out(u).wait()


def serve(meta, proj, state, window, conv_weight, conv_bias, dt_bias, decay_rate, skip_gain, norm_gain):
    cached = state.shape[0]
    items, _, width = proj.shape
    channels = window.shape[2]
    heads = jnp.stack([dt_bias, decay_rate, skip_gain])
    gain = norm_gain.reshape(HEADS, HEAD_DIM)
    gain = jnp.concatenate([gain, gain], axis=1)
    vmem = pl.BlockSpec(memory_space=pltpu.VMEM)
    hbm = pl.BlockSpec(memory_space=pl.ANY)
    return pl.pallas_call(
        functools.partial(serve_kernel, channels),
        in_specs=[pl.BlockSpec(memory_space=pltpu.SMEM), vmem, hbm] + [vmem] * 6,
        out_specs=[hbm, vmem, vmem],
        out_shape=[
            jax.ShapeDtypeStruct(state.shape, jnp.bfloat16),
            jax.ShapeDtypeStruct(window.shape, jnp.bfloat16),
            jax.ShapeDtypeStruct((items, HEADS, LANES), jnp.bfloat16),
        ],
        scratch_shapes=[
            pltpu.VMEM(state.shape, jnp.bfloat16),
            pltpu.VMEM((STEPS, 16, channels), jnp.float32),
            pltpu.VMEM((HEADS * EVENTS, LANES), jnp.float32),
            pltpu.VMEM((LANES, LANES), jnp.float32),
            pltpu.VMEM((cached, HEADS, LANES), jnp.float32),
            pltpu.VMEM((cached * HEADS, EVENTS * HEAD_DIM), jnp.bfloat16),
            pltpu.VMEM((GROUP, cached * HEADS, LANES), jnp.bfloat16),
            pltpu.VMEM((cached, HEADS, LANES), jnp.float32),
            pltpu.VMEM((cached, EVENTS, LANES), jnp.float32),
            pltpu.SMEM((cached,), jnp.int32),
            pltpu.SemaphoreType.DMA((cached,)),
            pltpu.SemaphoreType.DMA((cached,)),
        ],
        compiler_params=pltpu.CompilerParams(vmem_limit_bytes=48 * 2**20),
        cost_estimate=pl.CostEstimate(flops=6 * 10**9, bytes_accessed=10**7, transcendentals=10**6),
        name="serve",
    )(meta, proj, state, window, conv_weight, conv_bias[None], heads, gain, order_matrix())


MESH = pl.DeviceIdType.MESH
TILE = 256
CHUNKS = (2, 4, 4, 4, 3)


def greet(partners):
    barrier = pltpu.get_barrier_semaphore()
    for partner in partners:
        pl.semaphore_signal(barrier, inc=1, device_id=partner, device_id_type=MESH)
    pl.semaphore_wait(barrier, len(partners))


def project_kernel(
    n_req,
    n_fsdp,
    x_ref,
    w_hbm,
    dt_ref,
    pack_ref,
    meta_ref,
    items_ref,
    meta_out,
    x_all,
    w_all,
    own_sum,
    part_out,
    part_in,
    packed,
    load_sems,
    x_send,
    x_recv,
    w_send,
    w_recv,
    f_send,
    f_recv,
    p_send,
    p_recv,
    i_send,
    i_recv,
    m_send,
    m_recv,
):
    f32, bf16 = jnp.float32, jnp.bfloat16
    rows = x_ref.shape[1]
    depth, channels = w_hbm.shape
    chips = n_req // 2
    me_r, me_z = lax.axis_index("req"), lax.axis_index("fsdp")
    me_chip, core = me_r // 2, me_r % 2
    sibling = {"req": me_chip * 2 + 1 - core}

    def at_req(shift):
        return lax.rem(me_r + shift + n_req, n_req)

    def at_fsdp(shift):
        return lax.rem(me_z + shift + n_fsdp, n_fsdp)

    def at_chip(shift):
        return lax.rem(me_chip + shift + chips, chips) * 2 + core

    starts, sizes, at = [], [], 0
    for tiles in CHUNKS:
        starts.append(at)
        sizes.append(tiles * TILE)
        at += tiles * TILE
    chunks = range(len(CHUNKS))

    def remote(src, dst, send, recv, device):
        return pltpu.make_async_remote_copy(
            src_ref=src,
            dst_ref=dst,
            send_sem=send,
            recv_sem=recv,
            device_id=device,
            device_id_type=MESH,
        )

    def x_copy(d):
        return remote(
            x_ref.at[at_fsdp(d)], x_all.at[d], x_send.at[d], x_recv.at[d], {"fsdp": at_fsdp(d)}
        )

    def m_copy(d):
        return remote(
            meta_ref.at[at_req(d)],
            meta_out.at[me_r],
            m_send.at[d],
            m_recv.at[d],
            {"req": at_req(d)},
        )

    def cols(c):
        return pl.ds(starts[c], sizes[c])

    def w_copy(c, d):
        piece = w_all.at[me_r, :, cols(c)]
        return remote(piece, piece, w_send.at[c, d], w_recv.at[c, d], {"req": at_chip(d)})

    def w_forward(c, d):
        piece = w_all.at[at_chip(-d), :, cols(c)]
        return remote(piece, piece, f_send.at[c, d], f_recv.at[c, d], sibling)

    def p_copy(c, d):
        return remote(
            part_out.at[d, :, cols(c)],
            part_in.at[d, :, cols(c)],
            p_send.at[c, d],
            p_recv.at[c, d],
            {"fsdp": at_fsdp(-d)},
        )

    def i_copy(c, d):
        return remote(
            packed.at[at_req(d), :, cols(c)],
            items_ref.at[me_r, :, cols(c)],
            i_send.at[c, d],
            i_recv.at[c, d],
            {"req": at_req(d)},
        )

    def load(c):
        width = min(sizes[c], channels - starts[c])
        return pltpu.make_async_copy(
            w_hbm.at[:, pl.ds(starts[c], width)],
            w_all.at[me_r, :, pl.ds(starts[c], width)],
            load_sems.at[c],
        )

    for c in chunks:
        load(c).start()
    w_all[me_r, :, channels:] = jnp.concatenate(
        [dt_ref[...], jnp.zeros((depth, LANES - HEADS), bf16)], axis=1
    )
    x_all[0] = x_ref[me_z]
    meta_out[me_r] = meta_ref[me_r]
    greet(
        [{"req": at_req(d)} for d in range(1, n_req)]
        + [{"fsdp": at_fsdp(d)} for d in range(1, n_fsdp)]
    )
    for d in range(1, n_fsdp):
        x_copy(d).start()
    for c in chunks:
        load(c).wait()
        for d in range(1, chips):
            w_copy(c, d).start()
        w_forward(c, 0).start()
    for d in range(1, n_req):
        m_copy(d).start()

    def forward(c):
        for d in range(1, chips):
            w_copy(c, d).wait_recv()
            w_forward(c, d).start()

    def multiply(c):
        for d in range(chips):
            w_forward(c, d).wait_recv()

        def tile(i, carry):
            at = pl.ds(pl.multiple_of(starts[c] + i * TILE, TILE), TILE)
            part = jnp.dot(
                x_all[...].reshape(n_fsdp * rows, n_req * depth),
                w_all[:, :, at].reshape(n_req * depth, TILE),
                preferred_element_type=f32,
            )
            own_sum[:, at] = part[:rows]
            for d in range(1, n_fsdp):
                part_out[d, :, at] = part[d * rows : (d + 1) * rows].astype(bf16)
            return carry

        lax.fori_loop(0, CHUNKS[c], tile, 0)
        for d in range(1, n_fsdp):
            p_copy(c, d).start()

    def route(c):
        for d in range(1, n_fsdp):
            p_copy(c, d).wait_recv()

        def tile(i, carry):
            at = pl.ds(pl.multiple_of(starts[c] + i * TILE, TILE), TILE)
            total = own_sum[:, at]
            for d in range(1, n_fsdp):
                total = total + part_in[d, :, at].astype(f32)
            chosen = jnp.dot(pack_ref[...], total.astype(bf16), preferred_element_type=f32)
            packed[:, :, at] = chosen.reshape(n_req, -1, TILE).astype(bf16)
            items_ref[me_r, :, at] = packed[me_r, :, at]
            return carry

        lax.fori_loop(0, CHUNKS[c], tile, 0)
        for d in range(1, n_req):
            i_copy(c, d).start()

    forward(0)
    for d in range(1, n_fsdp):
        x_copy(d).wait_recv()
    for c in chunks:
        if c + 1 < len(CHUNKS):
            forward(c + 1)
        multiply(c)
        if c >= 1:
            route(c - 1)
    route(len(CHUNKS) - 1)
    for d in range(1, n_req):
        m_copy(d).wait()
        for c in chunks:
            i_copy(c, d).wait()
    for d in range(1, n_fsdp):
        x_copy(d).wait_send()
        for c in chunks:
            p_copy(c, d).wait_send()
    for c in chunks:
        w_forward(c, 0).wait_send()
        for d in range(1, chips):
            w_copy(c, d).wait_send()
            w_forward(c, d).wait_send()


def project(x, in_weight, dt_weight, pack, meta):
    n_req, n_fsdp = lax.axis_size("req"), lax.axis_size("fsdp")
    rows = x.shape[1]
    depth, channels = in_weight.shape
    width = sum(CHUNKS) * TILE
    room = pack.shape[0] // n_req
    bf16 = jnp.bfloat16
    vmem = pl.BlockSpec(memory_space=pltpu.VMEM)
    dma = pltpu.SemaphoreType.DMA
    n = len(CHUNKS)
    return pl.pallas_call(
        functools.partial(project_kernel, n_req, n_fsdp),
        in_specs=[vmem, pl.BlockSpec(memory_space=pl.ANY), vmem, vmem, vmem],
        out_specs=[vmem, vmem],
        out_shape=[
            jax.ShapeDtypeStruct((n_req, room, width), bf16),
            jax.ShapeDtypeStruct(meta.shape, meta.dtype),
        ],
        scratch_shapes=[
            pltpu.VMEM((n_fsdp, rows, n_req * depth), bf16),
            pltpu.VMEM((n_req, depth, width), bf16),
            pltpu.VMEM((rows, width), jnp.float32),
            pltpu.VMEM((n_fsdp, rows, width), bf16),
            pltpu.VMEM((n_fsdp, rows, width), bf16),
            pltpu.VMEM((n_req, room, width), bf16),
            dma((n,)),
            dma((n_fsdp,)),
            dma((n_fsdp,)),
            dma((n, n_req // 2)),
            dma((n, n_req // 2)),
            dma((n, n_req // 2)),
            dma((n, n_req // 2)),
            dma((n, n_fsdp)),
            dma((n, n_fsdp)),
            dma((n, n_req)),
            dma((n, n_req)),
            dma((n_req,)),
            dma((n_req,)),
        ],
        compiler_params=pltpu.CompilerParams(
            collective_id=0, has_side_effects=True, vmem_limit_bytes=48 * 2**20
        ),
        cost_estimate=pl.CostEstimate(flops=10**9, bytes_accessed=10**7, transcendentals=0),
        name="project",
    )(x, in_weight, dt_weight, pack, meta)


def return_kernel(n_req, y_ref, index_ref, out_ref, back, send_sems, recv_sems):
    me_r = lax.axis_index("req")

    def at_req(shift):
        return lax.rem(me_r + shift, n_req)

    def copy(d):
        return pltpu.make_async_remote_copy(
            src_ref=y_ref.at[at_req(d)],
            dst_ref=back.at[me_r],
            send_sem=send_sems.at[d],
            recv_sem=recv_sems.at[d],
            device_id={"req": at_req(d)},
            device_id_type=MESH,
        )

    greet([{"req": at_req(d)} for d in range(1, n_req)])
    for d in range(1, n_req):
        copy(d).start()
    back[me_r] = y_ref[me_r]
    for d in range(1, n_req):
        copy(d).wait()
    for u in range(out_ref.shape[0]):
        out_ref[u] = back[index_ref[0, u], index_ref[1, u]]


def give_back(y, owner, rank):
    n_req = lax.axis_size("req")
    vmem = pl.BlockSpec(memory_space=pltpu.VMEM)
    y = y.reshape(n_req, SLOTS_PER_PAIR, HEADS, LANES)
    return pl.pallas_call(
        functools.partial(return_kernel, n_req),
        in_specs=[vmem, pl.BlockSpec(memory_space=pltpu.SMEM)],
        out_specs=vmem,
        out_shape=jax.ShapeDtypeStruct((owner.shape[0], HEADS, LANES), jnp.bfloat16),
        scratch_shapes=[
            pltpu.VMEM(y.shape, jnp.bfloat16),
            pltpu.SemaphoreType.DMA((n_req,)),
            pltpu.SemaphoreType.DMA((n_req,)),
        ],
        compiler_params=pltpu.CompilerParams(collective_id=1, has_side_effects=True),
        cost_estimate=pl.CostEstimate(flops=10**5, bytes_accessed=10**6, transcendentals=0),
        name="give_back",
    )(y, jnp.stack([owner, rank]))


def user_ranks(hash_owner):
    index = jnp.arange(hash_owner.shape[0], dtype=jnp.int32)
    same = (hash_owner[:, None] == hash_owner[None, :]) & (index[None, :] < index[:, None])
    return jnp.sum(same.astype(jnp.int32), axis=1)


def on_device(
    tokens,
    in_weight,
    dt_weight,
    conv_weight,
    conv_bias,
    dt_bias,
    decay_rate,
    skip_gain,
    norm_gain,
    state_cache,
    conv_cache,
    hash_owner,
    cache_slot,
    event_counts,
):
    owners = lax.axis_size("req")
    columns = lax.axis_size("fsdp")
    users = tokens.shape[1]
    depth = in_weight.shape[0]
    rank = user_ranks(hash_owner)
    places = (hash_owner == jnp.arange(owners, dtype=jnp.int32)[:, None, None]) & (
        rank == jnp.arange(SLOTS_PER_PAIR, dtype=jnp.int32)[:, None]
    )
    orders = jnp.stack([cache_slot + 1, event_counts[0], event_counts[1]], axis=1)
    meta = jnp.sum(jnp.where(places[..., None], orders, 0), axis=2)
    meta = jnp.pad(meta, ((0, 0), (0, 8 - SLOTS_PER_PAIR), (0, LANES - 3)))
    same_event = jnp.eye(EVENTS, dtype=jnp.bool_)
    pack = (places[:, :, None, :, None] & same_event[:, None, :]).astype(jnp.bfloat16)
    pack = pack.reshape(owners * SLOTS_PER_PAIR * EVENTS, users * EVENTS)
    x = tokens.reshape(STEPS, users, EV, owners, columns, depth).transpose(4, 1, 0, 2, 3, 5)
    x = x.reshape(columns, users * EVENTS, owners * depth)
    items, arrived = project(x, in_weight, dt_weight, pack, meta)
    new_state, new_window, y = serve(
        arrived,
        items.reshape(owners * SLOTS_PER_PAIR, EVENTS, -1),
        state_cache,
        conv_cache,
        conv_weight,
        conv_bias,
        dt_bias,
        decay_rate,
        skip_gain,
        norm_gain,
    )
    chosen = give_back(y, hash_owner, rank).reshape(users, HEADS, STEPS, HEAD_DIM)
    user_vectors = chosen.transpose(2, 0, 1, 3).reshape(STEPS, users, INNER)
    return (user_vectors, new_state, new_window)


def solution(mesh):
    split = ("groups", "req", "fsdp")
    in_specs = (
        P(None, split, None, None),
        P(("req", "fsdp"), None),
        P(("req", "fsdp"), None),
        P(),
        P(),
        P(),
        P(),
        P(),
        P(),
        P(split, None, None),
        P(split, None, None),
        P(split),
        P(split),
        P(None, split),
    )
    out_specs = (P(None, split, None), P(split, None, None), P(split, None, None))
    return jax.shard_map(
        on_device, mesh=mesh, in_specs=in_specs, out_specs=out_specs, check_vma=False
    )
```

```python
import functools

import jax
import jax.numpy as jnp
import numpy as np
from jax import lax
from jax.experimental import pallas as pl
from jax.experimental.pallas import tpu as pltpu
from jax.sharding import PartitionSpec as P

HEADS = 64
HEAD_DIM = 64
STATE = 64
STEPS = 2
EV = 8
EVENTS = STEPS * EV
INNER = HEADS * HEAD_DIM
LANES = 128
GROUP = 8
SLOTS_PER_PAIR = 2


def order_matrix():
    out = np.zeros((EVENTS * HEAD_DIM, EVENTS * HEAD_DIM), np.float32)
    t, p = np.meshgrid(np.arange(EVENTS), np.arange(HEAD_DIM), indexing="ij")
    out[t * HEAD_DIM + p, p * EVENTS + t] = 1.0
    return jnp.asarray(out, jnp.bfloat16)


def serve_kernel(
    channels,
    meta_ref,
    proj_ref,
    state_hbm,
    window_ref,
    cw_ref,
    cb_ref,
    head_ref,
    gain_ref,
    order_ref,
    new_state_hbm,
    new_window_ref,
    y_ref,
    state_buf,
    win_in,
    win_out,
    ext,
    stacked,
    table,
    columns,
    a_rows,
    a_sorted,
    y_part,
    b_save,
    row_item,
    in_sems,
    out_sems,
):
    cached = state_buf.shape[0]
    items = proj_ref.shape[0]
    f32, bf16 = jnp.float32, jnp.bfloat16

    def state_in(u):
        return pltpu.make_async_copy(state_hbm.at[u], state_buf.at[u], in_sems.at[u])

    def state_out(u):
        return pltpu.make_async_copy(state_buf.at[u], new_state_hbm.at[u], out_sems.at[u])

    for u in range(cached):
        state_in(u).start()
    for u in range(cached):
        found = jnp.int32(-1)
        for i in range(items):
            found = jnp.where(meta_ref[i // SLOTS_PER_PAIR, i % SLOTS_PER_PAIR, 0] == u + 1, i, found)
        row_item[u] = found

    left = lax.broadcasted_iota(jnp.int32, (1, LANES), 1) < 64
    row8 = lax.broadcasted_iota(jnp.int32, (EV, 1), 0)
    y_ref[...] = jnp.zeros(y_ref.shape, y_ref.dtype)
    table[...] = jnp.zeros(table.shape, f32)
    win_in[...] = window_ref[...].astype(f32)

    def lift(u, carry):
        item = row_item[u]

        @pl.when(item < 0)
        def _():
            for i in range(3):
                win_out[i, pl.ds(u, 1), :] = win_in[i, pl.ds(u, 1), :]
            a_rows[pl.ds(pl.multiple_of(u * HEADS, HEADS), HEADS), :] = jnp.zeros(
                (HEADS, EVENTS * HEAD_DIM), bf16
            )

        @pl.when(item >= 0)
        def _():
            pair, place = item // SLOTS_PER_PAIR, item % SLOTS_PER_PAIR
            counts = [meta_ref[pair, place, 1], meta_ref[pair, place, 2]]
            for i in range(3):
                ext[0, 5 + i : 6 + i, :] = win_in[i, pl.ds(u, 1), :]
            proj = proj_ref[item].astype(f32)
            actives = []
            for s in range(STEPS):
                ext[s, 8:16, :] = proj[s * EV : (s + 1) * EV, :channels]
                conv = cb_ref[...] + cw_ref[0:1, :] * ext[s, 5:13, :]
                for tap in range(1, 4):
                    conv = conv + cw_ref[tap : tap + 1, :] * ext[s, 5 + tap : 13 + tap, :]
                actives.append(conv * (1.0 / (1.0 + jnp.exp(-conv))))
                rolled = pltpu.roll(ext[s], 16 - counts[s], 0)
                if s + 1 < STEPS:
                    ext[s + 1, 0:8, :] = rolled[0:8]
                else:
                    for i in range(3):
                        win_out[i, pl.ds(u, 1), :] = rolled[5 + i : 6 + i]
            dt_bias, decay, skip = head_ref[0:1, :], head_ref[1:2, :], head_ref[2:3, :]
            weights, totals, reads, writes, picks = [], [], [], [], []
            for s in range(STEPS):
                raw = proj[s * EV : (s + 1) * EV, channels : channels + HEADS] + dt_bias
                size = jnp.maximum(raw, 0.0) + jnp.log1p(jnp.exp(-jnp.abs(raw)))
                size = jnp.where(row8 < counts[s], size, 0.0)
                cum = -decay * size
                for shift in (1, 2, 4):
                    cum = cum + jnp.where(row8 >= shift, pltpu.roll(cum, shift, 0), 0.0)
                total = cum[EV - 1 : EV, :]
                totals.append(total)
                weights.append(jnp.exp(total - cum) * size)
                picks.append((row8 == counts[s] - 1).astype(f32))
                writes.append(actives[s][:, INNER : INNER + STATE])
                reads.append(
                    jnp.sum(
                        picks[s] * actives[s][:, INNER + STATE : INNER + 2 * STATE],
                        axis=0,
                        keepdims=True,
                    )
                )
            carried = weights[0] * jnp.exp(totals[1])

            def gram(s, e):
                return jnp.sum(writes[e] * reads[s], axis=1, keepdims=True)

            table[0:8, 0:64] = weights[0] * gram(0, 0) + picks[0] * skip
            table[8:16, 0:64] = carried * gram(1, 0)
            table[16:24, 0:64] = weights[1] * gram(1, 1) + picks[1] * skip
            table[24:32, 0:64] = carried
            table[32:40, 0:64] = weights[1]
            table[40:41, 0:64] = jnp.exp(totals[0])
            table[41:42, 0:64] = jnp.exp(totals[0] + totals[1])
            table[42:43, 0:64] = reads[0]
            table[43:44, 0:64] = reads[1]
            cols = table[...].T[0:64]
            columns[u] = cols
            for s in range(STEPS):
                b_save[u, s * EV : (s + 1) * EV, :] = jnp.concatenate([writes[s], writes[s]], axis=1)
                for j in range(INNER // LANES):
                    x = actives[s][:, j * LANES : (j + 1) * LANES]
                    turned = pltpu.roll(x, 64, 1)
                    at = 2 * j * EVENTS + s * EV
                    stacked[at : at + EV, :] = jnp.where(left, x, turned)
                    stacked[at + EVENTS : at + EVENTS + EV, :] = jnp.where(left, turned, x)
            rows = pl.ds(pl.multiple_of(u * HEADS, HEADS), HEADS)
            part = jnp.zeros((HEADS, LANES), f32)
            for t in range(0, EVENTS, 2):
                pieces = []
                for e in (t, t + 1):
                    z = stacked[pl.ds(e, HEADS, stride=EVENTS), :]
                    second = cols[:, 8 + e : 9 + e]
                    if e < EV:
                        coef = jnp.where(left, cols[:, e : e + 1], second)
                    else:
                        coef = jnp.where(left, 0.0, second)
                    part = part + coef * z
                    pieces.append(cols[:, 24 + e : 25 + e] * z)
                a_rows[rows, t * HEAD_DIM : (t + 2) * HEAD_DIM] = jnp.where(
                    left, pieces[0], pieces[1]
                ).astype(bf16)
            y_part[u] = part

        return carry

    lax.fori_loop(0, cached, lift, 0)

    def arrange(q, carry):
        at = pl.ds(pl.multiple_of(q * LANES, LANES), LANES)
        a_sorted[q] = jnp.dot(
            a_rows[...], order_ref[:, at], preferred_element_type=f32
        ).astype(bf16)
        return carry

    lax.fori_loop(0, GROUP, arrange, 0)

    wide = GROUP * STATE
    block = lax.broadcasted_iota(jnp.int32, (GROUP * EVENTS, wide), 0) // EVENTS == (
        lax.broadcasted_iota(jnp.int32, (GROUP * EVENTS, wide), 1) // STATE
    )
    lane64 = lax.broadcasted_iota(jnp.int32, (1, LANES), 1) % 64

    def finish(u, carry):
        item = row_item[u]
        state_in(u).wait()

        @pl.when(item >= 0)
        def _():
            pair, place = item // SLOTS_PER_PAIR, item % SLOTS_PER_PAIR
            cols = columns[u]
            b = b_save[u]
            b_wide = jnp.concatenate([b] * (wide // LANES), axis=1)
            b_block = jnp.where(block, jnp.concatenate([b_wide] * GROUP, axis=0), 0.0).astype(bf16)
            lhs = a_sorted[:, pl.ds(pl.multiple_of(u * HEADS, HEADS), HEADS), :].reshape(
                GROUP * HEADS, LANES
            )
            update = jnp.dot(lhs, b_block, preferred_element_type=f32)
            read = jnp.where(left, cols[:, 42:43], cols[:, 43:44])
            decay = cols[:, 41:42]
            from_old = jnp.where(left, cols[:, 40:41], decay)
            total = jnp.zeros((HEADS, LANES), f32)
            for q in range(HEAD_DIM // GROUP):
                old = state_buf[u, :, q * wide : (q + 1) * wide]
                read_block = jnp.concatenate(
                    [jnp.where(lane64 == q * GROUP + i, read, 0.0) for i in range(GROUP)], axis=0
                ).astype(bf16)
                total = total + jnp.dot(old, read_block, preferred_element_type=f32)
                state_buf[u, :, q * wide : (q + 1) * wide] = (
                    decay * old.astype(f32) + update[q * HEADS : (q + 1) * HEADS]
                ).astype(bf16)
            y = from_old * total + y_part[u]
            square = jnp.sum(y * y, axis=0, keepdims=True)
            first = jnp.sum(jnp.where(left, square, 0.0), axis=1, keepdims=True)
            second = jnp.sum(jnp.where(left, 0.0, square), axis=1, keepdims=True)
            inverse = lax.rsqrt(jnp.where(left, first, second) * (1.0 / INNER) + 1e-05)
            y_ref[pair, place] = (y * inverse * gain_ref[...]).astype(bf16)

        state_out(u).start()
        return carry

    new_window_ref[...] = win_out[...].astype(bf16)
    lax.fori_loop(0, cached, finish, 0)
    for u in range(cached):
        state_out(u).wait()


def serve(meta, proj, state, window, conv_weight, conv_bias, dt_bias, decay_rate, skip_gain, norm_gain):
    cached = state.shape[0]
    items, _, width = proj.shape
    channels = window.shape[2]
    heads = jnp.stack([dt_bias, decay_rate, skip_gain])
    gain = norm_gain.reshape(HEADS, HEAD_DIM)
    gain = jnp.concatenate([gain, gain], axis=1)
    vmem = pl.BlockSpec(memory_space=pltpu.VMEM)
    hbm = pl.BlockSpec(memory_space=pl.ANY)
    return pl.pallas_call(
        functools.partial(serve_kernel, channels),
        in_specs=[pl.BlockSpec(memory_space=pltpu.SMEM), vmem, hbm] + [vmem] * 6,
        out_specs=[hbm, vmem, vmem],
        out_shape=[
            jax.ShapeDtypeStruct(state.shape, jnp.bfloat16),
            jax.ShapeDtypeStruct(window.shape, jnp.bfloat16),
            jax.ShapeDtypeStruct((items // SLOTS_PER_PAIR, SLOTS_PER_PAIR, HEADS, LANES), jnp.bfloat16),
        ],
        scratch_shapes=[
            pltpu.VMEM(state.shape, jnp.bfloat16),
            pltpu.VMEM(window.shape, jnp.float32),
            pltpu.VMEM(window.shape, jnp.float32),
            pltpu.VMEM((STEPS, 16, channels), jnp.float32),
            pltpu.VMEM((HEADS * EVENTS, LANES), jnp.float32),
            pltpu.VMEM((LANES, LANES), jnp.float32),
            pltpu.VMEM((cached, HEADS, LANES), jnp.float32),
            pltpu.VMEM((cached * HEADS, EVENTS * HEAD_DIM), jnp.bfloat16),
            pltpu.VMEM((GROUP, cached * HEADS, LANES), jnp.bfloat16),
            pltpu.VMEM((cached, HEADS, LANES), jnp.float32),
            pltpu.VMEM((cached, EVENTS, LANES), jnp.float32),
            pltpu.SMEM((cached,), jnp.int32),
            pltpu.SemaphoreType.DMA((cached,)),
            pltpu.SemaphoreType.DMA((cached,)),
        ],
        compiler_params=pltpu.CompilerParams(vmem_limit_bytes=48 * 2**20),
        cost_estimate=pl.CostEstimate(flops=6 * 10**9, bytes_accessed=10**7, transcendentals=10**6),
        name="serve",
    )(meta, proj, state, window, conv_weight, conv_bias[None], heads, gain, order_matrix())


MESH = pl.DeviceIdType.MESH
TILE = 256
CHUNKS = (2, 4, 4, 4, 3)


def greet(partners):
    barrier = pltpu.get_barrier_semaphore()
    for partner in partners:
        pl.semaphore_signal(barrier, inc=1, device_id=partner, device_id_type=MESH)
    pl.semaphore_wait(barrier, len(partners))


def ranks(owner):
    out = []
    for u in range(len(owner)):
        rank = jnp.zeros((1, 1), jnp.int32)
        for earlier in owner[:u]:
            rank = rank + (earlier == owner[u]).astype(jnp.int32)
        out.append(rank)
    return out


def project_kernel(
    n_req,
    n_fsdp,
    x_ref,
    w_hbm,
    dt_ref,
    owner_ref,
    slot_ref,
    count_ref,
    items_ref,
    meta_out,
    strips,
    x_all,
    w_all,
    own_sum,
    part_out,
    part_in,
    sum_out,
    sum_in,
    pack,
    packed,
    meta,
    load_sems,
    x_send,
    x_recv,
    w_send,
    w_recv,
    f_send,
    f_recv,
    p_send,
    p_recv,
    s_send,
    s_recv,
    i_send,
    i_recv,
    m_send,
    m_recv,
):
    f32, bf16, i32 = jnp.float32, jnp.bfloat16, jnp.int32
    rows = x_ref.shape[0]
    users = rows // EVENTS
    depth, channels = w_hbm.shape
    chips = n_req // 2
    pairs = n_fsdp // 2
    me_r, me_z = lax.axis_index("req"), lax.axis_index("fsdp")
    me_chip, core = me_r // 2, me_r % 2
    me_pair, side = me_z // 2, me_z % 2
    sibling = {"req": me_chip * 2 + 1 - core}

    def at_req(shift):
        return lax.rem(me_r + shift + n_req, n_req)

    def at_chip(shift):
        return lax.rem(me_chip + shift + chips, chips) * 2 + core

    def at_fsdp(pair, other):
        return lax.rem(me_pair + pair + pairs, pairs) * 2 + (1 - side if other else side)

    starts, sizes, at = [], [], 0
    for tiles in CHUNKS:
        starts.append(at)
        sizes.append(tiles * TILE)
        at += tiles * TILE
    chunks = range(len(CHUNKS))
    fsdp_shifts = [(d, o) for d in range(pairs) for o in (0, 1)][1:]

    def remote(src, dst, send, recv, device):
        return pltpu.make_async_remote_copy(
            src_ref=src,
            dst_ref=dst,
            send_sem=send,
            recv_sem=recv,
            device_id=device,
            device_id_type=MESH,
        )

    def x_copy(d, o):
        i = d * 2 + o
        target = at_fsdp(d, o)
        return remote(strips.at[target], x_all.at[i], x_send.at[i], x_recv.at[i], {"fsdp": target})

    def m_copy(d):
        target = at_req(d)
        return remote(
            meta.at[target], meta_out.at[me_r], m_send.at[d], m_recv.at[d], {"req": target}
        )

    def cols(c):
        return pl.ds(starts[c], sizes[c])

    def w_copy(c, d):
        piece = w_all.at[me_r, :, cols(c)]
        return remote(piece, piece, w_send.at[c, d], w_recv.at[c, d], {"req": at_chip(d)})

    def w_forward(c, d):
        piece = w_all.at[at_chip(-d), :, cols(c)]
        return remote(piece, piece, f_send.at[c, d], f_recv.at[c, d], sibling)

    def p_copy(c, d):
        return remote(
            part_out.at[d, :, cols(c)],
            part_in.at[d, :, cols(c)],
            p_send.at[c, d],
            p_recv.at[c, d],
            {"fsdp": at_fsdp(0, 1)},
        )

    def s_copy(c, d):
        return remote(
            sum_out.at[d, :, cols(c)],
            sum_in.at[d, :, cols(c)],
            s_send.at[c, d],
            s_recv.at[c, d],
            {"fsdp": at_fsdp(-d, 0)},
        )

    def i_copy(c, d):
        target = at_req(d)
        return remote(
            packed.at[pl.ds(target * SLOTS_PER_PAIR, SLOTS_PER_PAIR), :, cols(c)],
            items_ref.at[pl.ds(me_r * SLOTS_PER_PAIR, SLOTS_PER_PAIR), :, cols(c)],
            i_send.at[c, d],
            i_recv.at[c, d],
            {"req": target},
        )

    def load(c):
        width = min(sizes[c], channels - starts[c])
        return pltpu.make_async_copy(
            w_hbm.at[:, pl.ds(starts[c], width)],
            w_all.at[me_r, :, pl.ds(starts[c], width)],
            load_sems.at[c],
        )

    for c in chunks:
        load(c).start()
    barrier = pltpu.get_barrier_semaphore()
    partners = [{"req": at_req(d)} for d in range(1, n_req)]
    partners += [{"fsdp": at_fsdp(d, o)} for d, o in fsdp_shifts]
    for partner in partners:
        pl.semaphore_signal(barrier, inc=1, device_id=partner, device_id_type=MESH)
    for z in range(n_fsdp):
        for r in range(n_req):
            at = (r * n_fsdp + z) * depth
            strips[z, :, r * depth : (r + 1) * depth] = x_ref[:, at : at + depth]
    x_all[0] = strips[me_z]
    if dt_ref.shape[0] == depth:
        step_columns = jnp.concatenate(
            [dt_ref[...], jnp.zeros((depth, LANES - HEADS), bf16)], axis=1
        )
    else:
        step_columns = jnp.concatenate(
            [dt_ref[...].astype(f32), jnp.zeros((LANES - HEADS, depth), f32)], axis=0
        ).T.astype(bf16)
    w_all[me_r, :, channels:] = step_columns
    pl.semaphore_wait(barrier, len(partners))
    for d, o in fsdp_shifts:
        x_copy(d, o).start()
    for c in chunks:
        load(c).wait()
        for d in range(1, chips):
            w_copy(c, d).start()
        w_forward(c, 0).start()

    owner = [owner_ref[0:1, u : u + 1] for u in range(users)]
    rank = ranks(owner)
    high, wide = pack.shape
    row = lax.broadcasted_iota(i32, (high, wide), 0)
    col = lax.broadcasted_iota(i32, (high, wide), 1)
    user = (col // EV) % users
    hit = jnp.zeros((high, wide), jnp.bool_)
    pair_row = row // EVENTS
    for u in range(users):
        hit = hit | ((pair_row == owner[u] * SLOTS_PER_PAIR + rank[u]) & (user == u))
    same = (row % EV == col % EV) & ((row // EV) % STEPS == col // (EV * users))
    pack[...] = jnp.where(hit & same, 1.0, 0.0).astype(bf16)
    row = lax.broadcasted_iota(i32, (n_req * 8, LANES), 0)
    lane = lax.broadcasted_iota(i32, (n_req * 8, LANES), 1)
    notes = jnp.zeros((n_req * 8, LANES), i32)
    for u in range(users):
        note = jnp.where(lane == 0, slot_ref[0:1, u : u + 1] + 1, 0)
        for s in range(STEPS):
            note = jnp.where(lane == 1 + s, count_ref[s : s + 1, u : u + 1], note)
        notes = jnp.where(row == owner[u] * 8 + rank[u], note, notes)
    meta[...] = notes.reshape(meta.shape)
    for d in range(1, n_req):
        m_copy(d).start()
    meta_out[me_r] = meta[me_r]

    def forward(c):
        for d in range(1, chips):
            w_copy(c, d).wait_recv()
            w_forward(c, d).start()

    def tiles(c, body):
        def step(i, carry):
            body(pl.ds(pl.multiple_of(starts[c] + i * TILE, TILE), TILE))
            return carry

        lax.fori_loop(0, CHUNKS[c], step, 0)

    def multiply(c):
        for d in range(chips):
            w_forward(c, d).wait_recv()

        def tile(at):
            part = jnp.dot(
                x_all[...].reshape(n_fsdp * rows, n_req * depth),
                w_all[:, :, at].reshape(n_req * depth, TILE),
                preferred_element_type=f32,
            )
            for d in range(pairs):
                own_sum[d, :, at] = part[2 * d * rows : (2 * d + 1) * rows]
                part_out[d, :, at] = part[(2 * d + 1) * rows : (2 * d + 2) * rows].astype(bf16)

        tiles(c, tile)
        for d in (*range(1, pairs), 0):
            p_copy(c, d).start()

    def combine(c):
        for d in range(1, pairs):
            p_copy(c, d).wait_recv()

        def tile(at):
            for d in range(1, pairs):
                sum_out[d, :, at] = (own_sum[d, :, at] + part_in[d, :, at].astype(f32)).astype(bf16)

        tiles(c, tile)
        for d in range(1, pairs):
            s_copy(c, d).start()

    def route(c):
        p_copy(c, 0).wait_recv()
        for d in range(1, pairs):
            s_copy(c, d).wait_recv()

        def tile(at):
            total = own_sum[0, :, at] + part_in[0, :, at].astype(f32)
            for d in range(1, pairs):
                total = total + sum_in[d, :, at].astype(f32)
            chosen = jnp.dot(pack[...], total.astype(bf16), preferred_element_type=f32)
            packed[:, :, at] = chosen.reshape(-1, EVENTS, TILE).astype(bf16)
            for i in range(SLOTS_PER_PAIR):
                mine = me_r * SLOTS_PER_PAIR + i
                items_ref[mine, :, at] = packed[mine, :, at]

        tiles(c, tile)
        for d in range(1, n_req):
            i_copy(c, d).start()

    last = len(CHUNKS)
    forward(0)
    for d, o in fsdp_shifts:
        x_copy(d, o).wait_recv()
    for c in range(last + 2):
        if c + 1 < last:
            forward(c + 1)
        if c < last:
            multiply(c)
        if 1 <= c <= last:
            combine(c - 1)
        if c >= 2:
            route(c - 2)
    for d in range(1, n_req):
        m_copy(d).wait()
        for c in chunks:
            i_copy(c, d).wait()
    for d, o in fsdp_shifts:
        x_copy(d, o).wait_send()
    for c in chunks:
        for d in range(pairs):
            p_copy(c, d).wait_send()
        for d in range(1, pairs):
            s_copy(c, d).wait_send()
        w_forward(c, 0).wait_send()
        for d in range(1, chips):
            w_copy(c, d).wait_send()
            w_forward(c, d).wait_send()


def project(x, in_weight, dt_weight, owner, slot, counts):
    n_req, n_fsdp = lax.axis_size("req"), lax.axis_size("fsdp")
    rows = x.shape[0]
    depth, channels = in_weight.shape
    width = sum(CHUNKS) * TILE
    items = n_req * SLOTS_PER_PAIR
    pairs = n_fsdp // 2
    f32, bf16, i32 = jnp.float32, jnp.bfloat16, jnp.int32
    vmem = pl.BlockSpec(memory_space=pltpu.VMEM)
    dma = pltpu.SemaphoreType.DMA
    n = len(CHUNKS)
    return pl.pallas_call(
        functools.partial(project_kernel, n_req, n_fsdp),
        in_specs=[vmem, pl.BlockSpec(memory_space=pl.ANY), vmem, vmem, vmem, vmem],
        out_specs=[vmem, vmem],
        out_shape=[
            jax.ShapeDtypeStruct((items, EVENTS, width), bf16),
            jax.ShapeDtypeStruct((n_req, 8, LANES), i32),
        ],
        scratch_shapes=[
            pltpu.VMEM((n_fsdp, rows, n_req * depth), bf16),
            pltpu.VMEM((n_fsdp, rows, n_req * depth), bf16),
            pltpu.VMEM((n_req, depth, width), bf16),
            pltpu.VMEM((pairs, rows, width), f32),
            pltpu.VMEM((pairs, rows, width), bf16),
            pltpu.VMEM((pairs, rows, width), bf16),
            pltpu.VMEM((pairs, rows, width), bf16),
            pltpu.VMEM((pairs, rows, width), bf16),
            pltpu.VMEM((items * EVENTS, rows), bf16),
            pltpu.VMEM((items, EVENTS, width), bf16),
            pltpu.VMEM((n_req, 8, LANES), i32),
            dma((n,)),
            dma((n_fsdp,)),
            dma((n_fsdp,)),
            dma((n, n_req // 2)),
            dma((n, n_req // 2)),
            dma((n, n_req // 2)),
            dma((n, n_req // 2)),
            dma((n, pairs)),
            dma((n, pairs)),
            dma((n, pairs)),
            dma((n, pairs)),
            dma((n, n_req)),
            dma((n, n_req)),
            dma((n_req,)),
            dma((n_req,)),
        ],
        compiler_params=pltpu.CompilerParams(
            collective_id=0, has_side_effects=True, vmem_limit_bytes=48 * 2**20
        ),
        cost_estimate=pl.CostEstimate(flops=10**9, bytes_accessed=10**7, transcendentals=0),
        name="project",
    )(x, in_weight, dt_weight, owner, slot, counts)


def return_kernel(n_req, y_ref, owner_ref, out_ref, back, rows, flat, send_sems, recv_sems):
    me_r = lax.axis_index("req")
    users = owner_ref.shape[0]

    def at_req(shift):
        return lax.rem(me_r + shift, n_req)

    def copy(d):
        return pltpu.make_async_remote_copy(
            src_ref=y_ref.at[at_req(d)],
            dst_ref=back.at[me_r],
            send_sem=send_sems.at[d],
            recv_sem=recv_sems.at[d],
            device_id={"req": at_req(d)},
            device_id_type=MESH,
        )

    greet([{"req": at_req(d)} for d in range(1, n_req)])
    for d in range(1, n_req):
        copy(d).start()
    back[me_r] = y_ref[me_r]
    for d in range(1, n_req):
        copy(d).wait()
    left = lax.broadcasted_iota(jnp.int32, (1, LANES), 1) < 64
    for u in range(users):
        rank = jnp.int32(0)
        for earlier in range(u):
            rank = rank + (owner_ref[earlier] == owner_ref[u]).astype(jnp.int32)
        rank = jnp.minimum(rank, SLOTS_PER_PAIR - 1)
        rows[u] = back[owner_ref[u], rank].astype(jnp.float32)
        even = rows[u, pl.ds(0, HEADS // 2, stride=2), :]
        odd = rows[u, pl.ds(1, HEADS // 2, stride=2), :]
        steps = [
            jnp.where(left, even, pltpu.roll(odd, 64, 1)),
            jnp.where(left, pltpu.roll(even, 64, 1), odd),
        ]
        for s in range(STEPS):
            for j in range(INNER // LANES):
                flat[s, u : u + 1, j * LANES : (j + 1) * LANES] = steps[s][j : j + 1]
    out_ref[...] = flat[...].astype(jnp.bfloat16)


def give_back(y, owner):
    n_req = lax.axis_size("req")
    users = owner.shape[0]
    vmem = pl.BlockSpec(memory_space=pltpu.VMEM)
    return pl.pallas_call(
        functools.partial(return_kernel, n_req),
        in_specs=[vmem, pl.BlockSpec(memory_space=pltpu.SMEM)],
        out_specs=vmem,
        out_shape=jax.ShapeDtypeStruct((STEPS, users, INNER), jnp.bfloat16),
        scratch_shapes=[
            pltpu.VMEM(y.shape, jnp.bfloat16),
            pltpu.VMEM((users, HEADS, LANES), jnp.float32),
            pltpu.VMEM((STEPS, users, INNER), jnp.float32),
            pltpu.SemaphoreType.DMA((n_req,)),
            pltpu.SemaphoreType.DMA((n_req,)),
        ],
        compiler_params=pltpu.CompilerParams(collective_id=1, has_side_effects=True),
        cost_estimate=pl.CostEstimate(flops=10**5, bytes_accessed=10**6, transcendentals=0),
        name="give_back",
    )(y, owner)


def on_device(
    tokens,
    in_weight,
    dt_weight,
    conv_weight,
    conv_bias,
    dt_bias,
    decay_rate,
    skip_gain,
    norm_gain,
    state_cache,
    conv_cache,
    hash_owner,
    cache_slot,
    event_counts,
):
    users = tokens.shape[1]
    if in_weight.shape[0] % LANES == 0:
        dt_weight = dt_weight.T
    items, arrived = project(
        tokens.reshape(STEPS * users * EV, -1),
        in_weight,
        dt_weight,
        hash_owner[None],
        cache_slot[None],
        event_counts,
    )
    new_state, new_window, y = serve(
        arrived,
        items,
        state_cache,
        conv_cache.transpose(1, 0, 2),
        conv_weight,
        conv_bias,
        dt_bias,
        decay_rate,
        skip_gain,
        norm_gain,
    )
    return (give_back(y, hash_owner), new_state, new_window.transpose(1, 0, 2))


def solution(mesh):
    split = ("groups", "req", "fsdp")
    in_specs = (
        P(None, split, None, None),
        P(("req", "fsdp"), None),
        P(("req", "fsdp"), None),
        P(),
        P(),
        P(),
        P(),
        P(),
        P(),
        P(split, None, None),
        P(split, None, None),
        P(split),
        P(split),
        P(None, split),
    )
    out_specs = (P(None, split, None), P(split, None, None), P(split, None, None))
    return jax.shard_map(
        on_device, mesh=mesh, in_specs=in_specs, out_specs=out_specs, check_vma=False
    )
```

```python
import functools

import jax
import jax.numpy as jnp
import numpy as np
from jax import lax
from jax.experimental import pallas as pl
from jax.experimental.pallas import tpu as pltpu
from jax.sharding import PartitionSpec as P

HEADS = 64
HEAD_DIM = 64
STATE = 64
STEPS = 2
EV = 8
EVENTS = STEPS * EV
INNER = HEADS * HEAD_DIM
LANES = 128
GROUP = 8
SLOTS_PER_PAIR = 2


def order_matrix():
    out = np.zeros((EVENTS * HEAD_DIM, EVENTS * HEAD_DIM), np.float32)
    t, p = np.meshgrid(np.arange(EVENTS), np.arange(HEAD_DIM), indexing="ij")
    out[t * HEAD_DIM + p, p * EVENTS + t] = 1.0
    return jnp.asarray(out, jnp.bfloat16)


MESH = pl.DeviceIdType.MESH
TILE = 256
TAPS = 4
BLOCK = 16
FIRST = 16 - EV - (TAPS - 1)
COMBINE_LAG = 1
ROUTE_LAG = 2
LIFT_LAG = 3
CHUNKS = ((INNER, 1),) + tuple((512 * i, 2) for i in range(8))


def serve_kernel(
    n_req,
    n_fsdp,
    x_hbm,
    w_hbm,
    dt_hbm,
    cw_hbm,
    cb_hbm,
    dt_bias_hbm,
    decay_hbm,
    skip_hbm,
    gain_hbm,
    state_hbm,
    window_hbm,
    owner_hbm,
    slot_hbm,
    count_hbm,
    order_hbm,
    out_ref,
    new_state_hbm,
    new_window_ref,
    x_ref,
    dt_ref,
    cw_ref,
    cb_ref,
    dt_bias_ref,
    decay_ref,
    skip_ref,
    gain_ref,
    window_ref,
    owner_ref,
    slot_ref,
    count_ref,
    order_ref,
    state_buf,
    strips,
    x_all,
    w_all,
    own_sum,
    part_out,
    part_in,
    sum_out,
    sum_in,
    pack,
    packed,
    items,
    meta,
    meta_in,
    placing,
    live,
    by_slot,
    win_in,
    win_out,
    ext,
    stacked,
    table,
    columns,
    gains,
    a_rows,
    a_sorted,
    y_read,
    y_part,
    b_save,
    y_out,
    y_back,
    y_rows,
    flat,
    fetch_sems,
    load_sems,
    state_sem,
    store_sems,
    x_send,
    x_recv,
    w_send,
    w_recv,
    f_send,
    f_recv,
    p_send,
    p_recv,
    s_send,
    s_recv,
    i_send,
    i_recv,
    m_send,
    m_recv,
    y_send,
    y_recv,
):
    f32, bf16, i32 = jnp.float32, jnp.bfloat16, jnp.int32
    rows = x_ref.shape[0]
    users = rows // EVENTS
    depth, channels = w_hbm.shape
    cached = state_buf.shape[0]
    chips = n_req // 2
    pairs = n_fsdp // 2
    n_items = items.shape[0]
    me_r, me_z = lax.axis_index("req"), lax.axis_index("fsdp")
    me_chip, core = me_r // 2, me_r % 2
    me_pair, side = me_z // 2, me_z % 2
    sibling = {"req": me_chip * 2 + 1 - core}

    def at_req(shift):
        return lax.rem(me_r + shift + n_req, n_req)

    def at_chip(shift):
        return lax.rem(me_chip + shift + chips, chips) * 2 + core

    def at_fsdp(pair, other):
        return lax.rem(me_pair + pair + pairs, pairs) * 2 + (1 - side if other else side)

    chunks = range(len(CHUNKS))
    fsdp_shifts = [(d, o) for d in range(pairs) for o in (0, 1)][1:]

    def remote(src, dst, send, recv, device):
        return pltpu.make_async_remote_copy(
            src_ref=src,
            dst_ref=dst,
            send_sem=send,
            recv_sem=recv,
            device_id=device,
            device_id_type=MESH,
        )

    def x_copy(d, o):
        i = d * 2 + o
        target = at_fsdp(d, o)
        return remote(strips.at[target], x_all.at[i], x_send.at[i], x_recv.at[i], {"fsdp": target})

    def m_copy(d):
        target = at_req(d)
        return remote(
            meta.at[target], meta_in.at[me_r], m_send.at[d], m_recv.at[d], {"req": target}
        )

    def y_copy(d):
        target = at_req(d)
        return remote(
            y_out.at[target], y_back.at[me_r], y_send.at[d], y_recv.at[d], {"req": target}
        )

    def cols(c):
        return pl.ds(CHUNKS[c][0], CHUNKS[c][1] * TILE)

    def w_copy(c, d):
        piece = w_all.at[me_r, :, cols(c)]
        return remote(piece, piece, w_send.at[c, d], w_recv.at[c, d], {"req": at_chip(d)})

    def w_forward(c, d):
        piece = w_all.at[at_chip(-d), :, cols(c)]
        return remote(piece, piece, f_send.at[c, d], f_recv.at[c, d], sibling)

    def p_copy(c, d):
        return remote(
            part_out.at[d, :, cols(c)],
            part_in.at[d, :, cols(c)],
            p_send.at[c, d],
            p_recv.at[c, d],
            {"fsdp": at_fsdp(0, 1)},
        )

    def s_copy(c, d):
        return remote(
            sum_out.at[d, :, cols(c)],
            sum_in.at[d, :, cols(c)],
            s_send.at[c, d],
            s_recv.at[c, d],
            {"fsdp": at_fsdp(-d, 0)},
        )

    def i_copy(c, d):
        target = at_req(d)
        return remote(
            packed.at[pl.ds(target * SLOTS_PER_PAIR, SLOTS_PER_PAIR), :, cols(c)],
            items.at[pl.ds(me_r * SLOTS_PER_PAIR, SLOTS_PER_PAIR), :, cols(c)],
            i_send.at[c, d],
            i_recv.at[c, d],
            {"req": target},
        )

    def load(c):
        width = min(CHUNKS[c][1] * TILE, channels - CHUNKS[c][0])
        at = pl.ds(CHUNKS[c][0], width)
        return pltpu.make_async_copy(w_hbm.at[:, at], w_all.at[me_r, :, at], load_sems.at[c])

    early = [
        pltpu.make_async_copy(a, b, fetch_sems.at[i])
        for i, (a, b) in enumerate(
            [
                (x_hbm, x_ref),
                (dt_hbm, dt_ref),
                (owner_hbm, owner_ref),
                (slot_hbm, slot_ref),
                (count_hbm, count_ref),
            ]
        )
    ]
    late = [
        pltpu.make_async_copy(a, b, fetch_sems.at[5 + i])
        for i, (a, b) in enumerate(
            [
                (cw_hbm, cw_ref),
                (cb_hbm, cb_ref),
                (dt_bias_hbm, dt_bias_ref),
                (decay_hbm, decay_ref),
                (skip_hbm, skip_ref),
                (gain_hbm, gain_ref),
                (window_hbm, window_ref),
                (order_hbm, order_ref),
            ]
        )
    ]
    fetch_state = pltpu.make_async_copy(state_hbm, state_buf, state_sem)

    def store_state(block):
        heads = pl.ds(block * BLOCK, BLOCK)
        return pltpu.make_async_copy(
            state_buf.at[:, heads, :], new_state_hbm.at[:, heads, :], store_sems.at[block]
        )

    barrier = pltpu.get_barrier_semaphore()
    partners = [{"req": at_req(d)} for d in range(1, n_req)]
    partners += [{"fsdp": at_fsdp(d, o)} for d, o in fsdp_shifts]
    for partner in partners:
        pl.semaphore_signal(barrier, inc=1, device_id=partner, device_id_type=MESH)
    early[0].start()
    load(0).start()
    for copy in early[1:]:
        copy.start()
    for c in chunks[1:]:
        load(c).start()
    for copy in late:
        copy.start()
    fetch_state.start()
    for copy in early:
        copy.wait()
    for z in range(n_fsdp):
        for r in range(n_req):
            at = (r * n_fsdp + z) * depth
            strips[z, :, r * depth : (r + 1) * depth] = x_ref[:, at : at + depth]
    x_all[0] = strips[me_z]
    if dt_ref.shape[0] == depth:
        step_columns = jnp.concatenate(
            [dt_ref[...], jnp.zeros((depth, LANES - HEADS), bf16)], axis=1
        )
    else:
        step_columns = jnp.concatenate(
            [dt_ref[...].astype(f32), jnp.zeros((LANES - HEADS, depth), f32)], axis=0
        ).T.astype(bf16)
    w_all[me_r, :, channels:] = step_columns
    pl.semaphore_wait(barrier, len(partners))
    for d, o in fsdp_shifts:
        x_copy(d, o).start()
    for c in chunks:
        load(c).wait()
        for d in range(1, chips):
            w_copy(c, d).start()
        w_forward(c, 0).start()

    owner = [owner_ref[0:1, u : u + 1] for u in range(users)]
    rank = ranks(owner)
    high, wide = pack.shape
    row = lax.broadcasted_iota(i32, (high, wide), 0)
    col = lax.broadcasted_iota(i32, (high, wide), 1)
    user = (col // EV) % users
    hit = jnp.zeros((high, wide), jnp.bool_)
    pair_row = row // EVENTS
    for u in range(users):
        hit = hit | ((pair_row == owner[u] * SLOTS_PER_PAIR + rank[u]) & (user == u))
    same = (row % EV == col % EV) & ((row // EV) % STEPS == col // (EV * users))
    pack[...] = jnp.where(hit & same, 1.0, 0.0).astype(bf16)
    row = lax.broadcasted_iota(i32, (n_req * 8, LANES), 0)
    lane = lax.broadcasted_iota(i32, (n_req * 8, LANES), 1)
    notes = jnp.zeros((n_req * 8, LANES), i32)
    for u in range(users):
        note = jnp.where(lane == 0, slot_ref[0:1, u : u + 1] + 1, 0)
        for s in range(STEPS):
            note = jnp.where(lane == 1 + s, count_ref[s : s + 1, u : u + 1], note)
        notes = jnp.where(row == owner[u] * 8 + rank[u], note, notes)
    meta[...] = notes.reshape(meta.shape)
    for d in range(1, n_req):
        m_copy(d).start()
    meta_in[me_r] = meta[me_r]

    left = lax.broadcasted_iota(i32, (1, LANES), 1) < HEAD_DIM
    lane64 = lax.broadcasted_iota(i32, (1, LANES), 1) % HEAD_DIM
    row8 = lax.broadcasted_iota(i32, (EV, 1), 0)
    row16 = lax.broadcasted_iota(i32, (16, 1), 0)

    def both_halves(v):
        turned = pltpu.roll(v, HEAD_DIM, 1)
        return jnp.where(left, v, turned), jnp.where(left, turned, v)

    def prepare():
        for copy in late:
            copy.wait()
        win_in[...] = jnp.zeros(win_in.shape, f32)
        ext[...] = jnp.zeros(ext.shape, f32)
        for i in range(TAPS - 1):
            old = window_ref[i].astype(f32)
            for u in range(cached):
                win_in[u, FIRST + i : FIRST + i + 1, :] = old[u : u + 1]
        table[...] = jnp.zeros(table.shape, f32)
        y_part[...] = jnp.zeros(y_part.shape, f32)
        gain = gain_ref[...].reshape(1, INNER)
        for j in range(INNER // LANES):
            first, second = both_halves(gain[:, j * LANES : (j + 1) * LANES])
            gains[2 * j : 2 * j + 1, :] = first
            gains[2 * j + 1 : 2 * j + 2, :] = second

    def find_rows():
        for d in range(1, n_req):
            m_copy(d).wait_recv()
        slots = lax.broadcasted_iota(i32, (cached, 1), 0)
        counts = jnp.zeros((cached, LANES), i32)
        item = lax.broadcasted_iota(i32, (1, n_items * EVENTS), 1) // EVENTS
        goal = jnp.zeros((1, n_items * EVENTS), i32) - 1
        for i in range(n_items):
            note = meta_in[i // SLOTS_PER_PAIR, i % SLOTS_PER_PAIR : i % SLOTS_PER_PAIR + 1, :]
            slot = note[:, 0:1] - 1
            counts = jnp.where(slots == slot, note, counts)
            goal = jnp.where(item == i, slot, goal)
        live[...] = counts
        shape = (cached * EVENTS, n_items * EVENTS)
        row = lax.broadcasted_iota(i32, shape, 0)
        col = lax.broadcasted_iota(i32, shape, 1)
        match = (row // EVENTS == goal) & (row % EVENTS == col % EVENTS)
        placing[...] = jnp.where(match, 1.0, 0.0).astype(bf16)

    def forward(c):
        for d in range(1, chips):
            w_copy(c, d).wait_recv()
            w_forward(c, d).start()

    def tiles(c, body):
        def step(i, carry):
            body(pl.ds(pl.multiple_of(CHUNKS[c][0] + i * TILE, TILE), TILE))
            return carry

        lax.fori_loop(0, CHUNKS[c][1], step, 0)

    def multiply(c):
        for d in range(chips):
            w_forward(c, d).wait_recv()

        def tile(at):
            part = jnp.dot(
                x_all[...].reshape(n_fsdp * rows, n_req * depth),
                w_all[:, :, at].reshape(n_req * depth, TILE),
                preferred_element_type=f32,
            )
            for d in range(pairs):
                own_sum[d, :, at] = part[2 * d * rows : (2 * d + 1) * rows]
                part_out[d, :, at] = part[(2 * d + 1) * rows : (2 * d + 2) * rows].astype(bf16)

        tiles(c, tile)
        for d in (*range(1, pairs), 0):
            p_copy(c, d).start()

    def combine(c):
        for d in range(1, pairs):
            p_copy(c, d).wait_recv()

        def tile(at):
            for d in range(1, pairs):
                sum_out[d, :, at] = (own_sum[d, :, at] + part_in[d, :, at].astype(f32)).astype(bf16)

        tiles(c, tile)
        for d in range(1, pairs):
            s_copy(c, d).start()

    def route(c):
        p_copy(c, 0).wait_recv()
        for d in range(1, pairs):
            s_copy(c, d).wait_recv()

        def tile(at):
            total = own_sum[0, :, at] + part_in[0, :, at].astype(f32)
            for d in range(1, pairs):
                total = total + sum_in[d, :, at].astype(f32)
            chosen = jnp.dot(pack[...], total.astype(bf16), preferred_element_type=f32)
            packed[:, :, at] = chosen.reshape(-1, EVENTS, TILE).astype(bf16)
            for i in range(SLOTS_PER_PAIR):
                mine = me_r * SLOTS_PER_PAIR + i
                items[mine, :, at] = packed[mine, :, at]

        tiles(c, tile)
        for d in range(1, n_req):
            i_copy(c, d).start()

    def arrive(c):
        for d in range(1, n_req):
            i_copy(c, d).wait_recv()

        def tile(at):
            by_slot[:, at] = jnp.dot(
                placing[...],
                items[:, :, at].reshape(n_items * EVENTS, TILE),
                preferred_element_type=f32,
            ).astype(bf16)

        tiles(c, tile)

    def counts_of(u):
        note = live[pl.ds(u, 1), :]
        return [note[:, 1 + s : 2 + s] for s in range(STEPS)]

    def convolve(u, start, width):
        at = slice(start, start + width)
        counts = counts_of(u)
        mine = by_slot[pl.ds(pl.multiple_of(u * EVENTS, EVENTS), EVENTS), at].astype(f32)
        ext[0, 0:EV, :width] = win_in[u, :, at]
        bias = cb_ref[...].reshape(1, channels)[:, at]
        actives = []
        for s in range(STEPS):
            ext[s, EV : 2 * EV, :width] = mine[s * EV : (s + 1) * EV]
            conv = bias + cw_ref[0:1, at] * ext[s, FIRST : FIRST + EV, :width]
            for tap in range(1, TAPS):
                begin = FIRST + tap
                conv = conv + cw_ref[tap : tap + 1, at] * ext[s, begin : begin + EV, :width]
            actives.append(conv * (1.0 / (1.0 + jnp.exp(-conv))))
            whole = ext[s, :, :width]
            for i in range(TAPS - 1):
                wanted = (row16 == counts[s] + FIRST + i) & (row16 >= FIRST)
                kept = jnp.sum(jnp.where(wanted, whole, 0.0), axis=0, keepdims=True)
                if s + 1 < STEPS:
                    ext[s + 1, FIRST + i : FIRST + i + 1, :width] = kept
                else:
                    win_out[u, i : i + 1, at] = kept
        return actives

    def weigh(u, carry):
        counts = counts_of(u)
        actives = convolve(u, INNER, 2 * STATE)
        at = pl.ds(pl.multiple_of(u * EVENTS, EVENTS), EVENTS)
        raws = by_slot[at, channels : channels + LANES].astype(f32)[:, :HEADS]
        dt_bias = dt_bias_ref[...].reshape(1, HEADS)
        decay = decay_ref[...].reshape(1, HEADS)
        skip = skip_ref[...].reshape(1, HEADS)
        weights, totals, reads, writes, picks = [], [], [], [], []
        for s in range(STEPS):
            raw = raws[s * EV : (s + 1) * EV] + dt_bias
            size = jnp.maximum(raw, 0.0) + jnp.log1p(jnp.exp(-jnp.abs(raw)))
            size = jnp.where(row8 < counts[s], size, 0.0)
            cum = -decay * size
            for shift in (1, 2, 4):
                cum = cum + jnp.where(row8 >= shift, pltpu.roll(cum, shift, 0), 0.0)
            total = cum[EV - 1 : EV, :]
            totals.append(total)
            weights.append(jnp.exp(total - cum) * size)
            picks.append((row8 == counts[s] - 1).astype(f32))
            writes.append(actives[s][:, :STATE])
            reads.append(jnp.sum(picks[s] * actives[s][:, STATE:], axis=0, keepdims=True))
        carried = weights[0] * jnp.exp(totals[1])

        def gram(s, e):
            return jnp.sum(writes[e] * reads[s], axis=1, keepdims=True)

        table[0:8, 0:64] = weights[0] * gram(0, 0) + picks[0] * skip
        table[8:16, 0:64] = carried * gram(1, 0)
        table[16:24, 0:64] = weights[1] * gram(1, 1) + picks[1] * skip
        table[24:32, 0:64] = carried
        table[32:40, 0:64] = weights[1]
        table[40:41, 0:64] = jnp.exp(totals[0])
        table[41:42, 0:64] = jnp.exp(totals[0] + totals[1])
        table[42:43, 0:64] = reads[0]
        table[43:44, 0:64] = reads[1]
        columns[u] = table[...].T[0:64]
        for s in range(STEPS):
            b_save[u, s * EV : (s + 1) * EV, :] = jnp.concatenate([writes[s], writes[s]], axis=1)
        return carry

    wide = GROUP * STATE

    def read_old(u, carry):
        read = jnp.where(left, columns[u, :, 42:43], columns[u, :, 43:44])
        total = jnp.zeros((HEADS, LANES), f32)
        for q in range(HEAD_DIM // GROUP):
            read_block = jnp.concatenate(
                [jnp.where(lane64 == q * GROUP + i, read, 0.0) for i in range(GROUP)], axis=0
            ).astype(bf16)
            old = state_buf[u, :, q * wide : (q + 1) * wide]
            total = total + jnp.dot(old, read_block, preferred_element_type=f32)
        y_read[u] = jnp.where(left, columns[u, :, 40:41], columns[u, :, 41:42]) * total
        return carry

    def lift(block):
        heads = slice(block * BLOCK, (block + 1) * BLOCK)
        width = BLOCK * HEAD_DIM

        def one(u, carry):
            actives = convolve(u, block * width, width)
            for s in range(STEPS):
                for j in range(width // LANES):
                    first, second = both_halves(actives[s][:, j * LANES : (j + 1) * LANES])
                    at = 2 * j * EVENTS + s * EV
                    stacked[at : at + EV, :] = first
                    stacked[at + EVENTS : at + EVENTS + EV, :] = second
            mine = columns[u, heads, :]
            part = jnp.zeros((BLOCK, LANES), f32)
            for t in range(0, EVENTS, 2):
                pieces = []
                for e in (t, t + 1):
                    z = stacked[pl.ds(e, BLOCK, stride=EVENTS), :]
                    second = mine[:, 8 + e : 9 + e]
                    if e < EV:
                        coef = jnp.where(left, mine[:, e : e + 1], second)
                    else:
                        coef = jnp.where(left, 0.0, second)
                    part = part + coef * z
                    pieces.append(mine[:, 24 + e : 25 + e] * z)
                a_rows[
                    pl.ds(pl.multiple_of(u * BLOCK, BLOCK), BLOCK),
                    t * HEAD_DIM : (t + 2) * HEAD_DIM,
                ] = jnp.where(left, pieces[0], pieces[1]).astype(bf16)
            y_part[u, heads, :] = part
            return carry

        lax.fori_loop(0, cached, one, 0)

        def arrange(q, carry):
            at = pl.ds(pl.multiple_of(q * LANES, LANES), LANES)
            a_sorted[q] = jnp.dot(
                a_rows[...], order_ref[:, at], preferred_element_type=f32
            ).astype(bf16)
            return carry

        lax.fori_loop(0, HEAD_DIM // GROUP, arrange, 0)
        shape = (GROUP * EVENTS, wide)
        diagonal = lax.broadcasted_iota(i32, shape, 0) // EVENTS == (
            lax.broadcasted_iota(i32, shape, 1) // STATE
        )

        def update(u, carry):
            b_wide = jnp.concatenate([b_save[u]] * (wide // LANES), axis=1)
            b_block = jnp.where(diagonal, jnp.concatenate([b_wide] * GROUP, axis=0), 0.0)
            lhs = a_sorted[:, pl.ds(pl.multiple_of(u * BLOCK, BLOCK), BLOCK), :]
            change = jnp.dot(
                lhs.reshape(HEAD_DIM // GROUP * BLOCK, LANES),
                b_block.astype(bf16),
                preferred_element_type=f32,
            )
            decay = columns[u, heads, 41:42]
            for q in range(HEAD_DIM // GROUP):
                at = slice(q * wide, (q + 1) * wide)
                old = state_buf[u, heads, at].astype(f32)
                state_buf[u, heads, at] = (
                    decay * old + change[q * BLOCK : (q + 1) * BLOCK]
                ).astype(bf16)
            return carry

        lax.fori_loop(0, cached, update, 0)
        store_state(block).start()

    last = len(CHUNKS)
    blocks = HEADS // BLOCK
    for c in range(last + LIFT_LAG):
        if c == 0:
            forward(0)
        if c + 1 < last:
            forward(c + 1)
        if c == 0:
            for d, o in fsdp_shifts:
                x_copy(d, o).wait_recv()
        if c < last:
            multiply(c)
        if 0 <= c - COMBINE_LAG < last:
            combine(c - COMBINE_LAG)
        if c == 0:
            prepare()
        if c == 1:
            find_rows()
        if 0 <= c - ROUTE_LAG < last:
            route(c - ROUTE_LAG)
        done = c - LIFT_LAG
        if 0 <= done < last:
            arrive(done)
        if done == 0:
            lax.fori_loop(0, cached, weigh, 0)
            fetch_state.wait()
        if done == 1:
            lax.fori_loop(0, cached, read_old, 0)
        if done >= 2 and done % 2 == 0:
            lift(done // 2 - 1)

    y_rows[...] = jnp.zeros(y_rows.shape, f32)

    def norm(u, carry):
        y = y_read[u] + y_part[u]
        square = jnp.sum(y * y, axis=0, keepdims=True)
        first = jnp.sum(jnp.where(left, square, 0.0), axis=1, keepdims=True)
        second = jnp.sum(jnp.where(left, 0.0, square), axis=1, keepdims=True)
        inverse = lax.rsqrt(jnp.where(left, first, second) * (1.0 / INNER) + 1e-05)
        y = y * inverse * gains[...]
        for i in range(n_items):
            p, k = i // SLOTS_PER_PAIR, i % SLOTS_PER_PAIR
            y_rows[i] = jnp.where(meta_in[p, k : k + 1, 0:1] == u + 1, y, y_rows[i])
        return carry

    lax.fori_loop(0, cached, norm, 0)
    y_out[...] = y_rows[...].astype(bf16).reshape(y_out.shape)
    for d in range(1, n_req):
        y_copy(d).start()
    y_back[me_r] = y_out[me_r]
    for i in range(TAPS - 1):
        kept = [win_out[u, i : i + 1, :] for u in range(cached)]
        new_window_ref[i] = jnp.concatenate(kept, axis=0).astype(bf16)
    for d in range(1, n_req):
        m_copy(d).wait_send()
        for c in chunks:
            i_copy(c, d).wait_send()
    for d, o in fsdp_shifts:
        x_copy(d, o).wait_send()
    for c in chunks:
        for d in range(pairs):
            p_copy(c, d).wait_send()
        for d in range(1, pairs):
            s_copy(c, d).wait_send()
        w_forward(c, 0).wait_send()
        for d in range(1, chips):
            w_copy(c, d).wait_send()
            w_forward(c, d).wait_send()
    for d in range(1, n_req):
        y_copy(d).wait()
    for u in range(users):
        mine = jnp.zeros((HEADS, LANES), f32)
        for i in range(n_items):
            p, k = i // SLOTS_PER_PAIR, i % SLOTS_PER_PAIR
            hit = (owner[u] == p) & (rank[u] == k)
            mine = jnp.where(hit, y_back[p, k].astype(f32), mine)
        y_rows[u] = mine
        even = y_rows[u, pl.ds(0, HEADS // 2, stride=2), :]
        odd = y_rows[u, pl.ds(1, HEADS // 2, stride=2), :]
        steps = [
            jnp.where(left, even, pltpu.roll(odd, HEAD_DIM, 1)),
            jnp.where(left, pltpu.roll(even, HEAD_DIM, 1), odd),
        ]
        for s in range(STEPS):
            for j in range(INNER // LANES):
                flat[s, u : u + 1, j * LANES : (j + 1) * LANES] = steps[s][j : j + 1]
    out_ref[...] = flat[...].astype(bf16)
    for block in range(blocks):
        store_state(block).wait()


def ranks(owner):
    out = []
    for u in range(len(owner)):
        rank = jnp.zeros((1, 1), jnp.int32)
        for earlier in owner[:u]:
            rank = rank + (earlier == owner[u]).astype(jnp.int32)
        out.append(rank)
    return out


def serve(x, in_weight, dt_weight, vectors, state, window, owner, slot, counts):
    n_req, n_fsdp = lax.axis_size("req"), lax.axis_size("fsdp")
    rows = x.shape[0]
    users = rows // EVENTS
    depth, channels = in_weight.shape
    cached = state.shape[0]
    width = max(start + tiles * TILE for start, tiles in CHUNKS)
    n_items = n_req * SLOTS_PER_PAIR
    pairs = n_fsdp // 2
    f32, bf16, i32 = jnp.float32, jnp.bfloat16, jnp.int32
    vmem, hbm = pl.BlockSpec(memory_space=pltpu.VMEM), pl.BlockSpec(memory_space=pltpu.HBM)
    dma = pltpu.SemaphoreType.DMA
    n = len(CHUNKS)
    order = order_matrix()
    arrays = (x, in_weight, dt_weight, *vectors, state, window, owner, slot, counts, order)
    fetched = (x, dt_weight, *vectors, window, owner, slot, counts, order)
    return pl.pallas_call(
        functools.partial(serve_kernel, n_req, n_fsdp),
        in_specs=[hbm] * len(arrays),
        out_specs=[vmem, hbm, vmem],
        out_shape=[
            jax.ShapeDtypeStruct((STEPS, users, INNER), bf16),
            jax.ShapeDtypeStruct(state.shape, bf16),
            jax.ShapeDtypeStruct(window.shape, bf16),
        ],
        scratch_shapes=[pltpu.VMEM(a.shape, a.dtype) for a in fetched]
        + [
            pltpu.VMEM(state.shape, bf16),
            pltpu.VMEM((n_fsdp, rows, n_req * depth), bf16),
            pltpu.VMEM((n_fsdp, rows, n_req * depth), bf16),
            pltpu.VMEM((n_req, depth, width), bf16),
            pltpu.VMEM((pairs, rows, width), f32),
            pltpu.VMEM((pairs, rows, width), bf16),
            pltpu.VMEM((pairs, rows, width), bf16),
            pltpu.VMEM((pairs, rows, width), bf16),
            pltpu.VMEM((pairs, rows, width), bf16),
            pltpu.VMEM((n_items * EVENTS, rows), bf16),
            pltpu.VMEM((n_items, EVENTS, width), bf16),
            pltpu.VMEM((n_items, EVENTS, width), bf16),
            pltpu.VMEM((n_req, 8, LANES), i32),
            pltpu.VMEM((n_req, 8, LANES), i32),
            pltpu.VMEM((cached * EVENTS, n_items * EVENTS), bf16),
            pltpu.VMEM((cached, LANES), i32),
            pltpu.VMEM((cached * EVENTS, width), bf16),
            pltpu.VMEM((cached, EV, channels), f32),
            pltpu.VMEM((cached, EV, channels), f32),
            pltpu.VMEM((STEPS, 2 * EV, BLOCK * HEAD_DIM), f32),
            pltpu.VMEM((BLOCK * EVENTS, LANES), f32),
            pltpu.VMEM((LANES, LANES), f32),
            pltpu.VMEM((cached, HEADS, LANES), f32),
            pltpu.VMEM((HEADS, LANES), f32),
            pltpu.VMEM((cached * BLOCK, EVENTS * HEAD_DIM), bf16),
            pltpu.VMEM((HEAD_DIM // GROUP, cached * BLOCK, LANES), bf16),
            pltpu.VMEM((cached, HEADS, LANES), f32),
            pltpu.VMEM((cached, HEADS, LANES), f32),
            pltpu.VMEM((cached, EVENTS, LANES), f32),
            pltpu.VMEM((n_req, SLOTS_PER_PAIR, HEADS, LANES), bf16),
            pltpu.VMEM((n_req, SLOTS_PER_PAIR, HEADS, LANES), bf16),
            pltpu.VMEM((n_items, HEADS, LANES), f32),
            pltpu.VMEM((STEPS, users, INNER), f32),
            dma((len(fetched),)),
            dma((n,)),
            dma(()),
            dma((HEADS // BLOCK,)),
            dma((n_fsdp,)),
            dma((n_fsdp,)),
            dma((n, n_req // 2)),
            dma((n, n_req // 2)),
            dma((n, n_req // 2)),
            dma((n, n_req // 2)),
            dma((n, pairs)),
            dma((n, pairs)),
            dma((n, pairs)),
            dma((n, pairs)),
            dma((n, n_req)),
            dma((n, n_req)),
            dma((n_req,)),
            dma((n_req,)),
            dma((n_req,)),
            dma((n_req,)),
        ],
        compiler_params=pltpu.CompilerParams(
            collective_id=0, has_side_effects=True, vmem_limit_bytes=56 * 2**20
        ),
        cost_estimate=pl.CostEstimate(flops=7 * 10**9, bytes_accessed=10**7, transcendentals=0),
        name="serve",
    )(*arrays)


def on_device(
    tokens,
    in_weight,
    dt_weight,
    conv_weight,
    conv_bias,
    dt_bias,
    decay_rate,
    skip_gain,
    norm_gain,
    state_cache,
    conv_cache,
    hash_owner,
    cache_slot,
    event_counts,
):
    users = tokens.shape[1]
    if in_weight.shape[0] % LANES == 0:
        dt_weight = dt_weight.T
    vectors = (conv_weight, conv_bias, dt_bias, decay_rate, skip_gain, norm_gain)
    out, new_state, new_window = serve(
        tokens.reshape(STEPS * users * EV, -1),
        in_weight,
        dt_weight,
        vectors,
        state_cache,
        conv_cache.transpose(1, 0, 2),
        hash_owner[None],
        cache_slot[None],
        event_counts,
    )
    return (out, new_state, new_window.transpose(1, 0, 2))


def solution(mesh):
    split = ("groups", "req", "fsdp")
    in_specs = (
        P(None, split, None, None),
        P(("req", "fsdp"), None),
        P(("req", "fsdp"), None),
        P(),
        P(),
        P(),
        P(),
        P(),
        P(),
        P(split, None, None),
        P(split, None, None),
        P(split),
        P(split),
        P(None, split),
    )
    out_specs = (P(None, split, None), P(split, None, None), P(split, None, None))
    return jax.shard_map(
        on_device, mesh=mesh, in_specs=in_specs, out_specs=out_specs, check_vma=False
    )
```

```python
import functools

import jax
import jax.numpy as jnp
import numpy as np
from jax import lax
from jax.experimental import pallas as pl
from jax.experimental.pallas import tpu as pltpu
from jax.sharding import PartitionSpec as P

HEADS = 64
HEAD_DIM = 64
STATE = 64
STEPS = 2
EV = 8
EVENTS = STEPS * EV
INNER = HEADS * HEAD_DIM
LANES = 128
GROUP = 8
SLOTS_PER_PAIR = 2


def order_matrix():
    out = np.zeros((EVENTS * HEAD_DIM, EVENTS * HEAD_DIM), np.float32)
    t, p = np.meshgrid(np.arange(EVENTS), np.arange(HEAD_DIM), indexing="ij")
    out[t * HEAD_DIM + p, p * EVENTS + t] = 1.0
    return jnp.asarray(out, jnp.bfloat16)


MESH = pl.DeviceIdType.MESH
TILE = 256
TAPS = 4
BLOCK = 16
FIRST = 16 - EV - (TAPS - 1)
COMBINE_LAG = 2
ROUTE_LAG = 4
LIFT_LAG = 6
AHEAD = 3
CHUNKS = ((INNER, 1),) + tuple((512 * i, 2) for i in range(8))


def serve_kernel(
    n_req,
    n_fsdp,
    x_hbm,
    w_hbm,
    dt_hbm,
    cw_hbm,
    cb_hbm,
    dt_bias_hbm,
    decay_hbm,
    skip_hbm,
    gain_hbm,
    state_hbm,
    window_hbm,
    owner_hbm,
    slot_hbm,
    count_hbm,
    out_ref,
    a_rows,
    columns,
    b_save,
    win_out,
    x_ref,
    dt_ref,
    cw_ref,
    cb_ref,
    dt_bias_ref,
    decay_ref,
    skip_ref,
    gain_ref,
    window_ref,
    owner_ref,
    slot_ref,
    count_ref,
    state_buf,
    strips,
    x_all,
    w_all,
    own_sum,
    part_out,
    part_in,
    sum_out,
    sum_in,
    pack,
    packed,
    items,
    meta,
    meta_in,
    placing,
    live,
    by_slot,
    win_in,
    ext,
    stacked,
    table,
    gains,
    y_read,
    y_part,
    y_out,
    y_back,
    y_rows,
    flat,
    fetch_sems,
    load_sems,
    state_sem,
    x_send,
    x_recv,
    w_send,
    w_recv,
    f_send,
    f_recv,
    p_send,
    p_recv,
    s_send,
    s_recv,
    i_send,
    i_recv,
    m_send,
    m_recv,
    y_send,
    y_recv,
):
    f32, bf16, i32 = jnp.float32, jnp.bfloat16, jnp.int32
    rows = x_ref.shape[0]
    users = rows // EVENTS
    depth, channels = w_hbm.shape
    cached = state_buf.shape[0]
    chips = n_req // 2
    pairs = n_fsdp // 2
    n_items = items.shape[0]
    me_r, me_z = lax.axis_index("req"), lax.axis_index("fsdp")
    me_chip, core = me_r // 2, me_r % 2
    me_pair, side = me_z // 2, me_z % 2
    sibling = {"req": me_chip * 2 + 1 - core}

    def at_req(shift):
        return lax.rem(me_r + shift + n_req, n_req)

    def at_chip(shift):
        return lax.rem(me_chip + shift + chips, chips) * 2 + core

    def at_fsdp(pair, other):
        return lax.rem(me_pair + pair + pairs, pairs) * 2 + (1 - side if other else side)

    chunks = range(len(CHUNKS))
    fsdp_shifts = [(d, o) for d in range(pairs) for o in (0, 1)][1:]

    def remote(src, dst, send, recv, device):
        return pltpu.make_async_remote_copy(
            src_ref=src,
            dst_ref=dst,
            send_sem=send,
            recv_sem=recv,
            device_id=device,
            device_id_type=MESH,
        )

    def x_copy(d, o):
        i = d * 2 + o
        target = at_fsdp(d, o)
        return remote(strips.at[target], x_all.at[i], x_send.at[i], x_recv.at[i], {"fsdp": target})

    def m_copy(d):
        target = at_req(d)
        return remote(
            meta.at[target], meta_in.at[me_r], m_send.at[d], m_recv.at[d], {"req": target}
        )

    def y_copy(d):
        target = at_req(d)
        return remote(
            y_out.at[target], y_back.at[me_r], y_send.at[d], y_recv.at[d], {"req": target}
        )

    def cols(c):
        return pl.ds(CHUNKS[c][0], CHUNKS[c][1] * TILE)

    def w_copy(c, d):
        piece = w_all.at[me_r, :, cols(c)]
        return remote(piece, piece, w_send.at[c, d], w_recv.at[c, d], {"req": at_chip(d)})

    def w_forward(c, d):
        piece = w_all.at[at_chip(-d), :, cols(c)]
        return remote(piece, piece, f_send.at[c, d], f_recv.at[c, d], sibling)

    def p_copy(c, d):
        return remote(
            part_out.at[d, :, cols(c)],
            part_in.at[d, :, cols(c)],
            p_send.at[c, d],
            p_recv.at[c, d],
            {"fsdp": at_fsdp(0, 1)},
        )

    def s_copy(c, d):
        return remote(
            sum_out.at[d, :, cols(c)],
            sum_in.at[d, :, cols(c)],
            s_send.at[c, d],
            s_recv.at[c, d],
            {"fsdp": at_fsdp(-d, 0)},
        )

    def i_copy(c, d):
        target = at_req(d)
        return remote(
            packed.at[pl.ds(target * SLOTS_PER_PAIR, SLOTS_PER_PAIR), :, cols(c)],
            items.at[pl.ds(me_r * SLOTS_PER_PAIR, SLOTS_PER_PAIR), :, cols(c)],
            i_send.at[c, d],
            i_recv.at[c, d],
            {"req": target},
        )

    def load(c):
        width = min(CHUNKS[c][1] * TILE, channels - CHUNKS[c][0])
        at = pl.ds(CHUNKS[c][0], width)
        return pltpu.make_async_copy(w_hbm.at[:, at], w_all.at[me_r, :, at], load_sems.at[c])

    early = [
        pltpu.make_async_copy(a, b, fetch_sems.at[i])
        for i, (a, b) in enumerate(
            [
                (x_hbm, x_ref),
                (dt_hbm, dt_ref),
                (owner_hbm, owner_ref),
                (slot_hbm, slot_ref),
                (count_hbm, count_ref),
            ]
        )
    ]
    late = [
        pltpu.make_async_copy(a, b, fetch_sems.at[5 + i])
        for i, (a, b) in enumerate(
            [
                (cw_hbm, cw_ref),
                (cb_hbm, cb_ref),
                (dt_bias_hbm, dt_bias_ref),
                (decay_hbm, decay_ref),
                (skip_hbm, skip_ref),
                (gain_hbm, gain_ref),
                (window_hbm, window_ref),
            ]
        )
    ]
    fetch_state = pltpu.make_async_copy(state_hbm, state_buf, state_sem)

    barrier = pltpu.get_barrier_semaphore()
    partners = [{"req": at_req(d)} for d in range(1, n_req)]
    partners += [{"fsdp": at_fsdp(d, o)} for d, o in fsdp_shifts]
    for partner in partners:
        pl.semaphore_signal(barrier, inc=1, device_id=partner, device_id_type=MESH)
    early[0].start()
    load(0).start()
    for copy in early[1:]:
        copy.start()
    for c in chunks[1:]:
        load(c).start()
    for copy in early:
        copy.wait()
    for z in range(n_fsdp):
        for r in range(n_req):
            at = (r * n_fsdp + z) * depth
            strips[z, :, r * depth : (r + 1) * depth] = x_ref[:, at : at + depth]
    x_all[0] = strips[me_z]
    if dt_ref.shape[0] == depth:
        step_columns = jnp.concatenate(
            [dt_ref[...], jnp.zeros((depth, LANES - HEADS), bf16)], axis=1
        )
    else:
        step_columns = jnp.concatenate(
            [dt_ref[...].astype(f32), jnp.zeros((LANES - HEADS, depth), f32)], axis=0
        ).T.astype(bf16)
    w_all[me_r, :, channels:] = step_columns
    pl.semaphore_wait(barrier, len(partners))
    for d, o in fsdp_shifts:
        x_copy(d, o).start()

    def spread(c):
        load(c).wait()
        for d in range(1, chips):
            w_copy(c, d).start()
        w_forward(c, 0).start()

    for c in chunks[:AHEAD]:
        spread(c)
    for copy in late:
        copy.start()
    fetch_state.start()

    owner = [owner_ref[0:1, u : u + 1] for u in range(users)]
    rank = ranks(owner)
    high, wide = pack.shape
    row = lax.broadcasted_iota(i32, (high, wide), 0)
    col = lax.broadcasted_iota(i32, (high, wide), 1)
    user = (col // EV) % users
    hit = jnp.zeros((high, wide), jnp.bool_)
    pair_row = row // EVENTS
    for u in range(users):
        hit = hit | ((pair_row == owner[u] * SLOTS_PER_PAIR + rank[u]) & (user == u))
    same = (row % EV == col % EV) & ((row // EV) % STEPS == col // (EV * users))
    pack[...] = jnp.where(hit & same, 1.0, 0.0).astype(bf16)
    row = lax.broadcasted_iota(i32, (n_req * 8, LANES), 0)
    lane = lax.broadcasted_iota(i32, (n_req * 8, LANES), 1)
    notes = jnp.zeros((n_req * 8, LANES), i32)
    for u in range(users):
        note = jnp.where(lane == 0, slot_ref[0:1, u : u + 1] + 1, 0)
        for s in range(STEPS):
            note = jnp.where(lane == 1 + s, count_ref[s : s + 1, u : u + 1], note)
        notes = jnp.where(row == owner[u] * 8 + rank[u], note, notes)
    meta[...] = notes.reshape(meta.shape)
    for d in range(1, n_req):
        m_copy(d).start()
    meta_in[me_r] = meta[me_r]

    left = lax.broadcasted_iota(i32, (1, LANES), 1) < HEAD_DIM
    lane64 = lax.broadcasted_iota(i32, (1, LANES), 1) % HEAD_DIM
    row8 = lax.broadcasted_iota(i32, (EV, 1), 0)
    row16 = lax.broadcasted_iota(i32, (16, 1), 0)

    def both_halves(v):
        turned = pltpu.roll(v, HEAD_DIM, 1)
        return jnp.where(left, v, turned), jnp.where(left, turned, v)

    def prepare():
        for copy in late:
            copy.wait()
        win_in[...] = jnp.zeros(win_in.shape, f32)
        ext[...] = jnp.zeros(ext.shape, f32)
        for i in range(TAPS - 1):
            old = window_ref[i].astype(f32)
            for u in range(cached):
                win_in[u, FIRST + i : FIRST + i + 1, :] = old[u : u + 1]
        table[...] = jnp.zeros(table.shape, f32)
        y_part[...] = jnp.zeros(y_part.shape, f32)
        gain = gain_ref[...].reshape(1, INNER)
        for j in range(INNER // LANES):
            first, second = both_halves(gain[:, j * LANES : (j + 1) * LANES])
            gains[2 * j : 2 * j + 1, :] = first
            gains[2 * j + 1 : 2 * j + 2, :] = second

    def find_rows():
        for d in range(1, n_req):
            m_copy(d).wait_recv()
        slots = lax.broadcasted_iota(i32, (cached, 1), 0)
        counts = jnp.zeros((cached, LANES), i32)
        item = lax.broadcasted_iota(i32, (1, n_items * EVENTS), 1) // EVENTS
        goal = jnp.zeros((1, n_items * EVENTS), i32) - 1
        for i in range(n_items):
            note = meta_in[i // SLOTS_PER_PAIR, i % SLOTS_PER_PAIR : i % SLOTS_PER_PAIR + 1, :]
            slot = note[:, 0:1] - 1
            counts = jnp.where(slots == slot, note, counts)
            goal = jnp.where(item == i, slot, goal)
        live[...] = counts
        shape = (cached * EVENTS, n_items * EVENTS)
        row = lax.broadcasted_iota(i32, shape, 0)
        col = lax.broadcasted_iota(i32, shape, 1)
        match = (row // EVENTS == goal) & (row % EVENTS == col % EVENTS)
        placing[...] = jnp.where(match, 1.0, 0.0).astype(bf16)

    def forward(c):
        for d in range(1, chips):
            w_copy(c, d).wait_recv()
            w_forward(c, d).start()

    def tiles(c, body):
        def step(i, carry):
            body(pl.ds(pl.multiple_of(CHUNKS[c][0] + i * TILE, TILE), TILE))
            return carry

        lax.fori_loop(0, CHUNKS[c][1], step, 0)

    def multiply(c):
        for d in range(chips):
            w_forward(c, d).wait_recv()

        def tile(at):
            part = jnp.dot(
                x_all[...].reshape(n_fsdp * rows, n_req * depth),
                w_all[:, :, at].reshape(n_req * depth, TILE),
                preferred_element_type=f32,
            )
            for d in range(pairs):
                own_sum[d, :, at] = part[2 * d * rows : (2 * d + 1) * rows]
                part_out[d, :, at] = part[(2 * d + 1) * rows : (2 * d + 2) * rows].astype(bf16)

        tiles(c, tile)
        for d in (*range(1, pairs), 0):
            p_copy(c, d).start()

    def combine(c):
        for d in range(1, pairs):
            p_copy(c, d).wait_recv()

        def tile(at):
            for d in range(1, pairs):
                sum_out[d, :, at] = (own_sum[d, :, at] + part_in[d, :, at].astype(f32)).astype(bf16)

        tiles(c, tile)
        for d in range(1, pairs):
            s_copy(c, d).start()

    def route(c):
        p_copy(c, 0).wait_recv()
        for d in range(1, pairs):
            s_copy(c, d).wait_recv()

        def tile(at):
            total = own_sum[0, :, at] + part_in[0, :, at].astype(f32)
            for d in range(1, pairs):
                total = total + sum_in[d, :, at].astype(f32)
            chosen = jnp.dot(pack[...], total.astype(bf16), preferred_element_type=f32)
            packed[:, :, at] = chosen.reshape(-1, EVENTS, TILE).astype(bf16)
            for i in range(SLOTS_PER_PAIR):
                mine = me_r * SLOTS_PER_PAIR + i
                items[mine, :, at] = packed[mine, :, at]

        tiles(c, tile)
        for d in range(1, n_req):
            i_copy(c, d).start()

    def arrive(c):
        for d in range(1, n_req):
            i_copy(c, d).wait_recv()

        def tile(at):
            by_slot[:, at] = jnp.dot(
                placing[...],
                items[:, :, at].reshape(n_items * EVENTS, TILE),
                preferred_element_type=f32,
            ).astype(bf16)

        tiles(c, tile)

    def counts_of(u):
        note = live[pl.ds(u, 1), :]
        return [note[:, 1 + s : 2 + s] for s in range(STEPS)]

    def convolve(u, start, width):
        at = slice(start, start + width)
        counts = counts_of(u)
        mine = by_slot[pl.ds(pl.multiple_of(u * EVENTS, EVENTS), EVENTS), at].astype(f32)
        ext[0, 0:EV, :width] = win_in[u, :, at]
        bias = cb_ref[...].reshape(1, channels)[:, at]
        actives = []
        for s in range(STEPS):
            ext[s, EV : 2 * EV, :width] = mine[s * EV : (s + 1) * EV]
            conv = bias + cw_ref[0:1, at] * ext[s, FIRST : FIRST + EV, :width]
            for tap in range(1, TAPS):
                begin = FIRST + tap
                conv = conv + cw_ref[tap : tap + 1, at] * ext[s, begin : begin + EV, :width]
            actives.append(conv * (1.0 / (1.0 + jnp.exp(-conv))))
            whole = ext[s, :, :width]
            for i in range(TAPS - 1):
                wanted = (row16 == counts[s] + FIRST + i) & (row16 >= FIRST)
                kept = jnp.sum(jnp.where(wanted, whole, 0.0), axis=0, keepdims=True)
                if s + 1 < STEPS:
                    ext[s + 1, FIRST + i : FIRST + i + 1, :width] = kept
                else:
                    win_out[u, i : i + 1, at] = kept
        return actives

    def weigh(u, carry):
        counts = counts_of(u)
        actives = convolve(u, INNER, 2 * STATE)
        at = pl.ds(pl.multiple_of(u * EVENTS, EVENTS), EVENTS)
        raws = by_slot[at, channels : channels + LANES].astype(f32)[:, :HEADS]
        dt_bias = dt_bias_ref[...].reshape(1, HEADS)
        decay = decay_ref[...].reshape(1, HEADS)
        skip = skip_ref[...].reshape(1, HEADS)
        weights, totals, reads, writes, picks = [], [], [], [], []
        for s in range(STEPS):
            raw = raws[s * EV : (s + 1) * EV] + dt_bias
            size = jnp.maximum(raw, 0.0) + jnp.log1p(jnp.exp(-jnp.abs(raw)))
            size = jnp.where(row8 < counts[s], size, 0.0)
            cum = -decay * size
            for shift in (1, 2, 4):
                cum = cum + jnp.where(row8 >= shift, pltpu.roll(cum, shift, 0), 0.0)
            total = cum[EV - 1 : EV, :]
            totals.append(total)
            weights.append(jnp.exp(total - cum) * size)
            picks.append((row8 == counts[s] - 1).astype(f32))
            writes.append(actives[s][:, :STATE])
            reads.append(jnp.sum(picks[s] * actives[s][:, STATE:], axis=0, keepdims=True))
        carried = weights[0] * jnp.exp(totals[1])

        def gram(s, e):
            return jnp.sum(writes[e] * reads[s], axis=1, keepdims=True)

        table[0:8, 0:64] = weights[0] * gram(0, 0) + picks[0] * skip
        table[8:16, 0:64] = carried * gram(1, 0)
        table[16:24, 0:64] = weights[1] * gram(1, 1) + picks[1] * skip
        table[24:32, 0:64] = carried
        table[32:40, 0:64] = weights[1]
        table[40:41, 0:64] = jnp.exp(totals[0])
        table[41:42, 0:64] = jnp.exp(totals[0] + totals[1])
        table[42:43, 0:64] = reads[0]
        table[43:44, 0:64] = reads[1]
        columns[u] = table[...].T[0:64]
        for s in range(STEPS):
            b_save[u, s * EV : (s + 1) * EV, :] = jnp.concatenate([writes[s], writes[s]], axis=1)
        return carry

    wide = GROUP * STATE

    def read_old(u, carry):
        read = jnp.where(left, columns[u, :, 42:43], columns[u, :, 43:44])
        total = jnp.zeros((HEADS, LANES), f32)
        for q in range(HEAD_DIM // GROUP):
            read_block = jnp.concatenate(
                [jnp.where(lane64 == q * GROUP + i, read, 0.0) for i in range(GROUP)], axis=0
            ).astype(bf16)
            old = state_buf[u, :, q * wide : (q + 1) * wide]
            total = total + jnp.dot(old, read_block, preferred_element_type=f32)
        y_read[u] = jnp.where(left, columns[u, :, 40:41], columns[u, :, 41:42]) * total
        return carry

    def lift(block):
        heads = slice(block * BLOCK, (block + 1) * BLOCK)
        width = BLOCK * HEAD_DIM

        def one(u, carry):
            actives = convolve(u, block * width, width)
            for s in range(STEPS):
                for j in range(width // LANES):
                    first, second = both_halves(actives[s][:, j * LANES : (j + 1) * LANES])
                    at = 2 * j * EVENTS + s * EV
                    stacked[at : at + EV, :] = first
                    stacked[at + EVENTS : at + EVENTS + EV, :] = second
            mine = columns[u, heads, :]
            part = jnp.zeros((BLOCK, LANES), f32)
            for t in range(0, EVENTS, 2):
                pieces = []
                for e in (t, t + 1):
                    z = stacked[pl.ds(e, BLOCK, stride=EVENTS), :]
                    second = mine[:, 8 + e : 9 + e]
                    if e < EV:
                        coef = jnp.where(left, mine[:, e : e + 1], second)
                    else:
                        coef = jnp.where(left, 0.0, second)
                    part = part + coef * z
                    pieces.append(mine[:, 24 + e : 25 + e] * z)
                at = pl.multiple_of(u * HEADS + block * BLOCK, BLOCK)
                a_rows[pl.ds(at, BLOCK), t * HEAD_DIM : (t + 2) * HEAD_DIM] = jnp.where(left, pieces[0], pieces[1]).astype(bf16)
            y_part[u, heads, :] = part
            return carry

        lax.fori_loop(0, cached, one, 0)

    last = len(CHUNKS)
    forward(0)
    prepare()
    for c in range(last + LIFT_LAG):
        if c + AHEAD < last:
            spread(c + AHEAD)
        if c + 1 < last:
            forward(c + 1)
        if c == 0:
            for d, o in fsdp_shifts:
                x_copy(d, o).wait_recv()
        if c < last:
            multiply(c)
        if 0 <= c - COMBINE_LAG < last:
            combine(c - COMBINE_LAG)
        if c == 2:
            find_rows()
        if 0 <= c - ROUTE_LAG < last:
            route(c - ROUTE_LAG)
        done = c - LIFT_LAG
        if 0 <= done < last:
            arrive(done)
        if done == 0:
            lax.fori_loop(0, cached, weigh, 0)
            fetch_state.wait()
        if done == 1:
            lax.fori_loop(0, cached // 2, read_old, 0)
        if done == 3:
            lax.fori_loop(cached // 2, cached, read_old, 0)
        if done >= 2 and done % 2 == 0:
            lift(done // 2 - 1)

    y_rows[...] = jnp.zeros(y_rows.shape, f32)

    def norm(u, carry):
        y = y_read[u] + y_part[u]
        square = jnp.sum(y * y, axis=0, keepdims=True)
        first = jnp.sum(jnp.where(left, square, 0.0), axis=1, keepdims=True)
        second = jnp.sum(jnp.where(left, 0.0, square), axis=1, keepdims=True)
        inverse = lax.rsqrt(jnp.where(left, first, second) * (1.0 / INNER) + 1e-05)
        y = y * inverse * gains[...]
        for i in range(n_items):
            p, k = i // SLOTS_PER_PAIR, i % SLOTS_PER_PAIR
            y_rows[i] = jnp.where(meta_in[p, k : k + 1, 0:1] == u + 1, y, y_rows[i])
        return carry

    lax.fori_loop(0, cached, norm, 0)
    y_out[...] = y_rows[...].astype(bf16).reshape(y_out.shape)
    for d in range(1, n_req):
        y_copy(d).start()
    y_back[me_r] = y_out[me_r]
    for d in range(1, n_req):
        m_copy(d).wait_send()
        for c in chunks:
            i_copy(c, d).wait_send()
    for d, o in fsdp_shifts:
        x_copy(d, o).wait_send()
    for c in chunks:
        for d in range(pairs):
            p_copy(c, d).wait_send()
        for d in range(1, pairs):
            s_copy(c, d).wait_send()
        w_forward(c, 0).wait_send()
        for d in range(1, chips):
            w_copy(c, d).wait_send()
            w_forward(c, d).wait_send()
    for d in range(1, n_req):
        y_copy(d).wait()
    for u in range(users):
        mine = jnp.zeros((HEADS, LANES), f32)
        for i in range(n_items):
            p, k = i // SLOTS_PER_PAIR, i % SLOTS_PER_PAIR
            hit = (owner[u] == p) & (rank[u] == k)
            mine = jnp.where(hit, y_back[p, k].astype(f32), mine)
        y_rows[u] = mine
        even = y_rows[u, pl.ds(0, HEADS // 2, stride=2), :]
        odd = y_rows[u, pl.ds(1, HEADS // 2, stride=2), :]
        steps = [
            jnp.where(left, even, pltpu.roll(odd, HEAD_DIM, 1)),
            jnp.where(left, pltpu.roll(even, HEAD_DIM, 1), odd),
        ]
        for s in range(STEPS):
            for j in range(INNER // LANES):
                flat[s, u : u + 1, j * LANES : (j + 1) * LANES] = steps[s][j : j + 1]
    out_ref[...] = flat[...].astype(bf16)


def ranks(owner):
    out = []
    for u in range(len(owner)):
        rank = jnp.zeros((1, 1), jnp.int32)
        for earlier in owner[:u]:
            rank = rank + (earlier == owner[u]).astype(jnp.int32)
        out.append(rank)
    return out


def serve(x, in_weight, dt_weight, vectors, state, window, owner, slot, counts):
    n_req, n_fsdp = lax.axis_size("req"), lax.axis_size("fsdp")
    rows = x.shape[0]
    users = rows // EVENTS
    depth, channels = in_weight.shape
    cached = state.shape[0]
    width = max(start + tiles * TILE for start, tiles in CHUNKS)
    n_items = n_req * SLOTS_PER_PAIR
    pairs = n_fsdp // 2
    f32, bf16, i32 = jnp.float32, jnp.bfloat16, jnp.int32
    vmem, hbm = pl.BlockSpec(memory_space=pltpu.VMEM), pl.BlockSpec(memory_space=pltpu.HBM)
    dma = pltpu.SemaphoreType.DMA
    n = len(CHUNKS)
    arrays = (x, in_weight, dt_weight, *vectors, state, window, owner, slot, counts)
    fetched = (x, dt_weight, *vectors, window, owner, slot, counts)
    return pl.pallas_call(
        functools.partial(serve_kernel, n_req, n_fsdp),
        in_specs=[hbm] * len(arrays),
        out_specs=[vmem] * 5,
        out_shape=[
            jax.ShapeDtypeStruct((STEPS, users, INNER), bf16),
            jax.ShapeDtypeStruct((cached * HEADS, EVENTS * HEAD_DIM), bf16),
            jax.ShapeDtypeStruct((cached, HEADS, LANES), f32),
            jax.ShapeDtypeStruct((cached, EVENTS, LANES), f32),
            jax.ShapeDtypeStruct((cached, EV, channels), f32),
        ],
        scratch_shapes=[pltpu.VMEM(a.shape, a.dtype) for a in fetched]
        + [
            pltpu.VMEM(state.shape, bf16),
            pltpu.VMEM((n_fsdp, rows, n_req * depth), bf16),
            pltpu.VMEM((n_fsdp, rows, n_req * depth), bf16),
            pltpu.VMEM((n_req, depth, width), bf16),
            pltpu.VMEM((pairs, rows, width), f32),
            pltpu.VMEM((pairs, rows, width), bf16),
            pltpu.VMEM((pairs, rows, width), bf16),
            pltpu.VMEM((pairs, rows, width), bf16),
            pltpu.VMEM((pairs, rows, width), bf16),
            pltpu.VMEM((n_items * EVENTS, rows), bf16),
            pltpu.VMEM((n_items, EVENTS, width), bf16),
            pltpu.VMEM((n_items, EVENTS, width), bf16),
            pltpu.VMEM((n_req, 8, LANES), i32),
            pltpu.VMEM((n_req, 8, LANES), i32),
            pltpu.VMEM((cached * EVENTS, n_items * EVENTS), bf16),
            pltpu.VMEM((cached, LANES), i32),
            pltpu.VMEM((cached * EVENTS, width), bf16),
            pltpu.VMEM((cached, EV, channels), f32),
            pltpu.VMEM((STEPS, 2 * EV, BLOCK * HEAD_DIM), f32),
            pltpu.VMEM((BLOCK * EVENTS, LANES), f32),
            pltpu.VMEM((LANES, LANES), f32),
            pltpu.VMEM((HEADS, LANES), f32),
            pltpu.VMEM((cached, HEADS, LANES), f32),
            pltpu.VMEM((cached, HEADS, LANES), f32),
            pltpu.VMEM((n_req, SLOTS_PER_PAIR, HEADS, LANES), bf16),
            pltpu.VMEM((n_req, SLOTS_PER_PAIR, HEADS, LANES), bf16),
            pltpu.VMEM((n_items, HEADS, LANES), f32),
            pltpu.VMEM((STEPS, users, INNER), f32),
            dma((len(fetched),)),
            dma((n,)),
            dma(()),
            dma((n_fsdp,)),
            dma((n_fsdp,)),
            dma((n, n_req // 2)),
            dma((n, n_req // 2)),
            dma((n, n_req // 2)),
            dma((n, n_req // 2)),
            dma((n, pairs)),
            dma((n, pairs)),
            dma((n, pairs)),
            dma((n, pairs)),
            dma((n, n_req)),
            dma((n, n_req)),
            dma((n_req,)),
            dma((n_req,)),
            dma((n_req,)),
            dma((n_req,)),
        ],
        compiler_params=pltpu.CompilerParams(
            collective_id=0, has_side_effects=True, vmem_limit_bytes=60 * 2**20
        ),
        cost_estimate=pl.CostEstimate(flops=7 * 10**9, bytes_accessed=10**7, transcendentals=0),
        name="serve",
    )(*arrays)


def store_kernel(
    state_hbm,
    a_hbm,
    columns_hbm,
    b_hbm,
    win_hbm,
    order_hbm,
    new_state_hbm,
    new_window_ref,
    a_ref,
    columns_ref,
    b_ref,
    win_ref,
    order_ref,
    state_buf,
    a_sorted,
    fetch_sems,
    in_sems,
    out_sems,
):
    f32, bf16 = jnp.float32, jnp.bfloat16
    cached = state_buf.shape[0]
    groups = HEAD_DIM // GROUP
    wide = GROUP * STATE

    def state_in(u):
        return pltpu.make_async_copy(state_hbm.at[u], state_buf.at[u], in_sems.at[u])

    def state_out(u):
        return pltpu.make_async_copy(state_buf.at[u], new_state_hbm.at[u], out_sems.at[u])

    pairs = [(order_hbm, order_ref), (a_hbm, a_ref), (columns_hbm, columns_ref), (b_hbm, b_ref)]
    pairs.append((win_hbm, win_ref))
    fetches = [pltpu.make_async_copy(a, b, fetch_sems.at[i]) for i, (a, b) in enumerate(pairs)]
    for fetch in fetches[:-1]:
        fetch.start()
    for u in range(cached):
        state_in(u).start()
    fetches[-1].start()
    for fetch in fetches[:-1]:
        fetch.wait()

    def arrange(q, carry):
        at = pl.ds(pl.multiple_of(q * LANES, LANES), LANES)
        a_sorted[q] = jnp.dot(a_ref[...], order_ref[:, at], preferred_element_type=f32).astype(bf16)
        return carry

    lax.fori_loop(0, groups, arrange, 0)
    shape = (GROUP * EVENTS, wide)
    diagonal = lax.broadcasted_iota(jnp.int32, shape, 0) // EVENTS == (
        lax.broadcasted_iota(jnp.int32, shape, 1) // STATE
    )

    def update(u, carry):
        b_wide = jnp.concatenate([b_ref[u]] * (wide // LANES), axis=1)
        b_block = jnp.where(diagonal, jnp.concatenate([b_wide] * GROUP, axis=0), 0.0)
        lhs = a_sorted[:, pl.ds(pl.multiple_of(u * HEADS, HEADS), HEADS), :]
        change = jnp.dot(
            lhs.reshape(groups * HEADS, LANES), b_block.astype(bf16), preferred_element_type=f32
        )
        decay = columns_ref[u, :, 41:42]
        state_in(u).wait()
        for q in range(groups):
            at = slice(q * wide, (q + 1) * wide)
            old = state_buf[u, :, at].astype(f32)
            state_buf[u, :, at] = (decay * old + change[q * HEADS : (q + 1) * HEADS]).astype(bf16)
        state_out(u).start()
        return carry

    lax.fori_loop(0, cached, update, 0)
    fetches[-1].wait()
    for i in range(TAPS - 1):
        kept = [win_ref[u, i : i + 1, :] for u in range(cached)]
        new_window_ref[i] = jnp.concatenate(kept, axis=0).astype(bf16)
    for u in range(cached):
        state_out(u).wait()


def store(state, a_rows, columns, b_save, win_out, window):
    vmem, hbm = pl.BlockSpec(memory_space=pltpu.VMEM), pl.BlockSpec(memory_space=pltpu.HBM)
    cached = state.shape[0]
    return pl.pallas_call(
        store_kernel,
        in_specs=[hbm] * 6,
        out_specs=[hbm, vmem],
        out_shape=[
            jax.ShapeDtypeStruct(state.shape, jnp.bfloat16),
            jax.ShapeDtypeStruct(window.shape, jnp.bfloat16),
        ],
        scratch_shapes=[
            pltpu.VMEM(a_rows.shape, a_rows.dtype),
            pltpu.VMEM(columns.shape, columns.dtype),
            pltpu.VMEM(b_save.shape, b_save.dtype),
            pltpu.VMEM(win_out.shape, win_out.dtype),
            pltpu.VMEM((EVENTS * HEAD_DIM, EVENTS * HEAD_DIM), jnp.bfloat16),
            pltpu.VMEM(state.shape, jnp.bfloat16),
            pltpu.VMEM((HEAD_DIM // GROUP, cached * HEADS, LANES), jnp.bfloat16),
            pltpu.SemaphoreType.DMA((5,)),
            pltpu.SemaphoreType.DMA((cached,)),
            pltpu.SemaphoreType.DMA((cached,)),
        ],
        compiler_params=pltpu.CompilerParams(vmem_limit_bytes=60 * 2**20),
        cost_estimate=pl.CostEstimate(flops=3 * 10**9, bytes_accessed=10**7, transcendentals=0),
        name="store",
    )(state, a_rows, columns, b_save, win_out, order_matrix())


def on_device(
    tokens,
    in_weight,
    dt_weight,
    conv_weight,
    conv_bias,
    dt_bias,
    decay_rate,
    skip_gain,
    norm_gain,
    state_cache,
    conv_cache,
    hash_owner,
    cache_slot,
    event_counts,
):
    users = tokens.shape[1]
    if in_weight.shape[0] % LANES == 0:
        dt_weight = dt_weight.T
    vectors = (conv_weight, conv_bias, dt_bias, decay_rate, skip_gain, norm_gain)
    window = conv_cache.transpose(1, 0, 2)
    out, a_rows, columns, b_save, win_out = serve(
        tokens.reshape(STEPS * users * EV, -1),
        in_weight,
        dt_weight,
        vectors,
        state_cache,
        window,
        hash_owner[None],
        cache_slot[None],
        event_counts,
    )
    new_state, new_window = store(state_cache, a_rows, columns, b_save, win_out, window)
    return (out, new_state, new_window.transpose(1, 0, 2))


def solution(mesh):
    split = ("groups", "req", "fsdp")
    in_specs = (
        P(None, split, None, None),
        P(("req", "fsdp"), None),
        P(("req", "fsdp"), None),
        P(),
        P(),
        P(),
        P(),
        P(),
        P(),
        P(split, None, None),
        P(split, None, None),
        P(split),
        P(split),
        P(None, split),
    )
    out_specs = (P(None, split, None), P(split, None, None), P(split, None, None))
    return jax.shard_map(
        on_device, mesh=mesh, in_specs=in_specs, out_specs=out_specs, check_vma=False
    )
```

```python
import functools

import jax
import jax.numpy as jnp
import numpy as np
from jax import lax
from jax.experimental import pallas as pl
from jax.experimental.pallas import tpu as pltpu
from jax.sharding import PartitionSpec as P

HEADS = 64
HEAD_DIM = 64
STATE = 64
STEPS = 2
EV = 8
EVENTS = STEPS * EV
INNER = HEADS * HEAD_DIM
LANES = 128
GROUP = 8
SLOTS_PER_PAIR = 2


def order_matrix():
    out = np.zeros((EVENTS * HEAD_DIM, EVENTS * HEAD_DIM), np.float32)
    t, p = np.meshgrid(np.arange(EVENTS), np.arange(HEAD_DIM), indexing="ij")
    out[t * HEAD_DIM + p, p * EVENTS + t] = 1.0
    return jnp.asarray(out, jnp.bfloat16)


MESH = pl.DeviceIdType.MESH
TILE = 256
TAPS = 4
BLOCK = 16
FIRST = 16 - EV - (TAPS - 1)
COMBINE_LAG = 2
ROUTE_LAG = 4
LIFT_LAG = 6
AHEAD = 3
CHUNKS = ((INNER, 1),) + tuple((512 * i, 2) for i in range(8))


def serve_kernel(
    n_req,
    n_fsdp,
    x_hbm,
    w_hbm,
    dt_hbm,
    cw_hbm,
    cb_hbm,
    dt_bias_hbm,
    decay_hbm,
    skip_hbm,
    gain_hbm,
    state_hbm,
    window_hbm,
    owner_hbm,
    slot_hbm,
    count_hbm,
    order_hbm,
    out_ref,
    sorted_hbm,
    columns_hbm,
    b_hbm,
    new_window_ref,
    x_ref,
    dt_ref,
    cw_ref,
    cb_ref,
    dt_bias_ref,
    decay_ref,
    skip_ref,
    gain_ref,
    window_ref,
    owner_ref,
    slot_ref,
    count_ref,
    order_ref,
    state_buf,
    strips,
    x_all,
    w_all,
    own_sum,
    part_out,
    part_in,
    sum_out,
    sum_in,
    pack,
    packed,
    items,
    meta,
    meta_in,
    placing,
    live,
    by_slot,
    win_in,
    win_out,
    ext,
    stacked,
    table,
    columns,
    gains,
    a_rows,
    a_sorted,
    b_save,
    y_read,
    y_part,
    y_out,
    y_back,
    y_rows,
    flat,
    fetch_sems,
    load_sems,
    state_sem,
    out_sems,
    x_send,
    x_recv,
    w_send,
    w_recv,
    f_send,
    f_recv,
    p_send,
    p_recv,
    s_send,
    s_recv,
    i_send,
    i_recv,
    m_send,
    m_recv,
    y_send,
    y_recv,
):
    f32, bf16, i32 = jnp.float32, jnp.bfloat16, jnp.int32
    rows = x_ref.shape[0]
    users = rows // EVENTS
    depth, channels = w_hbm.shape
    cached = state_buf.shape[0]
    chips = n_req // 2
    pairs = n_fsdp // 2
    n_items = items.shape[0]
    me_r, me_z = lax.axis_index("req"), lax.axis_index("fsdp")
    me_chip, core = me_r // 2, me_r % 2
    me_pair, side = me_z // 2, me_z % 2
    sibling = {"req": me_chip * 2 + 1 - core}

    def at_req(shift):
        return lax.rem(me_r + shift + n_req, n_req)

    def at_chip(shift):
        return lax.rem(me_chip + shift + chips, chips) * 2 + core

    def at_fsdp(pair, other):
        return lax.rem(me_pair + pair + pairs, pairs) * 2 + (1 - side if other else side)

    chunks = range(len(CHUNKS))
    fsdp_shifts = [(d, o) for d in range(pairs) for o in (0, 1)][1:]

    def remote(src, dst, send, recv, device):
        return pltpu.make_async_remote_copy(
            src_ref=src,
            dst_ref=dst,
            send_sem=send,
            recv_sem=recv,
            device_id=device,
            device_id_type=MESH,
        )

    def x_copy(d, o):
        i = d * 2 + o
        target = at_fsdp(d, o)
        return remote(strips.at[target], x_all.at[i], x_send.at[i], x_recv.at[i], {"fsdp": target})

    def m_copy(d):
        target = at_req(d)
        return remote(
            meta.at[target], meta_in.at[me_r], m_send.at[d], m_recv.at[d], {"req": target}
        )

    def y_copy(d):
        target = at_req(d)
        return remote(
            y_out.at[target], y_back.at[me_r], y_send.at[d], y_recv.at[d], {"req": target}
        )

    def cols(c):
        return pl.ds(CHUNKS[c][0], CHUNKS[c][1] * TILE)

    def w_copy(c, d):
        piece = w_all.at[me_r, :, cols(c)]
        return remote(piece, piece, w_send.at[c, d], w_recv.at[c, d], {"req": at_chip(d)})

    def w_forward(c, d):
        piece = w_all.at[at_chip(-d), :, cols(c)]
        return remote(piece, piece, f_send.at[c, d], f_recv.at[c, d], sibling)

    def p_copy(c, d):
        return remote(
            part_out.at[d, :, cols(c)],
            part_in.at[d, :, cols(c)],
            p_send.at[c, d],
            p_recv.at[c, d],
            {"fsdp": at_fsdp(0, 1)},
        )

    def s_copy(c, d):
        return remote(
            sum_out.at[d, :, cols(c)],
            sum_in.at[d, :, cols(c)],
            s_send.at[c, d],
            s_recv.at[c, d],
            {"fsdp": at_fsdp(-d, 0)},
        )

    def i_copy(c, d):
        target = at_req(d)
        return remote(
            packed.at[pl.ds(target * SLOTS_PER_PAIR, SLOTS_PER_PAIR), :, cols(c)],
            items.at[pl.ds(me_r * SLOTS_PER_PAIR, SLOTS_PER_PAIR), :, cols(c)],
            i_send.at[c, d],
            i_recv.at[c, d],
            {"req": target},
        )

    def load(c):
        width = min(CHUNKS[c][1] * TILE, channels - CHUNKS[c][0])
        at = pl.ds(CHUNKS[c][0], width)
        return pltpu.make_async_copy(w_hbm.at[:, at], w_all.at[me_r, :, at], load_sems.at[c])

    early = [
        pltpu.make_async_copy(a, b, fetch_sems.at[i])
        for i, (a, b) in enumerate(
            [
                (x_hbm, x_ref),
                (dt_hbm, dt_ref),
                (owner_hbm, owner_ref),
                (slot_hbm, slot_ref),
                (count_hbm, count_ref),
            ]
        )
    ]
    late = [
        pltpu.make_async_copy(a, b, fetch_sems.at[5 + i])
        for i, (a, b) in enumerate(
            [
                (cw_hbm, cw_ref),
                (cb_hbm, cb_ref),
                (dt_bias_hbm, dt_bias_ref),
                (decay_hbm, decay_ref),
                (skip_hbm, skip_ref),
                (gain_hbm, gain_ref),
                (window_hbm, window_ref),
            ]
        )
    ]
    fetch_state = pltpu.make_async_copy(state_hbm, state_buf, state_sem)
    fetch_order = pltpu.make_async_copy(order_hbm, order_ref, fetch_sems.at[5 + len(late)])
    keep_columns = pltpu.make_async_copy(columns, columns_hbm, out_sems.at[0])
    keep_writes = pltpu.make_async_copy(b_save, b_hbm, out_sems.at[1])

    def keep_block(block):
        return pltpu.make_async_copy(
            a_sorted.at[block], sorted_hbm.at[block], out_sems.at[2 + block]
        )

    barrier = pltpu.get_barrier_semaphore()
    partners = [{"req": at_req(d)} for d in range(1, n_req)]
    partners += [{"fsdp": at_fsdp(d, o)} for d, o in fsdp_shifts]
    for partner in partners:
        pl.semaphore_signal(barrier, inc=1, device_id=partner, device_id_type=MESH)
    early[0].start()
    load(0).start()
    for copy in early[1:]:
        copy.start()
    for c in chunks[1:]:
        load(c).start()
    for copy in early:
        copy.wait()
    for z in range(n_fsdp):
        for r in range(n_req):
            at = (r * n_fsdp + z) * depth
            strips[z, :, r * depth : (r + 1) * depth] = x_ref[:, at : at + depth]
    x_all[0] = strips[me_z]
    if dt_ref.shape[0] == depth:
        step_columns = jnp.concatenate(
            [dt_ref[...], jnp.zeros((depth, LANES - HEADS), bf16)], axis=1
        )
    else:
        step_columns = jnp.concatenate(
            [dt_ref[...].astype(f32), jnp.zeros((LANES - HEADS, depth), f32)], axis=0
        ).T.astype(bf16)
    w_all[me_r, :, channels:] = step_columns
    pl.semaphore_wait(barrier, len(partners))
    for d, o in fsdp_shifts:
        x_copy(d, o).start()

    def spread(c):
        load(c).wait()
        for d in range(1, chips):
            w_copy(c, d).start()
        w_forward(c, 0).start()

    for c in chunks[:AHEAD]:
        spread(c)
    for copy in late:
        copy.start()
    fetch_state.start()
    fetch_order.start()

    owner = [owner_ref[0:1, u : u + 1] for u in range(users)]
    rank = ranks(owner)
    high, wide = pack.shape
    row = lax.broadcasted_iota(i32, (high, wide), 0)
    col = lax.broadcasted_iota(i32, (high, wide), 1)
    user = (col // EV) % users
    hit = jnp.zeros((high, wide), jnp.bool_)
    pair_row = row // EVENTS
    for u in range(users):
        hit = hit | ((pair_row == owner[u] * SLOTS_PER_PAIR + rank[u]) & (user == u))
    same = (row % EV == col % EV) & ((row // EV) % STEPS == col // (EV * users))
    pack[...] = jnp.where(hit & same, 1.0, 0.0).astype(bf16)
    row = lax.broadcasted_iota(i32, (n_req * 8, LANES), 0)
    lane = lax.broadcasted_iota(i32, (n_req * 8, LANES), 1)
    notes = jnp.zeros((n_req * 8, LANES), i32)
    for u in range(users):
        note = jnp.where(lane == 0, slot_ref[0:1, u : u + 1] + 1, 0)
        for s in range(STEPS):
            note = jnp.where(lane == 1 + s, count_ref[s : s + 1, u : u + 1], note)
        notes = jnp.where(row == owner[u] * 8 + rank[u], note, notes)
    meta[...] = notes.reshape(meta.shape)
    for d in range(1, n_req):
        m_copy(d).start()
    meta_in[me_r] = meta[me_r]

    left = lax.broadcasted_iota(i32, (1, LANES), 1) < HEAD_DIM
    lane64 = lax.broadcasted_iota(i32, (1, LANES), 1) % HEAD_DIM
    row8 = lax.broadcasted_iota(i32, (EV, 1), 0)
    row16 = lax.broadcasted_iota(i32, (16, 1), 0)

    def both_halves(v):
        turned = pltpu.roll(v, HEAD_DIM, 1)
        return jnp.where(left, v, turned), jnp.where(left, turned, v)

    def prepare():
        for copy in late:
            copy.wait()
        win_in[...] = jnp.zeros(win_in.shape, f32)
        ext[...] = jnp.zeros(ext.shape, f32)
        for i in range(TAPS - 1):
            old = window_ref[i].astype(f32)
            for u in range(cached):
                win_in[u, FIRST + i : FIRST + i + 1, :] = old[u : u + 1]
        table[...] = jnp.zeros(table.shape, f32)
        y_part[...] = jnp.zeros(y_part.shape, f32)
        gain = gain_ref[...].reshape(1, INNER)
        for j in range(INNER // LANES):
            first, second = both_halves(gain[:, j * LANES : (j + 1) * LANES])
            gains[2 * j : 2 * j + 1, :] = first
            gains[2 * j + 1 : 2 * j + 2, :] = second

    def find_rows():
        for d in range(1, n_req):
            m_copy(d).wait_recv()
        slots = lax.broadcasted_iota(i32, (cached, 1), 0)
        counts = jnp.zeros((cached, LANES), i32)
        item = lax.broadcasted_iota(i32, (1, n_items * EVENTS), 1) // EVENTS
        goal = jnp.zeros((1, n_items * EVENTS), i32) - 1
        for i in range(n_items):
            note = meta_in[i // SLOTS_PER_PAIR, i % SLOTS_PER_PAIR : i % SLOTS_PER_PAIR + 1, :]
            slot = note[:, 0:1] - 1
            counts = jnp.where(slots == slot, note, counts)
            goal = jnp.where(item == i, slot, goal)
        live[...] = counts
        shape = (cached * EVENTS, n_items * EVENTS)
        row = lax.broadcasted_iota(i32, shape, 0)
        col = lax.broadcasted_iota(i32, shape, 1)
        match = (row // EVENTS == goal) & (row % EVENTS == col % EVENTS)
        placing[...] = jnp.where(match, 1.0, 0.0).astype(bf16)

    def forward(c):
        for d in range(1, chips):
            w_copy(c, d).wait_recv()
            w_forward(c, d).start()

    def tiles(c, body):
        def step(i, carry):
            body(pl.ds(pl.multiple_of(CHUNKS[c][0] + i * TILE, TILE), TILE))
            return carry

        lax.fori_loop(0, CHUNKS[c][1], step, 0)

    def multiply(c):
        for d in range(chips):
            w_forward(c, d).wait_recv()

        def tile(at):
            part = jnp.dot(
                x_all[...].reshape(n_fsdp * rows, n_req * depth),
                w_all[:, :, at].reshape(n_req * depth, TILE),
                preferred_element_type=f32,
            )
            for d in range(pairs):
                own_sum[d, :, at] = part[2 * d * rows : (2 * d + 1) * rows]
                part_out[d, :, at] = part[(2 * d + 1) * rows : (2 * d + 2) * rows].astype(bf16)

        tiles(c, tile)
        for d in (*range(1, pairs), 0):
            p_copy(c, d).start()

    def combine(c):
        for d in range(1, pairs):
            p_copy(c, d).wait_recv()

        def tile(at):
            for d in range(1, pairs):
                sum_out[d, :, at] = (own_sum[d, :, at] + part_in[d, :, at].astype(f32)).astype(bf16)

        tiles(c, tile)
        for d in range(1, pairs):
            s_copy(c, d).start()

    def route(c):
        p_copy(c, 0).wait_recv()
        for d in range(1, pairs):
            s_copy(c, d).wait_recv()

        def tile(at):
            total = own_sum[0, :, at] + part_in[0, :, at].astype(f32)
            for d in range(1, pairs):
                total = total + sum_in[d, :, at].astype(f32)
            chosen = jnp.dot(pack[...], total.astype(bf16), preferred_element_type=f32)
            packed[:, :, at] = chosen.reshape(-1, EVENTS, TILE).astype(bf16)
            for i in range(SLOTS_PER_PAIR):
                mine = me_r * SLOTS_PER_PAIR + i
                items[mine, :, at] = packed[mine, :, at]

        tiles(c, tile)
        for d in range(1, n_req):
            i_copy(c, d).start()

    def arrive(c):
        for d in range(1, n_req):
            i_copy(c, d).wait_recv()

        def tile(at):
            by_slot[:, at] = jnp.dot(
                placing[...],
                items[:, :, at].reshape(n_items * EVENTS, TILE),
                preferred_element_type=f32,
            ).astype(bf16)

        tiles(c, tile)

    def counts_of(u):
        note = live[pl.ds(u, 1), :]
        return [note[:, 1 + s : 2 + s] for s in range(STEPS)]

    def convolve(u, start, width):
        at = slice(start, start + width)
        counts = counts_of(u)
        mine = by_slot[pl.ds(pl.multiple_of(u * EVENTS, EVENTS), EVENTS), at].astype(f32)
        ext[0, 0:EV, :width] = win_in[u, :, at]
        bias = cb_ref[...].reshape(1, channels)[:, at]
        actives = []
        for s in range(STEPS):
            ext[s, EV : 2 * EV, :width] = mine[s * EV : (s + 1) * EV]
            conv = bias + cw_ref[0:1, at] * ext[s, FIRST : FIRST + EV, :width]
            for tap in range(1, TAPS):
                begin = FIRST + tap
                conv = conv + cw_ref[tap : tap + 1, at] * ext[s, begin : begin + EV, :width]
            actives.append(conv * (1.0 / (1.0 + jnp.exp(-conv))))
            whole = ext[s, :, :width]
            for i in range(TAPS - 1):
                wanted = (row16 == counts[s] + FIRST + i) & (row16 >= FIRST)
                kept = jnp.sum(jnp.where(wanted, whole, 0.0), axis=0, keepdims=True)
                if s + 1 < STEPS:
                    ext[s + 1, FIRST + i : FIRST + i + 1, :width] = kept
                else:
                    win_out[u, i : i + 1, at] = kept
        return actives

    def weigh(u, carry):
        counts = counts_of(u)
        actives = convolve(u, INNER, 2 * STATE)
        at = pl.ds(pl.multiple_of(u * EVENTS, EVENTS), EVENTS)
        raws = by_slot[at, channels : channels + LANES].astype(f32)[:, :HEADS]
        dt_bias = dt_bias_ref[...].reshape(1, HEADS)
        decay = decay_ref[...].reshape(1, HEADS)
        skip = skip_ref[...].reshape(1, HEADS)
        weights, totals, reads, writes, picks = [], [], [], [], []
        for s in range(STEPS):
            raw = raws[s * EV : (s + 1) * EV] + dt_bias
            size = jnp.maximum(raw, 0.0) + jnp.log1p(jnp.exp(-jnp.abs(raw)))
            size = jnp.where(row8 < counts[s], size, 0.0)
            cum = -decay * size
            for shift in (1, 2, 4):
                cum = cum + jnp.where(row8 >= shift, pltpu.roll(cum, shift, 0), 0.0)
            total = cum[EV - 1 : EV, :]
            totals.append(total)
            weights.append(jnp.exp(total - cum) * size)
            picks.append((row8 == counts[s] - 1).astype(f32))
            writes.append(actives[s][:, :STATE])
            reads.append(jnp.sum(picks[s] * actives[s][:, STATE:], axis=0, keepdims=True))
        carried = weights[0] * jnp.exp(totals[1])

        def gram(s, e):
            return jnp.sum(writes[e] * reads[s], axis=1, keepdims=True)

        table[0:8, 0:64] = weights[0] * gram(0, 0) + picks[0] * skip
        table[8:16, 0:64] = carried * gram(1, 0)
        table[16:24, 0:64] = weights[1] * gram(1, 1) + picks[1] * skip
        table[24:32, 0:64] = carried
        table[32:40, 0:64] = weights[1]
        table[40:41, 0:64] = jnp.exp(totals[0])
        table[41:42, 0:64] = jnp.exp(totals[0] + totals[1])
        table[42:43, 0:64] = reads[0]
        table[43:44, 0:64] = reads[1]
        columns[u] = table[...].T[0:64]
        for s in range(STEPS):
            b_save[u, s * EV : (s + 1) * EV, :] = jnp.concatenate([writes[s], writes[s]], axis=1)
        return carry

    wide = GROUP * STATE

    def read_old(u, carry):
        read = jnp.where(left, columns[u, :, 42:43], columns[u, :, 43:44])
        total = jnp.zeros((HEADS, LANES), f32)
        for q in range(HEAD_DIM // GROUP):
            read_block = jnp.concatenate(
                [jnp.where(lane64 == q * GROUP + i, read, 0.0) for i in range(GROUP)], axis=0
            ).astype(bf16)
            old = state_buf[u, :, q * wide : (q + 1) * wide]
            total = total + jnp.dot(old, read_block, preferred_element_type=f32)
        y_read[u] = jnp.where(left, columns[u, :, 40:41], columns[u, :, 41:42]) * total
        return carry

    def lift(block):
        heads = slice(block * BLOCK, (block + 1) * BLOCK)
        width = BLOCK * HEAD_DIM

        def one(u, carry):
            actives = convolve(u, block * width, width)
            for s in range(STEPS):
                for j in range(width // LANES):
                    first, second = both_halves(actives[s][:, j * LANES : (j + 1) * LANES])
                    at = 2 * j * EVENTS + s * EV
                    stacked[at : at + EV, :] = first
                    stacked[at + EVENTS : at + EVENTS + EV, :] = second
            mine = columns[u, heads, :]
            part = jnp.zeros((BLOCK, LANES), f32)
            for t in range(0, EVENTS, 2):
                pieces = []
                for e in (t, t + 1):
                    z = stacked[pl.ds(e, BLOCK, stride=EVENTS), :]
                    second = mine[:, 8 + e : 9 + e]
                    if e < EV:
                        coef = jnp.where(left, mine[:, e : e + 1], second)
                    else:
                        coef = jnp.where(left, 0.0, second)
                    part = part + coef * z
                    pieces.append(mine[:, 24 + e : 25 + e] * z)
                at = pl.multiple_of(u * BLOCK, BLOCK)
                a_rows[pl.ds(at, BLOCK), t * HEAD_DIM : (t + 2) * HEAD_DIM] = jnp.where(left, pieces[0], pieces[1]).astype(bf16)
            y_part[u, heads, :] = part
            return carry

        lax.fori_loop(0, cached, one, 0)

    def arrange(block):
        def step(q, carry):
            at = pl.ds(pl.multiple_of(q * LANES, LANES), LANES)
            a_sorted[block, q] = jnp.dot(
                a_rows[...], order_ref[:, at], preferred_element_type=f32
            ).astype(bf16)
            return carry

        lax.fori_loop(0, HEAD_DIM // GROUP, step, 0)
        keep_block(block).start()

    last = len(CHUNKS)
    blocks = HEADS // BLOCK
    ready = {}
    for c in chunks[1:]:
        done = CHUNKS[c][0] + CHUNKS[c][1] * TILE
        if done % (BLOCK * HEAD_DIM) == 0:
            ready[c] = done // (BLOCK * HEAD_DIM) - 1
    forward(0)
    prepare()
    for c in range(last + LIFT_LAG):
        if c + AHEAD < last:
            spread(c + AHEAD)
        if c + 1 < last:
            forward(c + 1)
        if c == 0:
            for d, o in fsdp_shifts:
                x_copy(d, o).wait_recv()
        if c < last:
            multiply(c)
        if 0 <= c - COMBINE_LAG < last:
            combine(c - COMBINE_LAG)
        if c == 2:
            find_rows()
        if 0 <= c - ROUTE_LAG < last:
            route(c - ROUTE_LAG)
        done = c - LIFT_LAG
        if 0 <= done < last:
            arrive(done)
        if done == 0:
            lax.fori_loop(0, cached, weigh, 0)
            keep_columns.start()
            keep_writes.start()
            fetch_state.wait()
            fetch_order.wait()
        if done == 1:
            lax.fori_loop(0, cached // 2, read_old, 0)
        if done == 3:
            lax.fori_loop(cached // 2, cached, read_old, 0)
        if done in ready:
            lift(ready[done])
            if ready[done] + 1 < blocks:
                arrange(ready[done])

    y_rows[...] = jnp.zeros(y_rows.shape, f32)

    def norm(u, carry):
        y = y_read[u] + y_part[u]
        square = jnp.sum(y * y, axis=0, keepdims=True)
        first = jnp.sum(jnp.where(left, square, 0.0), axis=1, keepdims=True)
        second = jnp.sum(jnp.where(left, 0.0, square), axis=1, keepdims=True)
        inverse = lax.rsqrt(jnp.where(left, first, second) * (1.0 / INNER) + 1e-05)
        y = y * inverse * gains[...]
        for i in range(n_items):
            p, k = i // SLOTS_PER_PAIR, i % SLOTS_PER_PAIR
            y_rows[i] = jnp.where(meta_in[p, k : k + 1, 0:1] == u + 1, y, y_rows[i])
        return carry

    lax.fori_loop(0, cached, norm, 0)
    y_out[...] = y_rows[...].astype(bf16).reshape(y_out.shape)
    for d in range(1, n_req):
        y_copy(d).start()
    y_back[me_r] = y_out[me_r]
    arrange(blocks - 1)
    for i in range(TAPS - 1):
        kept = [win_out[u, i : i + 1, :] for u in range(cached)]
        new_window_ref[i] = jnp.concatenate(kept, axis=0).astype(bf16)
    for d in range(1, n_req):
        m_copy(d).wait_send()
        for c in chunks:
            i_copy(c, d).wait_send()
    for d, o in fsdp_shifts:
        x_copy(d, o).wait_send()
    for c in chunks:
        for d in range(pairs):
            p_copy(c, d).wait_send()
        for d in range(1, pairs):
            s_copy(c, d).wait_send()
        w_forward(c, 0).wait_send()
        for d in range(1, chips):
            w_copy(c, d).wait_send()
            w_forward(c, d).wait_send()
    for d in range(1, n_req):
        y_copy(d).wait()
    for u in range(users):
        mine = jnp.zeros((HEADS, LANES), f32)
        for i in range(n_items):
            p, k = i // SLOTS_PER_PAIR, i % SLOTS_PER_PAIR
            hit = (owner[u] == p) & (rank[u] == k)
            mine = jnp.where(hit, y_back[p, k].astype(f32), mine)
        y_rows[u] = mine
        even = y_rows[u, pl.ds(0, HEADS // 2, stride=2), :]
        odd = y_rows[u, pl.ds(1, HEADS // 2, stride=2), :]
        steps = [
            jnp.where(left, even, pltpu.roll(odd, HEAD_DIM, 1)),
            jnp.where(left, pltpu.roll(even, HEAD_DIM, 1), odd),
        ]
        for s in range(STEPS):
            for j in range(INNER // LANES):
                flat[s, u : u + 1, j * LANES : (j + 1) * LANES] = steps[s][j : j + 1]
    out_ref[...] = flat[...].astype(bf16)
    keep_columns.wait()
    keep_writes.wait()
    for block in range(blocks):
        keep_block(block).wait()


def ranks(owner):
    out = []
    for u in range(len(owner)):
        rank = jnp.zeros((1, 1), jnp.int32)
        for earlier in owner[:u]:
            rank = rank + (earlier == owner[u]).astype(jnp.int32)
        out.append(rank)
    return out


def serve(x, in_weight, dt_weight, vectors, state, window, owner, slot, counts):
    n_req, n_fsdp = lax.axis_size("req"), lax.axis_size("fsdp")
    rows = x.shape[0]
    users = rows // EVENTS
    depth, channels = in_weight.shape
    cached = state.shape[0]
    width = max(start + tiles * TILE for start, tiles in CHUNKS)
    n_items = n_req * SLOTS_PER_PAIR
    pairs = n_fsdp // 2
    f32, bf16, i32 = jnp.float32, jnp.bfloat16, jnp.int32
    vmem, hbm = pl.BlockSpec(memory_space=pltpu.VMEM), pl.BlockSpec(memory_space=pltpu.HBM)
    dma = pltpu.SemaphoreType.DMA
    n = len(CHUNKS)
    order = order_matrix()
    arrays = (x, in_weight, dt_weight, *vectors, state, window, owner, slot, counts, order)
    sorted_shape = (HEADS // BLOCK, HEAD_DIM // GROUP, cached * BLOCK, LANES)
    fetched = (x, dt_weight, *vectors, window, owner, slot, counts, order)
    return pl.pallas_call(
        functools.partial(serve_kernel, n_req, n_fsdp),
        in_specs=[hbm] * len(arrays),
        out_specs=[vmem, hbm, hbm, hbm, vmem],
        out_shape=[
            jax.ShapeDtypeStruct((STEPS, users, INNER), bf16),
            jax.ShapeDtypeStruct(sorted_shape, bf16),
            jax.ShapeDtypeStruct((cached, HEADS, LANES), f32),
            jax.ShapeDtypeStruct((cached, EVENTS, LANES), f32),
            jax.ShapeDtypeStruct(window.shape, bf16),
        ],
        scratch_shapes=[pltpu.VMEM(a.shape, a.dtype) for a in fetched]
        + [
            pltpu.VMEM(state.shape, bf16),
            pltpu.VMEM((n_fsdp, rows, n_req * depth), bf16),
            pltpu.VMEM((n_fsdp, rows, n_req * depth), bf16),
            pltpu.VMEM((n_req, depth, width), bf16),
            pltpu.VMEM((pairs, rows, width), f32),
            pltpu.VMEM((pairs, rows, width), bf16),
            pltpu.VMEM((pairs, rows, width), bf16),
            pltpu.VMEM((pairs, rows, width), bf16),
            pltpu.VMEM((pairs, rows, width), bf16),
            pltpu.VMEM((n_items * EVENTS, rows), bf16),
            pltpu.VMEM((n_items, EVENTS, width), bf16),
            pltpu.VMEM((n_items, EVENTS, width), bf16),
            pltpu.VMEM((n_req, 8, LANES), i32),
            pltpu.VMEM((n_req, 8, LANES), i32),
            pltpu.VMEM((cached * EVENTS, n_items * EVENTS), bf16),
            pltpu.VMEM((cached, LANES), i32),
            pltpu.VMEM((cached * EVENTS, width), bf16),
            pltpu.VMEM((cached, EV, channels), f32),
            pltpu.VMEM((cached, EV, channels), f32),
            pltpu.VMEM((STEPS, 2 * EV, BLOCK * HEAD_DIM), f32),
            pltpu.VMEM((BLOCK * EVENTS, LANES), f32),
            pltpu.VMEM((LANES, LANES), f32),
            pltpu.VMEM((cached, HEADS, LANES), f32),
            pltpu.VMEM((HEADS, LANES), f32),
            pltpu.VMEM((cached * BLOCK, EVENTS * HEAD_DIM), bf16),
            pltpu.VMEM(sorted_shape, bf16),
            pltpu.VMEM((cached, EVENTS, LANES), f32),
            pltpu.VMEM((cached, HEADS, LANES), f32),
            pltpu.VMEM((cached, HEADS, LANES), f32),
            pltpu.VMEM((n_req, SLOTS_PER_PAIR, HEADS, LANES), bf16),
            pltpu.VMEM((n_req, SLOTS_PER_PAIR, HEADS, LANES), bf16),
            pltpu.VMEM((n_items, HEADS, LANES), f32),
            pltpu.VMEM((STEPS, users, INNER), f32),
            dma((len(fetched),)),
            dma((n,)),
            dma(()),
            dma((2 + HEADS // BLOCK,)),
            dma((n_fsdp,)),
            dma((n_fsdp,)),
            dma((n, n_req // 2)),
            dma((n, n_req // 2)),
            dma((n, n_req // 2)),
            dma((n, n_req // 2)),
            dma((n, pairs)),
            dma((n, pairs)),
            dma((n, pairs)),
            dma((n, pairs)),
            dma((n, n_req)),
            dma((n, n_req)),
            dma((n_req,)),
            dma((n_req,)),
            dma((n_req,)),
            dma((n_req,)),
        ],
        compiler_params=pltpu.CompilerParams(
            collective_id=0, has_side_effects=True, vmem_limit_bytes=60 * 2**20
        ),
        cost_estimate=pl.CostEstimate(flops=7 * 10**9, bytes_accessed=10**7, transcendentals=0),
        name="serve",
    )(*arrays)


def store_kernel(
    state_hbm,
    sorted_hbm,
    columns_hbm,
    b_hbm,
    window_hbm,
    out_hbm,
    new_state_hbm,
    new_window_hbm,
    final_hbm,
    a_sorted,
    columns,
    writes,
    window_buf,
    out_buf,
    state_buf,
    fetch_sems,
    pass_sems,
    in_sems,
    out_sems,
):
    f32, bf16 = jnp.float32, jnp.bfloat16
    cached = state_buf.shape[0]
    groups = HEAD_DIM // GROUP
    wide = GROUP * STATE

    def state_in(u):
        return pltpu.make_async_copy(state_hbm.at[u], state_buf.at[u], in_sems.at[u])

    def state_out(u):
        return pltpu.make_async_copy(state_buf.at[u], new_state_hbm.at[u], out_sems.at[u])

    pairs = [
        (b_hbm, writes),
        (columns_hbm, columns),
        (sorted_hbm, a_sorted),
        (window_hbm, window_buf),
        (out_hbm, out_buf),
    ]
    passed = [(window_buf, new_window_hbm), (out_buf, final_hbm)]
    passes = [pltpu.make_async_copy(a, b, pass_sems.at[i]) for i, (a, b) in enumerate(passed)]
    copies = [pltpu.make_async_copy(a, b, fetch_sems.at[i]) for i, (a, b) in enumerate(pairs)]
    for copy in copies:
        copy.start()
    for u in range(cached):
        state_in(u).start()
    shape = (GROUP * EVENTS, wide)
    diagonal = lax.broadcasted_iota(jnp.int32, shape, 0) // EVENTS == (
        lax.broadcasted_iota(jnp.int32, shape, 1) // STATE
    )
    for copy in copies[:3]:
        copy.wait()
    for copy, onward in zip(copies[3:], passes):
        copy.wait()
        onward.start()

    def update(u, carry):
        b_wide = jnp.concatenate([writes[u]] * (wide // LANES), axis=1)
        b_block = jnp.where(diagonal, jnp.concatenate([b_wide] * GROUP, axis=0), 0.0)
        lhs = a_sorted[:, :, pl.ds(pl.multiple_of(u * BLOCK, BLOCK), BLOCK), :]
        change = jnp.dot(
            lhs.reshape(groups * HEADS, LANES), b_block.astype(bf16), preferred_element_type=f32
        )
        state_in(u).wait()
        for block in range(HEADS // BLOCK):
            heads = slice(block * BLOCK, (block + 1) * BLOCK)
            decay = columns[u, heads, 41:42]
            for q in range(groups):
                at = slice(q * wide, (q + 1) * wide)
                row = (block * groups + q) * BLOCK
                old = state_buf[u, heads, at].astype(f32)
                state_buf[u, heads, at] = (decay * old + change[row : row + BLOCK]).astype(bf16)
        state_out(u).start()
        return carry

    lax.fori_loop(0, cached, update, 0, unroll=2)
    for onward in passes:
        onward.wait()
    for u in range(cached):
        state_out(u).wait()


def store(state, a_sorted, columns, b_save, window, out):
    hbm = pl.BlockSpec(memory_space=pltpu.HBM)
    cached = state.shape[0]
    return pl.pallas_call(
        store_kernel,
        in_specs=[hbm] * 6,
        out_specs=[hbm] * 3,
        out_shape=[jax.ShapeDtypeStruct(a.shape, a.dtype) for a in (state, window, out)],
        scratch_shapes=[
            pltpu.VMEM(a_sorted.shape, a_sorted.dtype),
            pltpu.VMEM(columns.shape, columns.dtype),
            pltpu.VMEM(b_save.shape, b_save.dtype),
            pltpu.VMEM(window.shape, window.dtype),
            pltpu.VMEM(out.shape, out.dtype),
            pltpu.VMEM(state.shape, jnp.bfloat16),
            pltpu.SemaphoreType.DMA((5,)),
            pltpu.SemaphoreType.DMA((2,)),
            pltpu.SemaphoreType.DMA((cached,)),
            pltpu.SemaphoreType.DMA((cached,)),
        ],
        compiler_params=pltpu.CompilerParams(vmem_limit_bytes=60 * 2**20),
        cost_estimate=pl.CostEstimate(flops=10**9, bytes_accessed=10**7, transcendentals=0),
        name="store",
    )(state, a_sorted, columns, b_save, window, out)


def on_device(
    tokens,
    in_weight,
    dt_weight,
    conv_weight,
    conv_bias,
    dt_bias,
    decay_rate,
    skip_gain,
    norm_gain,
    state_cache,
    conv_cache,
    hash_owner,
    cache_slot,
    event_counts,
):
    users = tokens.shape[1]
    if in_weight.shape[0] % LANES == 0:
        dt_weight = dt_weight.T
    vectors = (conv_weight, conv_bias, dt_bias, decay_rate, skip_gain, norm_gain)
    window = conv_cache.transpose(1, 0, 2)
    out, a_sorted, columns, b_save, new_window = serve(
        tokens.reshape(STEPS * users * EV, -1),
        in_weight,
        dt_weight,
        vectors,
        state_cache,
        window,
        hash_owner[None],
        cache_slot[None],
        event_counts,
    )
    new_state, new_window, out = store(state_cache, a_sorted, columns, b_save, new_window, out)
    return (out, new_state, new_window.transpose(1, 0, 2))


def solution(mesh):
    split = ("groups", "req", "fsdp")
    in_specs = (
        P(None, split, None, None),
        P(("req", "fsdp"), None),
        P(("req", "fsdp"), None),
        P(),
        P(),
        P(),
        P(),
        P(),
        P(),
        P(split, None, None),
        P(split, None, None),
        P(split),
        P(split),
        P(None, split),
    )
    out_specs = (P(None, split, None), P(split, None, None), P(split, None, None))
    return jax.shard_map(
        on_device, mesh=mesh, in_specs=in_specs, out_specs=out_specs, check_vma=False
    )
```

```python
import functools

import jax
import jax.numpy as jnp
import numpy as np
from jax import lax
from jax.experimental import pallas as pl
from jax.experimental.pallas import tpu as pltpu
from jax.sharding import PartitionSpec as P

HEADS = 64
HEAD_DIM = 64
STATE = 64
STEPS = 2
EV = 8
EVENTS = STEPS * EV
INNER = HEADS * HEAD_DIM
LANES = 128
GROUP = 8
SLOTS_PER_PAIR = 2


def order_matrix():
    out = np.zeros((EVENTS * HEAD_DIM, EVENTS * HEAD_DIM), np.float32)
    t, p = np.meshgrid(np.arange(EVENTS), np.arange(HEAD_DIM), indexing="ij")
    out[t * HEAD_DIM + p, p * EVENTS + t] = 1.0
    return jnp.asarray(out, jnp.bfloat16)


MESH = pl.DeviceIdType.MESH
TILE = 256
TAPS = 4
BLOCK = 16
FIRST = 16 - EV - (TAPS - 1)
COMBINE_LAG = 2
ROUTE_LAG = 4
LIFT_LAG = 6
AHEAD = 3
CHUNKS = ((INNER, 1),) + tuple((512 * i, 2) for i in range(8))


def serve_kernel(
    n_req,
    n_fsdp,
    x_hbm,
    w_hbm,
    dt_hbm,
    cw_hbm,
    cb_hbm,
    dt_bias_hbm,
    decay_hbm,
    skip_hbm,
    gain_hbm,
    state_hbm,
    window_hbm,
    owner_hbm,
    slot_hbm,
    count_hbm,
    order_hbm,
    out_ref,
    sorted_hbm,
    columns_hbm,
    b_hbm,
    new_window_ref,
    x_ref,
    dt_ref,
    cw_ref,
    cb_ref,
    dt_bias_ref,
    decay_ref,
    skip_ref,
    gain_ref,
    window_ref,
    owner_ref,
    slot_ref,
    count_ref,
    order_ref,
    state_buf,
    strips,
    x_all,
    w_all,
    own_sum,
    part_out,
    part_in,
    sum_out,
    sum_in,
    pack,
    packed,
    items,
    meta,
    meta_in,
    placing,
    live,
    by_slot,
    win_in,
    win_out,
    ext,
    stacked,
    table,
    columns,
    gains,
    a_rows,
    a_sorted,
    b_save,
    y_read,
    y_part,
    y_out,
    y_back,
    y_rows,
    flat,
    fetch_sems,
    load_sems,
    state_sem,
    out_sems,
    x_send,
    x_recv,
    w_send,
    w_recv,
    f_send,
    f_recv,
    p_send,
    p_recv,
    s_send,
    s_recv,
    i_send,
    i_recv,
    m_send,
    m_recv,
    y_send,
    y_recv,
):
    f32, bf16, i32 = jnp.float32, jnp.bfloat16, jnp.int32
    rows = x_ref.shape[0]
    users = rows // EVENTS
    depth, channels = w_hbm.shape
    cached = state_buf.shape[0]
    chips = n_req // 2
    pairs = n_fsdp // 2
    n_items = items.shape[0]
    me_r, me_z = lax.axis_index("req"), lax.axis_index("fsdp")
    me_chip, core = me_r // 2, me_r % 2
    me_pair, side = me_z // 2, me_z % 2
    sibling = {"req": me_chip * 2 + 1 - core}

    def at_req(shift):
        return lax.rem(me_r + shift + n_req, n_req)

    def at_chip(shift):
        return lax.rem(me_chip + shift + chips, chips) * 2 + core

    def at_fsdp(pair, other):
        return lax.rem(me_pair + pair + pairs, pairs) * 2 + (1 - side if other else side)

    chunks = range(len(CHUNKS))
    fsdp_shifts = [(d, o) for d in range(pairs) for o in (0, 1)][1:]

    def remote(src, dst, send, recv, device):
        return pltpu.make_async_remote_copy(
            src_ref=src,
            dst_ref=dst,
            send_sem=send,
            recv_sem=recv,
            device_id=device,
            device_id_type=MESH,
        )

    def x_copy(d, o):
        i = d * 2 + o
        target = at_fsdp(d, o)
        return remote(strips.at[target], x_all.at[i], x_send.at[i], x_recv.at[i], {"fsdp": target})

    def m_copy(d):
        target = at_req(d)
        return remote(
            meta.at[target], meta_in.at[me_r], m_send.at[d], m_recv.at[d], {"req": target}
        )

    def y_copy(d):
        target = at_req(d)
        return remote(
            y_out.at[target], y_back.at[me_r], y_send.at[d], y_recv.at[d], {"req": target}
        )

    def cols(c):
        return pl.ds(CHUNKS[c][0], CHUNKS[c][1] * TILE)

    def w_copy(c, d):
        piece = w_all.at[me_r, :, cols(c)]
        return remote(piece, piece, w_send.at[c, d], w_recv.at[c, d], {"req": at_chip(d)})

    def w_forward(c, d):
        piece = w_all.at[at_chip(-d), :, cols(c)]
        return remote(piece, piece, f_send.at[c, d], f_recv.at[c, d], sibling)

    def p_copy(c, d):
        return remote(
            part_out.at[d, :, cols(c)],
            part_in.at[d, :, cols(c)],
            p_send.at[c, d],
            p_recv.at[c, d],
            {"fsdp": at_fsdp(0, 1)},
        )

    def s_copy(c, d):
        return remote(
            sum_out.at[d, :, cols(c)],
            sum_in.at[d, :, cols(c)],
            s_send.at[c, d],
            s_recv.at[c, d],
            {"fsdp": at_fsdp(-d, 0)},
        )

    def i_copy(c, d):
        target = at_req(d)
        return remote(
            packed.at[pl.ds(target * SLOTS_PER_PAIR, SLOTS_PER_PAIR), :, cols(c)],
            items.at[pl.ds(me_r * SLOTS_PER_PAIR, SLOTS_PER_PAIR), :, cols(c)],
            i_send.at[c, d],
            i_recv.at[c, d],
            {"req": target},
        )

    def load(c):
        width = min(CHUNKS[c][1] * TILE, channels - CHUNKS[c][0])
        at = pl.ds(CHUNKS[c][0], width)
        return pltpu.make_async_copy(w_hbm.at[:, at], w_all.at[me_r, :, at], load_sems.at[c])

    early = [
        pltpu.make_async_copy(a, b, fetch_sems.at[i])
        for i, (a, b) in enumerate(
            [
                (x_hbm, x_ref),
                (dt_hbm, dt_ref),
                (owner_hbm, owner_ref),
                (slot_hbm, slot_ref),
                (count_hbm, count_ref),
            ]
        )
    ]
    late = [
        pltpu.make_async_copy(a, b, fetch_sems.at[5 + i])
        for i, (a, b) in enumerate(
            [
                (cw_hbm, cw_ref),
                (cb_hbm, cb_ref),
                (dt_bias_hbm, dt_bias_ref),
                (decay_hbm, decay_ref),
                (skip_hbm, skip_ref),
                (gain_hbm, gain_ref),
                (window_hbm, window_ref),
            ]
        )
    ]
    fetch_state = pltpu.make_async_copy(state_hbm, state_buf, state_sem)
    fetch_order = pltpu.make_async_copy(order_hbm, order_ref, fetch_sems.at[5 + len(late)])
    keep_columns = pltpu.make_async_copy(columns, columns_hbm, out_sems.at[0])
    keep_writes = pltpu.make_async_copy(b_save, b_hbm, out_sems.at[1])

    def keep_block(block):
        return pltpu.make_async_copy(
            a_sorted.at[block], sorted_hbm.at[block], out_sems.at[2 + block]
        )

    barrier = pltpu.get_barrier_semaphore()
    partners = [{"req": at_req(d)} for d in range(1, n_req)]
    partners += [{"fsdp": at_fsdp(d, o)} for d, o in fsdp_shifts]
    for partner in partners:
        pl.semaphore_signal(barrier, inc=1, device_id=partner, device_id_type=MESH)
    early[0].start()
    load(0).start()
    for copy in early[1:]:
        copy.start()
    for c in chunks[1:]:
        load(c).start()
    for copy in early:
        copy.wait()
    for z in range(n_fsdp):
        for r in range(n_req):
            at = (r * n_fsdp + z) * depth
            strips[z, :, r * depth : (r + 1) * depth] = x_ref[:, at : at + depth]
    x_all[0] = strips[me_z]
    if dt_ref.shape[0] == depth:
        step_columns = jnp.concatenate(
            [dt_ref[...], jnp.zeros((depth, LANES - HEADS), bf16)], axis=1
        )
    else:
        step_columns = jnp.concatenate(
            [dt_ref[...].astype(f32), jnp.zeros((LANES - HEADS, depth), f32)], axis=0
        ).T.astype(bf16)
    w_all[me_r, :, channels:] = step_columns
    pl.semaphore_wait(barrier, len(partners))
    for d, o in fsdp_shifts:
        x_copy(d, o).start()

    def spread(c):
        load(c).wait()
        for d in range(1, chips):
            w_copy(c, d).start()
        w_forward(c, 0).start()

    for c in chunks[:AHEAD]:
        spread(c)
    for copy in late:
        copy.start()
    fetch_state.start()
    fetch_order.start()

    owner = [owner_ref[0:1, u : u + 1] for u in range(users)]
    rank = ranks(owner)
    high, wide = pack.shape
    row = lax.broadcasted_iota(i32, (high, wide), 0)
    col = lax.broadcasted_iota(i32, (high, wide), 1)
    user = (col // EV) % users
    hit = jnp.zeros((high, wide), jnp.bool_)
    pair_row = row // EVENTS
    for u in range(users):
        hit = hit | ((pair_row == owner[u] * SLOTS_PER_PAIR + rank[u]) & (user == u))
    same = (row % EV == col % EV) & ((row // EV) % STEPS == col // (EV * users))
    pack[...] = jnp.where(hit & same, 1.0, 0.0).astype(bf16)
    row = lax.broadcasted_iota(i32, (n_req * 8, LANES), 0)
    lane = lax.broadcasted_iota(i32, (n_req * 8, LANES), 1)
    notes = jnp.zeros((n_req * 8, LANES), i32)
    for u in range(users):
        note = jnp.where(lane == 0, slot_ref[0:1, u : u + 1] + 1, 0)
        for s in range(STEPS):
            note = jnp.where(lane == 1 + s, count_ref[s : s + 1, u : u + 1], note)
        notes = jnp.where(row == owner[u] * 8 + rank[u], note, notes)
    meta[...] = notes.reshape(meta.shape)
    for d in range(1, n_req):
        m_copy(d).start()
    meta_in[me_r] = meta[me_r]

    left = lax.broadcasted_iota(i32, (1, LANES), 1) < HEAD_DIM
    lane64 = lax.broadcasted_iota(i32, (1, LANES), 1) % HEAD_DIM
    row8 = lax.broadcasted_iota(i32, (EV, 1), 0)
    row16 = lax.broadcasted_iota(i32, (16, 1), 0)

    def both_halves(v):
        turned = pltpu.roll(v, HEAD_DIM, 1)
        return jnp.where(left, v, turned), jnp.where(left, turned, v)

    def prepare():
        for copy in late:
            copy.wait()
        win_in[...] = jnp.zeros(win_in.shape, f32)
        ext[...] = jnp.zeros(ext.shape, f32)
        for i in range(TAPS - 1):
            old = window_ref[i].astype(f32)
            for u in range(cached):
                win_in[u, FIRST + i : FIRST + i + 1, :] = old[u : u + 1]
        table[...] = jnp.zeros(table.shape, f32)
        y_part[...] = jnp.zeros(y_part.shape, f32)
        gain = gain_ref[...].reshape(1, INNER)
        for j in range(INNER // LANES):
            first, second = both_halves(gain[:, j * LANES : (j + 1) * LANES])
            gains[2 * j : 2 * j + 1, :] = first
            gains[2 * j + 1 : 2 * j + 2, :] = second

    def find_rows():
        for d in range(1, n_req):
            m_copy(d).wait_recv()
        slots = lax.broadcasted_iota(i32, (cached, 1), 0)
        counts = jnp.zeros((cached, LANES), i32)
        item = lax.broadcasted_iota(i32, (1, n_items * EVENTS), 1) // EVENTS
        goal = jnp.zeros((1, n_items * EVENTS), i32) - 1
        for i in range(n_items):
            note = meta_in[i // SLOTS_PER_PAIR, i % SLOTS_PER_PAIR : i % SLOTS_PER_PAIR + 1, :]
            slot = note[:, 0:1] - 1
            counts = jnp.where(slots == slot, note, counts)
            goal = jnp.where(item == i, slot, goal)
        live[...] = counts
        shape = (cached * EVENTS, n_items * EVENTS)
        row = lax.broadcasted_iota(i32, shape, 0)
        col = lax.broadcasted_iota(i32, shape, 1)
        match = (row // EVENTS == goal) & (row % EVENTS == col % EVENTS)
        placing[...] = jnp.where(match, 1.0, 0.0).astype(bf16)

    def forward(c):
        for d in range(1, chips):
            w_copy(c, d).wait_recv()
            w_forward(c, d).start()

    def tiles(c, body):
        def step(i, carry):
            body(pl.ds(pl.multiple_of(CHUNKS[c][0] + i * TILE, TILE), TILE))
            return carry

        lax.fori_loop(0, CHUNKS[c][1], step, 0)

    def multiply(c):
        for d in range(chips):
            w_forward(c, d).wait_recv()

        def tile(at):
            part = jnp.dot(
                x_all[...].reshape(n_fsdp * rows, n_req * depth),
                w_all[:, :, at].reshape(n_req * depth, TILE),
                preferred_element_type=f32,
            )
            for d in range(pairs):
                own_sum[d, :, at] = part[2 * d * rows : (2 * d + 1) * rows]
                part_out[d, :, at] = part[(2 * d + 1) * rows : (2 * d + 2) * rows].astype(bf16)

        tiles(c, tile)
        for d in (*range(1, pairs), 0):
            p_copy(c, d).start()

    def combine(c):
        for d in range(1, pairs):
            p_copy(c, d).wait_recv()

        def tile(at):
            for d in range(1, pairs):
                sum_out[d, :, at] = (own_sum[d, :, at] + part_in[d, :, at].astype(f32)).astype(bf16)

        tiles(c, tile)
        for d in range(1, pairs):
            s_copy(c, d).start()

    def route(c):
        p_copy(c, 0).wait_recv()
        for d in range(1, pairs):
            s_copy(c, d).wait_recv()

        def tile(at):
            total = own_sum[0, :, at] + part_in[0, :, at].astype(f32)
            for d in range(1, pairs):
                total = total + sum_in[d, :, at].astype(f32)
            chosen = jnp.dot(pack[...], total.astype(bf16), preferred_element_type=f32)
            packed[:, :, at] = chosen.reshape(-1, EVENTS, TILE).astype(bf16)
            for i in range(SLOTS_PER_PAIR):
                mine = me_r * SLOTS_PER_PAIR + i
                items[mine, :, at] = packed[mine, :, at]

        tiles(c, tile)
        for d in range(1, n_req):
            i_copy(c, d).start()

    def arrive(c):
        for d in range(1, n_req):
            i_copy(c, d).wait_recv()

        def tile(at):
            by_slot[:, at] = jnp.dot(
                placing[...],
                items[:, :, at].reshape(n_items * EVENTS, TILE),
                preferred_element_type=f32,
            ).astype(bf16)

        tiles(c, tile)

    def counts_of(u):
        note = live[pl.ds(u, 1), :]
        return [note[:, 1 + s : 2 + s] for s in range(STEPS)]

    def convolve(u, start, width):
        at = slice(start, start + width)
        counts = counts_of(u)
        mine = by_slot[pl.ds(pl.multiple_of(u * EVENTS, EVENTS), EVENTS), at].astype(f32)
        ext[0, 0:EV, :width] = win_in[u, :, at]
        bias = cb_ref[...].reshape(1, channels)[:, at]
        actives = []
        for s in range(STEPS):
            ext[s, EV : 2 * EV, :width] = mine[s * EV : (s + 1) * EV]
            conv = bias + cw_ref[0:1, at] * ext[s, FIRST : FIRST + EV, :width]
            for tap in range(1, TAPS):
                begin = FIRST + tap
                conv = conv + cw_ref[tap : tap + 1, at] * ext[s, begin : begin + EV, :width]
            actives.append(conv * (1.0 / (1.0 + jnp.exp(-conv))))
            whole = ext[s, :, :width]
            for i in range(TAPS - 1):
                wanted = (row16 == counts[s] + FIRST + i) & (row16 >= FIRST)
                kept = jnp.sum(jnp.where(wanted, whole, 0.0), axis=0, keepdims=True)
                if s + 1 < STEPS:
                    ext[s + 1, FIRST + i : FIRST + i + 1, :width] = kept
                else:
                    win_out[u, i : i + 1, at] = kept
        return actives

    def weigh(u, carry):
        counts = counts_of(u)
        actives = convolve(u, INNER, 2 * STATE)
        at = pl.ds(pl.multiple_of(u * EVENTS, EVENTS), EVENTS)
        raws = by_slot[at, channels : channels + LANES].astype(f32)[:, :HEADS]
        dt_bias = dt_bias_ref[...].reshape(1, HEADS)
        decay = decay_ref[...].reshape(1, HEADS)
        skip = skip_ref[...].reshape(1, HEADS)
        weights, totals, reads, writes, picks = [], [], [], [], []
        for s in range(STEPS):
            raw = raws[s * EV : (s + 1) * EV] + dt_bias
            size = jnp.maximum(raw, 0.0) + jnp.log1p(jnp.exp(-jnp.abs(raw)))
            size = jnp.where(row8 < counts[s], size, 0.0)
            cum = -decay * size
            for shift in (1, 2, 4):
                cum = cum + jnp.where(row8 >= shift, pltpu.roll(cum, shift, 0), 0.0)
            total = cum[EV - 1 : EV, :]
            totals.append(total)
            weights.append(jnp.exp(total - cum) * size)
            picks.append((row8 == counts[s] - 1).astype(f32))
            writes.append(actives[s][:, :STATE])
            reads.append(jnp.sum(picks[s] * actives[s][:, STATE:], axis=0, keepdims=True))
        carried = weights[0] * jnp.exp(totals[1])

        def gram(s, e):
            return jnp.sum(writes[e] * reads[s], axis=1, keepdims=True)

        table[0:8, 0:64] = weights[0] * gram(0, 0) + picks[0] * skip
        table[8:16, 0:64] = carried * gram(1, 0)
        table[16:24, 0:64] = weights[1] * gram(1, 1) + picks[1] * skip
        table[24:32, 0:64] = carried
        table[32:40, 0:64] = weights[1]
        table[40:41, 0:64] = jnp.exp(totals[0])
        table[41:42, 0:64] = jnp.exp(totals[0] + totals[1])
        table[42:43, 0:64] = reads[0]
        table[43:44, 0:64] = reads[1]
        columns[u] = table[...].T[0:64]
        for s in range(STEPS):
            b_save[u, s * EV : (s + 1) * EV, :] = jnp.concatenate([writes[s], writes[s]], axis=1)
        return carry

    wide = GROUP * STATE

    def read_old(u, carry):
        read = jnp.where(left, columns[u, :, 42:43], columns[u, :, 43:44])
        total = jnp.zeros((HEADS, LANES), f32)
        for q in range(HEAD_DIM // GROUP):
            read_block = jnp.concatenate(
                [jnp.where(lane64 == q * GROUP + i, read, 0.0) for i in range(GROUP)], axis=0
            ).astype(bf16)
            old = state_buf[u, :, q * wide : (q + 1) * wide]
            total = total + jnp.dot(old, read_block, preferred_element_type=f32)
        y_read[u] = jnp.where(left, columns[u, :, 40:41], columns[u, :, 41:42]) * total
        return carry

    def lift(block):
        heads = slice(block * BLOCK, (block + 1) * BLOCK)
        width = BLOCK * HEAD_DIM

        def one(u, carry):
            actives = convolve(u, block * width, width)
            for s in range(STEPS):
                for j in range(width // LANES):
                    first, second = both_halves(actives[s][:, j * LANES : (j + 1) * LANES])
                    at = 2 * j * EVENTS + s * EV
                    stacked[at : at + EV, :] = first
                    stacked[at + EVENTS : at + EVENTS + EV, :] = second
            mine = columns[u, heads, :]
            part = jnp.zeros((BLOCK, LANES), f32)
            for t in range(0, EVENTS, 2):
                pieces = []
                for e in (t, t + 1):
                    z = stacked[pl.ds(e, BLOCK, stride=EVENTS), :]
                    second = mine[:, 8 + e : 9 + e]
                    if e < EV:
                        coef = jnp.where(left, mine[:, e : e + 1], second)
                    else:
                        coef = jnp.where(left, 0.0, second)
                    part = part + coef * z
                    pieces.append(mine[:, 24 + e : 25 + e] * z)
                at = pl.multiple_of(u * BLOCK, BLOCK)
                a_rows[pl.ds(at, BLOCK), t * HEAD_DIM : (t + 2) * HEAD_DIM] = jnp.where(left, pieces[0], pieces[1]).astype(bf16)
            y_part[u, heads, :] = part
            return carry

        lax.fori_loop(0, cached, one, 0)

    def arrange(block):
        def step(q, carry):
            at = pl.ds(pl.multiple_of(q * LANES, LANES), LANES)
            a_sorted[block, q] = jnp.dot(
                a_rows[...], order_ref[:, at], preferred_element_type=f32
            ).astype(bf16)
            return carry

        lax.fori_loop(0, HEAD_DIM // GROUP, step, 0)
        keep_block(block).start()

    last = len(CHUNKS)
    blocks = HEADS // BLOCK
    ready = {}
    for c in chunks[1:]:
        done = CHUNKS[c][0] + CHUNKS[c][1] * TILE
        if done % (BLOCK * HEAD_DIM) == 0:
            ready[c] = done // (BLOCK * HEAD_DIM) - 1
    forward(0)
    prepare()
    for c in range(last + LIFT_LAG):
        if c + AHEAD < last:
            spread(c + AHEAD)
        if c + 1 < last:
            forward(c + 1)
        if c == 0:
            for d, o in fsdp_shifts:
                x_copy(d, o).wait_recv()
        if c < last:
            multiply(c)
        if 0 <= c - COMBINE_LAG < last:
            combine(c - COMBINE_LAG)
        if c == 2:
            find_rows()
        if 0 <= c - ROUTE_LAG < last:
            route(c - ROUTE_LAG)
        done = c - LIFT_LAG
        if 0 <= done < last:
            arrive(done)
        if done == 0:
            lax.fori_loop(0, cached, weigh, 0)
            keep_columns.start()
            keep_writes.start()
            fetch_state.wait()
            fetch_order.wait()
        if done == 1:
            lax.fori_loop(0, cached, read_old, 0)
        if done in ready:
            lift(ready[done])
            if ready[done] + 1 < blocks:
                arrange(ready[done])

    y_rows[...] = jnp.zeros(y_rows.shape, f32)

    def norm(u, carry):
        y = y_read[u] + y_part[u]
        square = jnp.sum(y * y, axis=0, keepdims=True)
        first = jnp.sum(jnp.where(left, square, 0.0), axis=1, keepdims=True)
        second = jnp.sum(jnp.where(left, 0.0, square), axis=1, keepdims=True)
        inverse = lax.rsqrt(jnp.where(left, first, second) * (1.0 / INNER) + 1e-05)
        y = y * inverse * gains[...]
        for i in range(n_items):
            p, k = i // SLOTS_PER_PAIR, i % SLOTS_PER_PAIR
            y_rows[i] = jnp.where(meta_in[p, k : k + 1, 0:1] == u + 1, y, y_rows[i])
        return carry

    lax.fori_loop(0, cached, norm, 0)
    y_out[...] = y_rows[...].astype(bf16).reshape(y_out.shape)
    for d in range(1, n_req):
        y_copy(d).start()
    y_back[me_r] = y_out[me_r]
    arrange(blocks - 1)
    for i in range(TAPS - 1):
        kept = [win_out[u, i : i + 1, :] for u in range(cached)]
        new_window_ref[i] = jnp.concatenate(kept, axis=0).astype(bf16)
    for d in range(1, n_req):
        m_copy(d).wait_send()
        for c in chunks:
            i_copy(c, d).wait_send()
    for d, o in fsdp_shifts:
        x_copy(d, o).wait_send()
    for c in chunks:
        for d in range(pairs):
            p_copy(c, d).wait_send()
        for d in range(1, pairs):
            s_copy(c, d).wait_send()
        w_forward(c, 0).wait_send()
        for d in range(1, chips):
            w_copy(c, d).wait_send()
            w_forward(c, d).wait_send()
    for d in range(1, n_req):
        y_copy(d).wait()
    for u in range(users):
        mine = jnp.zeros((HEADS, LANES), f32)
        for i in range(n_items):
            p, k = i // SLOTS_PER_PAIR, i % SLOTS_PER_PAIR
            hit = (owner[u] == p) & (rank[u] == k)
            mine = jnp.where(hit, y_back[p, k].astype(f32), mine)
        y_rows[u] = mine
        even = y_rows[u, pl.ds(0, HEADS // 2, stride=2), :]
        odd = y_rows[u, pl.ds(1, HEADS // 2, stride=2), :]
        steps = [
            jnp.where(left, even, pltpu.roll(odd, HEAD_DIM, 1)),
            jnp.where(left, pltpu.roll(even, HEAD_DIM, 1), odd),
        ]
        for s in range(STEPS):
            for j in range(INNER // LANES):
                flat[s, u : u + 1, j * LANES : (j + 1) * LANES] = steps[s][j : j + 1]
    out_ref[...] = flat[...].astype(bf16)
    keep_columns.wait()
    keep_writes.wait()
    for block in range(blocks):
        keep_block(block).wait()


def ranks(owner):
    out = []
    for u in range(len(owner)):
        rank = jnp.zeros((1, 1), jnp.int32)
        for earlier in owner[:u]:
            rank = rank + (earlier == owner[u]).astype(jnp.int32)
        out.append(rank)
    return out


def serve(x, in_weight, dt_weight, vectors, state, window, owner, slot, counts):
    n_req, n_fsdp = lax.axis_size("req"), lax.axis_size("fsdp")
    rows = x.shape[0]
    users = rows // EVENTS
    depth, channels = in_weight.shape
    cached = state.shape[0]
    width = max(start + tiles * TILE for start, tiles in CHUNKS)
    n_items = n_req * SLOTS_PER_PAIR
    pairs = n_fsdp // 2
    f32, bf16, i32 = jnp.float32, jnp.bfloat16, jnp.int32
    vmem, hbm = pl.BlockSpec(memory_space=pltpu.VMEM), pl.BlockSpec(memory_space=pltpu.HBM)
    dma = pltpu.SemaphoreType.DMA
    n = len(CHUNKS)
    order = order_matrix()
    arrays = (x, in_weight, dt_weight, *vectors, state, window, owner, slot, counts, order)
    sorted_shape = (HEADS // BLOCK, HEAD_DIM // GROUP, cached * BLOCK, LANES)
    fetched = (x, dt_weight, *vectors, window, owner, slot, counts, order)
    return pl.pallas_call(
        functools.partial(serve_kernel, n_req, n_fsdp),
        in_specs=[hbm] * len(arrays),
        out_specs=[vmem, hbm, hbm, hbm, vmem],
        out_shape=[
            jax.ShapeDtypeStruct((STEPS, users, INNER), bf16),
            jax.ShapeDtypeStruct(sorted_shape, bf16),
            jax.ShapeDtypeStruct((cached, HEADS, LANES), f32),
            jax.ShapeDtypeStruct((cached, EVENTS, LANES), f32),
            jax.ShapeDtypeStruct(window.shape, bf16),
        ],
        scratch_shapes=[pltpu.VMEM(a.shape, a.dtype) for a in fetched]
        + [
            pltpu.VMEM(state.shape, bf16),
            pltpu.VMEM((n_fsdp, rows, n_req * depth), bf16),
            pltpu.VMEM((n_fsdp, rows, n_req * depth), bf16),
            pltpu.VMEM((n_req, depth, width), bf16),
            pltpu.VMEM((pairs, rows, width), f32),
            pltpu.VMEM((pairs, rows, width), bf16),
            pltpu.VMEM((pairs, rows, width), bf16),
            pltpu.VMEM((pairs, rows, width), bf16),
            pltpu.VMEM((pairs, rows, width), bf16),
            pltpu.VMEM((n_items * EVENTS, rows), bf16),
            pltpu.VMEM((n_items, EVENTS, width), bf16),
            pltpu.VMEM((n_items, EVENTS, width), bf16),
            pltpu.VMEM((n_req, 8, LANES), i32),
            pltpu.VMEM((n_req, 8, LANES), i32),
            pltpu.VMEM((cached * EVENTS, n_items * EVENTS), bf16),
            pltpu.VMEM((cached, LANES), i32),
            pltpu.VMEM((cached * EVENTS, width), bf16),
            pltpu.VMEM((cached, EV, channels), f32),
            pltpu.VMEM((cached, EV, channels), f32),
            pltpu.VMEM((STEPS, 2 * EV, BLOCK * HEAD_DIM), f32),
            pltpu.VMEM((BLOCK * EVENTS, LANES), f32),
            pltpu.VMEM((LANES, LANES), f32),
            pltpu.VMEM((cached, HEADS, LANES), f32),
            pltpu.VMEM((HEADS, LANES), f32),
            pltpu.VMEM((cached * BLOCK, EVENTS * HEAD_DIM), bf16),
            pltpu.VMEM(sorted_shape, bf16),
            pltpu.VMEM((cached, EVENTS, LANES), f32),
            pltpu.VMEM((cached, HEADS, LANES), f32),
            pltpu.VMEM((cached, HEADS, LANES), f32),
            pltpu.VMEM((n_req, SLOTS_PER_PAIR, HEADS, LANES), bf16),
            pltpu.VMEM((n_req, SLOTS_PER_PAIR, HEADS, LANES), bf16),
            pltpu.VMEM((n_items, HEADS, LANES), f32),
            pltpu.VMEM((STEPS, users, INNER), f32),
            dma((len(fetched),)),
            dma((n,)),
            dma(()),
            dma((2 + HEADS // BLOCK,)),
            dma((n_fsdp,)),
            dma((n_fsdp,)),
            dma((n, n_req // 2)),
            dma((n, n_req // 2)),
            dma((n, n_req // 2)),
            dma((n, n_req // 2)),
            dma((n, pairs)),
            dma((n, pairs)),
            dma((n, pairs)),
            dma((n, pairs)),
            dma((n, n_req)),
            dma((n, n_req)),
            dma((n_req,)),
            dma((n_req,)),
            dma((n_req,)),
            dma((n_req,)),
        ],
        compiler_params=pltpu.CompilerParams(
            collective_id=0, has_side_effects=True, vmem_limit_bytes=60 * 2**20
        ),
        cost_estimate=pl.CostEstimate(flops=7 * 10**9, bytes_accessed=10**7, transcendentals=0),
        name="serve",
    )(*arrays)


def store_kernel(
    state_hbm,
    sorted_hbm,
    columns_hbm,
    b_hbm,
    window_hbm,
    out_hbm,
    new_state_hbm,
    new_window_hbm,
    final_hbm,
    a_sorted,
    columns,
    writes,
    window_buf,
    out_buf,
    state_buf,
    fetch_sems,
    pass_sems,
    in_sems,
    out_sems,
):
    f32, bf16 = jnp.float32, jnp.bfloat16
    cached = state_buf.shape[0]
    groups = HEAD_DIM // GROUP
    wide = GROUP * STATE

    def state_in(u):
        return pltpu.make_async_copy(state_hbm.at[u], state_buf.at[u], in_sems.at[u])

    def state_out(u):
        return pltpu.make_async_copy(state_buf.at[u], new_state_hbm.at[u], out_sems.at[u])

    pairs = [
        (b_hbm, writes),
        (columns_hbm, columns),
        (sorted_hbm, a_sorted),
        (window_hbm, window_buf),
        (out_hbm, out_buf),
    ]
    passed = [(window_buf, new_window_hbm), (out_buf, final_hbm)]
    passes = [pltpu.make_async_copy(a, b, pass_sems.at[i]) for i, (a, b) in enumerate(passed)]
    copies = [pltpu.make_async_copy(a, b, fetch_sems.at[i]) for i, (a, b) in enumerate(pairs)]
    for copy in copies:
        copy.start()
    for u in range(cached):
        state_in(u).start()
    shape = (GROUP * EVENTS, wide)
    diagonal = lax.broadcasted_iota(jnp.int32, shape, 0) // EVENTS == (
        lax.broadcasted_iota(jnp.int32, shape, 1) // STATE
    )
    for copy in copies[:3]:
        copy.wait()
    for copy, onward in zip(copies[3:], passes):
        copy.wait()
        onward.start()

    def update(u, carry):
        b_wide = jnp.concatenate([writes[u]] * (wide // LANES), axis=1)
        b_block = jnp.where(diagonal, jnp.concatenate([b_wide] * GROUP, axis=0), 0.0)
        lhs = a_sorted[:, :, pl.ds(pl.multiple_of(u * BLOCK, BLOCK), BLOCK), :]
        change = jnp.dot(
            lhs.reshape(groups * HEADS, LANES), b_block.astype(bf16), preferred_element_type=f32
        )
        state_in(u).wait()
        for block in range(HEADS // BLOCK):
            heads = slice(block * BLOCK, (block + 1) * BLOCK)
            decay = columns[u, heads, 41:42]
            for q in range(groups):
                at = slice(q * wide, (q + 1) * wide)
                row = (block * groups + q) * BLOCK
                old = state_buf[u, heads, at].astype(f32)
                state_buf[u, heads, at] = (decay * old + change[row : row + BLOCK]).astype(bf16)
        state_out(u).start()
        return carry

    lax.fori_loop(0, cached, update, 0, unroll=2)
    for onward in passes:
        onward.wait()
    for u in range(cached):
        state_out(u).wait()


def store(state, a_sorted, columns, b_save, window, out):
    hbm = pl.BlockSpec(memory_space=pltpu.HBM)
    cached = state.shape[0]
    return pl.pallas_call(
        store_kernel,
        in_specs=[hbm] * 6,
        out_specs=[hbm] * 3,
        out_shape=[jax.ShapeDtypeStruct(a.shape, a.dtype) for a in (state, window, out)],
        scratch_shapes=[
            pltpu.VMEM(a_sorted.shape, a_sorted.dtype),
            pltpu.VMEM(columns.shape, columns.dtype),
            pltpu.VMEM(b_save.shape, b_save.dtype),
            pltpu.VMEM(window.shape, window.dtype),
            pltpu.VMEM(out.shape, out.dtype),
            pltpu.VMEM(state.shape, jnp.bfloat16),
            pltpu.SemaphoreType.DMA((5,)),
            pltpu.SemaphoreType.DMA((2,)),
            pltpu.SemaphoreType.DMA((cached,)),
            pltpu.SemaphoreType.DMA((cached,)),
        ],
        compiler_params=pltpu.CompilerParams(vmem_limit_bytes=60 * 2**20),
        cost_estimate=pl.CostEstimate(flops=10**9, bytes_accessed=10**7, transcendentals=0),
        name="store",
    )(state, a_sorted, columns, b_save, window, out)


def on_device(
    tokens,
    in_weight,
    dt_weight,
    conv_weight,
    conv_bias,
    dt_bias,
    decay_rate,
    skip_gain,
    norm_gain,
    state_cache,
    conv_cache,
    hash_owner,
    cache_slot,
    event_counts,
):
    users = tokens.shape[1]
    if in_weight.shape[0] % LANES == 0:
        dt_weight = dt_weight.T
    vectors = (conv_weight, conv_bias, dt_bias, decay_rate, skip_gain, norm_gain)
    window = conv_cache.transpose(1, 0, 2)
    out, a_sorted, columns, b_save, new_window = serve(
        tokens.reshape(STEPS * users * EV, -1),
        in_weight,
        dt_weight,
        vectors,
        state_cache,
        window,
        hash_owner[None],
        cache_slot[None],
        event_counts,
    )
    new_state, new_window, out = store(state_cache, a_sorted, columns, b_save, new_window, out)
    return (out, new_state, new_window.transpose(1, 0, 2))


def solution(mesh):
    split = ("groups", "req", "fsdp")
    in_specs = (
        P(None, split, None, None),
        P(("req", "fsdp"), None),
        P(("req", "fsdp"), None),
        P(),
        P(),
        P(),
        P(),
        P(),
        P(),
        P(split, None, None),
        P(split, None, None),
        P(split),
        P(split),
        P(None, split),
    )
    out_specs = (P(None, split, None), P(split, None, None), P(split, None, None))
    return jax.shard_map(
        on_device, mesh=mesh, in_specs=in_specs, out_specs=out_specs, check_vma=False
    )
```

```python
import functools

import jax
import jax.numpy as jnp
import numpy as np
from jax import lax
from jax.experimental import pallas as pl
from jax.experimental.pallas import tpu as pltpu
from jax.sharding import PartitionSpec as P

HEADS = 64
HEAD_DIM = 64
STATE = 64
STEPS = 2
EV = 8
EVENTS = STEPS * EV
INNER = HEADS * HEAD_DIM
LANES = 128
GROUP = 8
SLOTS_PER_PAIR = 2


def order_matrix():
    out = np.zeros((EVENTS * HEAD_DIM, EVENTS * HEAD_DIM), np.float32)
    t, p = np.meshgrid(np.arange(EVENTS), np.arange(HEAD_DIM), indexing="ij")
    out[t * HEAD_DIM + p, p * EVENTS + t] = 1.0
    return jnp.asarray(out, jnp.bfloat16)


MESH = pl.DeviceIdType.MESH
TILE = 256
TAPS = 4
BLOCK = 16
FIRST = 16 - EV - (TAPS - 1)
COMBINE_LAG = 2
ROUTE_LAG = 4
LIFT_LAG = 6
AHEAD = 3
CHUNKS = ((INNER, 1),) + tuple((512 * i, 2) for i in range(8))


def serve_kernel(
    n_req,
    n_fsdp,
    x_hbm,
    w_hbm,
    dt_hbm,
    cw_hbm,
    cb_hbm,
    dt_bias_hbm,
    decay_hbm,
    skip_hbm,
    gain_hbm,
    state_hbm,
    window_hbm,
    owner_hbm,
    slot_hbm,
    count_hbm,
    order_hbm,
    out_ref,
    sorted_hbm,
    columns_hbm,
    b_hbm,
    new_window_ref,
    x_ref,
    dt_ref,
    cw_ref,
    cb_ref,
    dt_bias_ref,
    decay_ref,
    skip_ref,
    gain_ref,
    window_ref,
    owner_ref,
    slot_ref,
    count_ref,
    order_ref,
    state_buf,
    strips,
    x_all,
    w_all,
    own_sum,
    part_out,
    part_in,
    sum_out,
    sum_in,
    pack,
    packed,
    items,
    meta,
    meta_in,
    placing,
    live,
    by_slot,
    win_in,
    win_out,
    ext,
    stacked,
    table,
    columns,
    gains,
    a_rows,
    a_sorted,
    b_save,
    y_read,
    y_part,
    y_out,
    y_back,
    y_rows,
    flat,
    fetch_sems,
    load_sems,
    state_sem,
    out_sems,
    x_send,
    x_recv,
    w_send,
    w_recv,
    f_send,
    f_recv,
    p_send,
    p_recv,
    s_send,
    s_recv,
    i_send,
    i_recv,
    m_send,
    m_recv,
    y_send,
    y_recv,
):
    f32, bf16, i32 = jnp.float32, jnp.bfloat16, jnp.int32
    rows = x_ref.shape[0]
    users = rows // EVENTS
    depth, channels = w_hbm.shape
    cached = state_buf.shape[0]
    chips = n_req // 2
    pairs = n_fsdp // 2
    n_items = items.shape[0]
    me_r, me_z = lax.axis_index("req"), lax.axis_index("fsdp")
    me_chip, core = me_r // 2, me_r % 2
    me_pair, side = me_z // 2, me_z % 2
    sibling = {"req": me_chip * 2 + 1 - core}

    def at_req(shift):
        return lax.rem(me_r + shift + n_req, n_req)

    def at_chip(shift):
        return lax.rem(me_chip + shift + chips, chips) * 2 + core

    def at_fsdp(pair, other):
        return lax.rem(me_pair + pair + pairs, pairs) * 2 + (1 - side if other else side)

    chunks = range(len(CHUNKS))
    fsdp_shifts = [(d, o) for d in range(pairs) for o in (0, 1)][1:]

    def remote(src, dst, send, recv, device):
        return pltpu.make_async_remote_copy(
            src_ref=src,
            dst_ref=dst,
            send_sem=send,
            recv_sem=recv,
            device_id=device,
            device_id_type=MESH,
        )

    def x_copy(d, o):
        i = d * 2 + o
        target = at_fsdp(d, o)
        return remote(strips.at[target], x_all.at[i], x_send.at[i], x_recv.at[i], {"fsdp": target})

    def m_copy(d):
        target = at_req(d)
        return remote(
            meta.at[target], meta_in.at[me_r], m_send.at[d], m_recv.at[d], {"req": target}
        )

    def y_copy(d):
        target = at_req(d)
        return remote(
            y_out.at[target], y_back.at[me_r], y_send.at[d], y_recv.at[d], {"req": target}
        )

    def cols(c):
        return pl.ds(CHUNKS[c][0], CHUNKS[c][1] * TILE)

    def w_copy(c, d):
        piece = w_all.at[me_r, :, cols(c)]
        return remote(piece, piece, w_send.at[c, d], w_recv.at[c, d], {"req": at_chip(d)})

    def w_forward(c, d):
        piece = w_all.at[at_chip(-d), :, cols(c)]
        return remote(piece, piece, f_send.at[c, d], f_recv.at[c, d], sibling)

    def p_copy(c, d):
        return remote(
            part_out.at[d, :, cols(c)],
            part_in.at[d, :, cols(c)],
            p_send.at[c, d],
            p_recv.at[c, d],
            {"fsdp": at_fsdp(0, 1)},
        )

    def s_copy(c, d):
        return remote(
            sum_out.at[d, :, cols(c)],
            sum_in.at[d, :, cols(c)],
            s_send.at[c, d],
            s_recv.at[c, d],
            {"fsdp": at_fsdp(-d, 0)},
        )

    def i_copy(c, d):
        target = at_req(d)
        return remote(
            packed.at[pl.ds(target * SLOTS_PER_PAIR, SLOTS_PER_PAIR), :, cols(c)],
            items.at[pl.ds(me_r * SLOTS_PER_PAIR, SLOTS_PER_PAIR), :, cols(c)],
            i_send.at[c, d],
            i_recv.at[c, d],
            {"req": target},
        )

    def load(c):
        width = min(CHUNKS[c][1] * TILE, channels - CHUNKS[c][0])
        at = pl.ds(CHUNKS[c][0], width)
        return pltpu.make_async_copy(w_hbm.at[:, at], w_all.at[me_r, :, at], load_sems.at[c])

    early = [
        pltpu.make_async_copy(a, b, fetch_sems.at[i])
        for i, (a, b) in enumerate(
            [
                (x_hbm, x_ref),
                (dt_hbm, dt_ref),
                (owner_hbm, owner_ref),
                (slot_hbm, slot_ref),
                (count_hbm, count_ref),
            ]
        )
    ]
    late = [
        pltpu.make_async_copy(a, b, fetch_sems.at[5 + i])
        for i, (a, b) in enumerate(
            [
                (cw_hbm, cw_ref),
                (cb_hbm, cb_ref),
                (dt_bias_hbm, dt_bias_ref),
                (decay_hbm, decay_ref),
                (skip_hbm, skip_ref),
                (gain_hbm, gain_ref),
                (window_hbm, window_ref),
            ]
        )
    ]
    fetch_state = pltpu.make_async_copy(state_hbm, state_buf, state_sem)
    fetch_order = pltpu.make_async_copy(order_hbm, order_ref, fetch_sems.at[5 + len(late)])
    keep_columns = pltpu.make_async_copy(columns, columns_hbm, out_sems.at[0])
    keep_writes = pltpu.make_async_copy(b_save, b_hbm, out_sems.at[1])

    def keep_block(block):
        return pltpu.make_async_copy(
            a_sorted.at[block], sorted_hbm.at[block], out_sems.at[2 + block]
        )

    barrier = pltpu.get_barrier_semaphore()
    partners = [{"req": at_req(d)} for d in range(1, n_req)]
    partners += [{"fsdp": at_fsdp(d, o)} for d, o in fsdp_shifts]
    for partner in partners:
        pl.semaphore_signal(barrier, inc=1, device_id=partner, device_id_type=MESH)
    early[0].start()
    load(0).start()
    for copy in early[1:]:
        copy.start()
    for c in chunks[1:]:
        load(c).start()
    for copy in early:
        copy.wait()
    for z in range(n_fsdp):
        for r in range(n_req):
            at = (r * n_fsdp + z) * depth
            strips[z, :, r * depth : (r + 1) * depth] = x_ref[:, at : at + depth]
    x_all[0] = strips[me_z]
    if dt_ref.shape[0] == depth:
        step_columns = jnp.concatenate(
            [dt_ref[...], jnp.zeros((depth, LANES - HEADS), bf16)], axis=1
        )
    else:
        step_columns = jnp.concatenate(
            [dt_ref[...].astype(f32), jnp.zeros((LANES - HEADS, depth), f32)], axis=0
        ).T.astype(bf16)
    w_all[me_r, :, channels:] = step_columns
    pl.semaphore_wait(barrier, len(partners))
    for d, o in fsdp_shifts:
        x_copy(d, o).start()

    def spread(c):
        load(c).wait()
        for d in range(1, chips):
            w_copy(c, d).start()
        w_forward(c, 0).start()

    for c in chunks[:AHEAD]:
        spread(c)
    for copy in late:
        copy.start()
    fetch_state.start()
    fetch_order.start()

    owner = [owner_ref[0:1, u : u + 1] for u in range(users)]
    rank = ranks(owner)
    high, wide = pack.shape
    row = lax.broadcasted_iota(i32, (high, wide), 0)
    col = lax.broadcasted_iota(i32, (high, wide), 1)
    user = (col // EV) % users
    hit = jnp.zeros((high, wide), jnp.bool_)
    pair_row = row // EVENTS
    for u in range(users):
        hit = hit | ((pair_row == owner[u] * SLOTS_PER_PAIR + rank[u]) & (user == u))
    same = (row % EV == col % EV) & ((row // EV) % STEPS == col // (EV * users))
    pack[...] = jnp.where(hit & same, 1.0, 0.0).astype(bf16)
    row = lax.broadcasted_iota(i32, (n_req * 8, LANES), 0)
    lane = lax.broadcasted_iota(i32, (n_req * 8, LANES), 1)
    notes = jnp.zeros((n_req * 8, LANES), i32)
    for u in range(users):
        note = jnp.where(lane == 0, slot_ref[0:1, u : u + 1] + 1, 0)
        for s in range(STEPS):
            note = jnp.where(lane == 1 + s, count_ref[s : s + 1, u : u + 1], note)
        notes = jnp.where(row == owner[u] * 8 + rank[u], note, notes)
    meta[...] = notes.reshape(meta.shape)
    for d in range(1, n_req):
        m_copy(d).start()
    meta_in[me_r] = meta[me_r]

    left = lax.broadcasted_iota(i32, (1, LANES), 1) < HEAD_DIM
    lane64 = lax.broadcasted_iota(i32, (1, LANES), 1) % HEAD_DIM
    row8 = lax.broadcasted_iota(i32, (EV, 1), 0)
    row16 = lax.broadcasted_iota(i32, (16, 1), 0)

    def both_halves(v):
        turned = pltpu.roll(v, HEAD_DIM, 1)
        return jnp.where(left, v, turned), jnp.where(left, turned, v)

    def prepare():
        for copy in late:
            copy.wait()
        win_in[...] = jnp.zeros(win_in.shape, f32)
        ext[...] = jnp.zeros(ext.shape, f32)
        for i in range(TAPS - 1):
            old = window_ref[i].astype(f32)
            for u in range(cached):
                win_in[u, FIRST + i : FIRST + i + 1, :] = old[u : u + 1]
        table[...] = jnp.zeros(table.shape, f32)
        y_part[...] = jnp.zeros(y_part.shape, f32)
        gain = gain_ref[...].reshape(1, INNER)
        for j in range(INNER // LANES):
            first, second = both_halves(gain[:, j * LANES : (j + 1) * LANES])
            gains[2 * j : 2 * j + 1, :] = first
            gains[2 * j + 1 : 2 * j + 2, :] = second

    def find_rows():
        for d in range(1, n_req):
            m_copy(d).wait_recv()
        slots = lax.broadcasted_iota(i32, (cached, 1), 0)
        counts = jnp.zeros((cached, LANES), i32)
        item = lax.broadcasted_iota(i32, (1, n_items * EVENTS), 1) // EVENTS
        goal = jnp.zeros((1, n_items * EVENTS), i32) - 1
        for i in range(n_items):
            note = meta_in[i // SLOTS_PER_PAIR, i % SLOTS_PER_PAIR : i % SLOTS_PER_PAIR + 1, :]
            slot = note[:, 0:1] - 1
            counts = jnp.where(slots == slot, note, counts)
            goal = jnp.where(item == i, slot, goal)
        live[...] = counts
        shape = (cached * EVENTS, n_items * EVENTS)
        row = lax.broadcasted_iota(i32, shape, 0)
        col = lax.broadcasted_iota(i32, shape, 1)
        match = (row // EVENTS == goal) & (row % EVENTS == col % EVENTS)
        placing[...] = jnp.where(match, 1.0, 0.0).astype(bf16)

    def forward(c):
        for d in range(1, chips):
            w_copy(c, d).wait_recv()
            w_forward(c, d).start()

    def tiles(c, body):
        def step(i, carry):
            body(pl.ds(pl.multiple_of(CHUNKS[c][0] + i * TILE, TILE), TILE))
            return carry

        lax.fori_loop(0, CHUNKS[c][1], step, 0)

    def multiply(c):
        for d in range(chips):
            w_forward(c, d).wait_recv()

        def tile(at):
            part = jnp.dot(
                x_all[...].reshape(n_fsdp * rows, n_req * depth),
                w_all[:, :, at].reshape(n_req * depth, TILE),
                preferred_element_type=f32,
            )
            for d in range(pairs):
                own_sum[d, :, at] = part[2 * d * rows : (2 * d + 1) * rows]
                part_out[d, :, at] = part[(2 * d + 1) * rows : (2 * d + 2) * rows].astype(bf16)

        tiles(c, tile)
        for d in (*range(1, pairs), 0):
            p_copy(c, d).start()

    def combine(c):
        for d in range(1, pairs):
            p_copy(c, d).wait_recv()

        def tile(at):
            for d in range(1, pairs):
                sum_out[d, :, at] = (own_sum[d, :, at] + part_in[d, :, at].astype(f32)).astype(bf16)

        tiles(c, tile)
        for d in range(1, pairs):
            s_copy(c, d).start()

    def route(c):
        p_copy(c, 0).wait_recv()
        for d in range(1, pairs):
            s_copy(c, d).wait_recv()

        def tile(at):
            total = own_sum[0, :, at] + part_in[0, :, at].astype(f32)
            for d in range(1, pairs):
                total = total + sum_in[d, :, at].astype(f32)
            chosen = jnp.dot(pack[...], total.astype(bf16), preferred_element_type=f32)
            packed[:, :, at] = chosen.reshape(-1, EVENTS, TILE).astype(bf16)
            for i in range(SLOTS_PER_PAIR):
                mine = me_r * SLOTS_PER_PAIR + i
                items[mine, :, at] = packed[mine, :, at]

        tiles(c, tile)
        for d in range(1, n_req):
            i_copy(c, d).start()

    def arrive(c):
        for d in range(1, n_req):
            i_copy(c, d).wait_recv()

        def tile(at):
            by_slot[:, at] = jnp.dot(
                placing[...],
                items[:, :, at].reshape(n_items * EVENTS, TILE),
                preferred_element_type=f32,
            ).astype(bf16)

        tiles(c, tile)

    def counts_of(u):
        note = live[pl.ds(u, 1), :]
        return [note[:, 1 + s : 2 + s] for s in range(STEPS)]

    def convolve(u, start, width):
        at = slice(start, start + width)
        counts = counts_of(u)
        mine = by_slot[pl.ds(pl.multiple_of(u * EVENTS, EVENTS), EVENTS), at].astype(f32)
        ext[0, 0:EV, :width] = win_in[u, :, at]
        bias = cb_ref[...].reshape(1, channels)[:, at]
        actives = []
        for s in range(STEPS):
            ext[s, EV : 2 * EV, :width] = mine[s * EV : (s + 1) * EV]
            conv = bias + cw_ref[0:1, at] * ext[s, FIRST : FIRST + EV, :width]
            for tap in range(1, TAPS):
                begin = FIRST + tap
                conv = conv + cw_ref[tap : tap + 1, at] * ext[s, begin : begin + EV, :width]
            actives.append(conv * (1.0 / (1.0 + jnp.exp(-conv))))
            whole = ext[s, :, :width]
            for i in range(TAPS - 1):
                wanted = (row16 == counts[s] + FIRST + i) & (row16 >= FIRST)
                kept = jnp.sum(jnp.where(wanted, whole, 0.0), axis=0, keepdims=True)
                if s + 1 < STEPS:
                    ext[s + 1, FIRST + i : FIRST + i + 1, :width] = kept
                else:
                    win_out[u, i : i + 1, at] = kept
        return actives

    def weigh(u, carry):
        counts = counts_of(u)
        actives = convolve(u, INNER, 2 * STATE)
        at = pl.ds(pl.multiple_of(u * EVENTS, EVENTS), EVENTS)
        raws = by_slot[at, channels : channels + LANES].astype(f32)[:, :HEADS]
        dt_bias = dt_bias_ref[...].reshape(1, HEADS)
        decay = decay_ref[...].reshape(1, HEADS)
        skip = skip_ref[...].reshape(1, HEADS)
        weights, totals, reads, writes, picks = [], [], [], [], []
        for s in range(STEPS):
            raw = raws[s * EV : (s + 1) * EV] + dt_bias
            size = jnp.maximum(raw, 0.0) + jnp.log1p(jnp.exp(-jnp.abs(raw)))
            size = jnp.where(row8 < counts[s], size, 0.0)
            cum = -decay * size
            for shift in (1, 2, 4):
                cum = cum + jnp.where(row8 >= shift, pltpu.roll(cum, shift, 0), 0.0)
            total = cum[EV - 1 : EV, :]
            totals.append(total)
            weights.append(jnp.exp(total - cum) * size)
            picks.append((row8 == counts[s] - 1).astype(f32))
            writes.append(actives[s][:, :STATE])
            reads.append(jnp.sum(picks[s] * actives[s][:, STATE:], axis=0, keepdims=True))
        carried = weights[0] * jnp.exp(totals[1])

        def gram(s, e):
            return jnp.sum(writes[e] * reads[s], axis=1, keepdims=True)

        table[0:8, 0:64] = weights[0] * gram(0, 0) + picks[0] * skip
        table[8:16, 0:64] = carried * gram(1, 0)
        table[16:24, 0:64] = weights[1] * gram(1, 1) + picks[1] * skip
        table[24:32, 0:64] = carried
        table[32:40, 0:64] = weights[1]
        table[40:41, 0:64] = jnp.exp(totals[0])
        table[41:42, 0:64] = jnp.exp(totals[0] + totals[1])
        table[42:43, 0:64] = reads[0]
        table[43:44, 0:64] = reads[1]
        columns[u] = table[...].T[0:64]
        for s in range(STEPS):
            b_save[u, s * EV : (s + 1) * EV, :] = jnp.concatenate([writes[s], writes[s]], axis=1)
        return carry

    wide = GROUP * STATE

    def read_old(u, carry):
        read = jnp.where(left, columns[u, :, 42:43], columns[u, :, 43:44])
        total = jnp.zeros((HEADS, LANES), f32)
        for q in range(HEAD_DIM // GROUP):
            read_block = jnp.concatenate(
                [jnp.where(lane64 == q * GROUP + i, read, 0.0) for i in range(GROUP)], axis=0
            ).astype(bf16)
            old = state_buf[u, :, q * wide : (q + 1) * wide]
            total = total + jnp.dot(old, read_block, preferred_element_type=f32)
        y_read[u] = jnp.where(left, columns[u, :, 40:41], columns[u, :, 41:42]) * total
        return carry

    def lift(block):
        heads = slice(block * BLOCK, (block + 1) * BLOCK)
        width = BLOCK * HEAD_DIM

        def one(u, carry):
            actives = convolve(u, block * width, width)
            for s in range(STEPS):
                for j in range(width // LANES):
                    first, second = both_halves(actives[s][:, j * LANES : (j + 1) * LANES])
                    at = 2 * j * EVENTS + s * EV
                    stacked[at : at + EV, :] = first
                    stacked[at + EVENTS : at + EVENTS + EV, :] = second
            mine = columns[u, heads, :]
            part = jnp.zeros((BLOCK, LANES), f32)
            for t in range(0, EVENTS, 2):
                pieces = []
                for e in (t, t + 1):
                    z = stacked[pl.ds(e, BLOCK, stride=EVENTS), :]
                    second = mine[:, 8 + e : 9 + e]
                    if e < EV:
                        coef = jnp.where(left, mine[:, e : e + 1], second)
                    else:
                        coef = jnp.where(left, 0.0, second)
                    part = part + coef * z
                    pieces.append(mine[:, 24 + e : 25 + e] * z)
                at = pl.multiple_of(u * BLOCK, BLOCK)
                a_rows[pl.ds(at, BLOCK), t * HEAD_DIM : (t + 2) * HEAD_DIM] = jnp.where(left, pieces[0], pieces[1]).astype(bf16)
            y_part[u, heads, :] = part
            return carry

        lax.fori_loop(0, cached, one, 0)

    def arrange(block):
        def step(q, carry):
            at = pl.ds(pl.multiple_of(q * LANES, LANES), LANES)
            a_sorted[block, q] = jnp.dot(
                a_rows[...], order_ref[:, at], preferred_element_type=f32
            ).astype(bf16)
            return carry

        lax.fori_loop(0, HEAD_DIM // GROUP, step, 0)
        keep_block(block).start()

    last = len(CHUNKS)
    blocks = HEADS // BLOCK
    ready = {}
    for c in chunks[1:]:
        done = CHUNKS[c][0] + CHUNKS[c][1] * TILE
        if done % (BLOCK * HEAD_DIM) == 0:
            ready[c] = done // (BLOCK * HEAD_DIM) - 1
    forward(0)
    prepare()
    for c in range(last + LIFT_LAG):
        if c + AHEAD < last:
            spread(c + AHEAD)
        if c + 1 < last:
            forward(c + 1)
        if c == 0:
            for d, o in fsdp_shifts:
                x_copy(d, o).wait_recv()
        if c < last:
            multiply(c)
        if 0 <= c - COMBINE_LAG < last:
            combine(c - COMBINE_LAG)
        if c == 2:
            find_rows()
        if 0 <= c - ROUTE_LAG < last:
            route(c - ROUTE_LAG)
        done = c - LIFT_LAG
        if 0 <= done < last:
            arrive(done)
        if done == 0:
            lax.fori_loop(0, cached, weigh, 0)
            keep_columns.start()
            keep_writes.start()
            fetch_state.wait()
            fetch_order.wait()
        if done == 1:
            lax.fori_loop(0, cached // 2, read_old, 0)
        if done == 3:
            lax.fori_loop(cached // 2, cached, read_old, 0)
        if done in ready:
            lift(ready[done])
            if ready[done] + 1 < blocks:
                arrange(ready[done])

    y_rows[...] = jnp.zeros(y_rows.shape, f32)

    def norm(u, carry):
        y = y_read[u] + y_part[u]
        square = jnp.sum(y * y, axis=0, keepdims=True)
        first = jnp.sum(jnp.where(left, square, 0.0), axis=1, keepdims=True)
        second = jnp.sum(jnp.where(left, 0.0, square), axis=1, keepdims=True)
        inverse = lax.rsqrt(jnp.where(left, first, second) * (1.0 / INNER) + 1e-05)
        y = y * inverse * gains[...]
        for i in range(n_items):
            p, k = i // SLOTS_PER_PAIR, i % SLOTS_PER_PAIR
            y_rows[i] = jnp.where(meta_in[p, k : k + 1, 0:1] == u + 1, y, y_rows[i])
        return carry

    lax.fori_loop(0, cached, norm, 0)
    y_out[...] = y_rows[...].astype(bf16).reshape(y_out.shape)
    for d in range(1, n_req):
        y_copy(d).start()
    y_back[me_r] = y_out[me_r]
    arrange(blocks - 1)
    for i in range(TAPS - 1):
        kept = [win_out[u, i : i + 1, :] for u in range(cached)]
        new_window_ref[i] = jnp.concatenate(kept, axis=0).astype(bf16)
    for d in range(1, n_req):
        m_copy(d).wait_send()
        for c in chunks:
            i_copy(c, d).wait_send()
    for d, o in fsdp_shifts:
        x_copy(d, o).wait_send()
    for c in chunks:
        for d in range(pairs):
            p_copy(c, d).wait_send()
        for d in range(1, pairs):
            s_copy(c, d).wait_send()
        w_forward(c, 0).wait_send()
        for d in range(1, chips):
            w_copy(c, d).wait_send()
            w_forward(c, d).wait_send()
    for d in range(1, n_req):
        y_copy(d).wait()
    for u in range(users):
        mine = jnp.zeros((HEADS, LANES), f32)
        for i in range(n_items):
            p, k = i // SLOTS_PER_PAIR, i % SLOTS_PER_PAIR
            hit = (owner[u] == p) & (rank[u] == k)
            mine = jnp.where(hit, y_back[p, k].astype(f32), mine)
        y_rows[u] = mine
        even = y_rows[u, pl.ds(0, HEADS // 2, stride=2), :]
        odd = y_rows[u, pl.ds(1, HEADS // 2, stride=2), :]
        steps = [
            jnp.where(left, even, pltpu.roll(odd, HEAD_DIM, 1)),
            jnp.where(left, pltpu.roll(even, HEAD_DIM, 1), odd),
        ]
        for s in range(STEPS):
            for j in range(INNER // LANES):
                flat[s, u : u + 1, j * LANES : (j + 1) * LANES] = steps[s][j : j + 1]
    out_ref[...] = flat[...].astype(bf16)
    keep_columns.wait()
    keep_writes.wait()
    for block in range(blocks):
        keep_block(block).wait()


def ranks(owner):
    out = []
    for u in range(len(owner)):
        rank = jnp.zeros((1, 1), jnp.int32)
        for earlier in owner[:u]:
            rank = rank + (earlier == owner[u]).astype(jnp.int32)
        out.append(rank)
    return out


def serve(x, in_weight, dt_weight, vectors, state, window, owner, slot, counts):
    n_req, n_fsdp = lax.axis_size("req"), lax.axis_size("fsdp")
    rows = x.shape[0]
    users = rows // EVENTS
    depth, channels = in_weight.shape
    cached = state.shape[0]
    width = max(start + tiles * TILE for start, tiles in CHUNKS)
    n_items = n_req * SLOTS_PER_PAIR
    pairs = n_fsdp // 2
    f32, bf16, i32 = jnp.float32, jnp.bfloat16, jnp.int32
    vmem, hbm = pl.BlockSpec(memory_space=pltpu.VMEM), pl.BlockSpec(memory_space=pltpu.HBM)
    dma = pltpu.SemaphoreType.DMA
    n = len(CHUNKS)
    order = order_matrix()
    arrays = (x, in_weight, dt_weight, *vectors, state, window, owner, slot, counts, order)
    sorted_shape = (HEADS // BLOCK, HEAD_DIM // GROUP, cached * BLOCK, LANES)
    fetched = (x, dt_weight, *vectors, window, owner, slot, counts, order)
    return pl.pallas_call(
        functools.partial(serve_kernel, n_req, n_fsdp),
        in_specs=[hbm] * len(arrays),
        out_specs=[vmem, hbm, hbm, hbm, vmem],
        out_shape=[
            jax.ShapeDtypeStruct((STEPS, users, INNER), bf16),
            jax.ShapeDtypeStruct(sorted_shape, bf16),
            jax.ShapeDtypeStruct((cached, HEADS, LANES), f32),
            jax.ShapeDtypeStruct((cached, EVENTS, LANES), f32),
            jax.ShapeDtypeStruct(window.shape, bf16),
        ],
        scratch_shapes=[pltpu.VMEM(a.shape, a.dtype) for a in fetched]
        + [
            pltpu.VMEM(state.shape, bf16),
            pltpu.VMEM((n_fsdp, rows, n_req * depth), bf16),
            pltpu.VMEM((n_fsdp, rows, n_req * depth), bf16),
            pltpu.VMEM((n_req, depth, width), bf16),
            pltpu.VMEM((pairs, rows, width), f32),
            pltpu.VMEM((pairs, rows, width), bf16),
            pltpu.VMEM((pairs, rows, width), bf16),
            pltpu.VMEM((pairs, rows, width), bf16),
            pltpu.VMEM((pairs, rows, width), bf16),
            pltpu.VMEM((n_items * EVENTS, rows), bf16),
            pltpu.VMEM((n_items, EVENTS, width), bf16),
            pltpu.VMEM((n_items, EVENTS, width), bf16),
            pltpu.VMEM((n_req, 8, LANES), i32),
            pltpu.VMEM((n_req, 8, LANES), i32),
            pltpu.VMEM((cached * EVENTS, n_items * EVENTS), bf16),
            pltpu.VMEM((cached, LANES), i32),
            pltpu.VMEM((cached * EVENTS, width), bf16),
            pltpu.VMEM((cached, EV, channels), f32),
            pltpu.VMEM((cached, EV, channels), f32),
            pltpu.VMEM((STEPS, 2 * EV, BLOCK * HEAD_DIM), f32),
            pltpu.VMEM((BLOCK * EVENTS, LANES), f32),
            pltpu.VMEM((LANES, LANES), f32),
            pltpu.VMEM((cached, HEADS, LANES), f32),
            pltpu.VMEM((HEADS, LANES), f32),
            pltpu.VMEM((cached * BLOCK, EVENTS * HEAD_DIM), bf16),
            pltpu.VMEM(sorted_shape, bf16),
            pltpu.VMEM((cached, EVENTS, LANES), f32),
            pltpu.VMEM((cached, HEADS, LANES), f32),
            pltpu.VMEM((cached, HEADS, LANES), f32),
            pltpu.VMEM((n_req, SLOTS_PER_PAIR, HEADS, LANES), bf16),
            pltpu.VMEM((n_req, SLOTS_PER_PAIR, HEADS, LANES), bf16),
            pltpu.VMEM((n_items, HEADS, LANES), f32),
            pltpu.VMEM((STEPS, users, INNER), f32),
            dma((len(fetched),)),
            dma((n,)),
            dma(()),
            dma((2 + HEADS // BLOCK,)),
            dma((n_fsdp,)),
            dma((n_fsdp,)),
            dma((n, n_req // 2)),
            dma((n, n_req // 2)),
            dma((n, n_req // 2)),
            dma((n, n_req // 2)),
            dma((n, pairs)),
            dma((n, pairs)),
            dma((n, pairs)),
            dma((n, pairs)),
            dma((n, n_req)),
            dma((n, n_req)),
            dma((n_req,)),
            dma((n_req,)),
            dma((n_req,)),
            dma((n_req,)),
        ],
        compiler_params=pltpu.CompilerParams(
            collective_id=0, has_side_effects=True, vmem_limit_bytes=60 * 2**20
        ),
        cost_estimate=pl.CostEstimate(flops=7 * 10**9, bytes_accessed=10**7, transcendentals=0),
        name="serve",
    )(*arrays)


def store_kernel(
    state_hbm,
    sorted_hbm,
    columns_hbm,
    b_hbm,
    window_hbm,
    out_hbm,
    new_state_hbm,
    new_window_hbm,
    final_hbm,
    a_sorted,
    columns,
    writes,
    window_buf,
    out_buf,
    state_buf,
    fetch_sems,
    pass_sems,
    in_sems,
    out_sems,
):
    f32, bf16 = jnp.float32, jnp.bfloat16
    cached = state_buf.shape[0]
    groups = HEAD_DIM // GROUP
    wide = GROUP * STATE

    def state_in(u):
        return pltpu.make_async_copy(state_hbm.at[u], state_buf.at[u], in_sems.at[u])

    def state_out(u):
        return pltpu.make_async_copy(state_buf.at[u], new_state_hbm.at[u], out_sems.at[u])

    pairs = [
        (b_hbm, writes),
        (columns_hbm, columns),
        (sorted_hbm, a_sorted),
        (window_hbm, window_buf),
        (out_hbm, out_buf),
    ]
    passed = [(window_buf, new_window_hbm), (out_buf, final_hbm)]
    passes = [pltpu.make_async_copy(a, b, pass_sems.at[i]) for i, (a, b) in enumerate(passed)]
    copies = [pltpu.make_async_copy(a, b, fetch_sems.at[i]) for i, (a, b) in enumerate(pairs)]
    for copy in copies:
        copy.start()
    for u in range(cached):
        state_in(u).start()
    shape = (GROUP * EVENTS, wide)
    diagonal = lax.broadcasted_iota(jnp.int32, shape, 0) // EVENTS == (
        lax.broadcasted_iota(jnp.int32, shape, 1) // STATE
    )
    for copy in copies[:3]:
        copy.wait()
    for copy, onward in zip(copies[3:], passes):
        copy.wait()
        onward.start()

    def update(u, carry):
        b_wide = jnp.concatenate([writes[u]] * (wide // LANES), axis=1)
        b_block = jnp.where(diagonal, jnp.concatenate([b_wide] * GROUP, axis=0), 0.0)
        lhs = a_sorted[:, :, pl.ds(pl.multiple_of(u * BLOCK, BLOCK), BLOCK), :]
        change = jnp.dot(
            lhs.reshape(groups * HEADS, LANES), b_block.astype(bf16), preferred_element_type=f32
        )
        state_in(u).wait()
        for block in range(HEADS // BLOCK):
            heads = slice(block * BLOCK, (block + 1) * BLOCK)
            decay = columns[u, heads, 41:42]
            for q in range(groups):
                at = slice(q * wide, (q + 1) * wide)
                row = (block * groups + q) * BLOCK
                old = state_buf[u, heads, at].astype(f32)
                state_buf[u, heads, at] = (decay * old + change[row : row + BLOCK]).astype(bf16)
        state_out(u).start()
        return carry

    lax.fori_loop(0, cached, update, 0, unroll=4)
    for onward in passes:
        onward.wait()
    for u in range(cached):
        state_out(u).wait()


def store(state, a_sorted, columns, b_save, window, out):
    hbm = pl.BlockSpec(memory_space=pltpu.HBM)
    cached = state.shape[0]
    return pl.pallas_call(
        store_kernel,
        in_specs=[hbm] * 6,
        out_specs=[hbm] * 3,
        out_shape=[jax.ShapeDtypeStruct(a.shape, a.dtype) for a in (state, window, out)],
        scratch_shapes=[
            pltpu.VMEM(a_sorted.shape, a_sorted.dtype),
            pltpu.VMEM(columns.shape, columns.dtype),
            pltpu.VMEM(b_save.shape, b_save.dtype),
            pltpu.VMEM(window.shape, window.dtype),
            pltpu.VMEM(out.shape, out.dtype),
            pltpu.VMEM(state.shape, jnp.bfloat16),
            pltpu.SemaphoreType.DMA((5,)),
            pltpu.SemaphoreType.DMA((2,)),
            pltpu.SemaphoreType.DMA((cached,)),
            pltpu.SemaphoreType.DMA((cached,)),
        ],
        compiler_params=pltpu.CompilerParams(vmem_limit_bytes=60 * 2**20),
        cost_estimate=pl.CostEstimate(flops=10**9, bytes_accessed=10**7, transcendentals=0),
        name="store",
    )(state, a_sorted, columns, b_save, window, out)


def on_device(
    tokens,
    in_weight,
    dt_weight,
    conv_weight,
    conv_bias,
    dt_bias,
    decay_rate,
    skip_gain,
    norm_gain,
    state_cache,
    conv_cache,
    hash_owner,
    cache_slot,
    event_counts,
):
    users = tokens.shape[1]
    if in_weight.shape[0] % LANES == 0:
        dt_weight = dt_weight.T
    vectors = (conv_weight, conv_bias, dt_bias, decay_rate, skip_gain, norm_gain)
    window = conv_cache.transpose(1, 0, 2)
    out, a_sorted, columns, b_save, new_window = serve(
        tokens.reshape(STEPS * users * EV, -1),
        in_weight,
        dt_weight,
        vectors,
        state_cache,
        window,
        hash_owner[None],
        cache_slot[None],
        event_counts,
    )
    new_state, new_window, out = store(state_cache, a_sorted, columns, b_save, new_window, out)
    return (out, new_state, new_window.transpose(1, 0, 2))


def solution(mesh):
    split = ("groups", "req", "fsdp")
    in_specs = (
        P(None, split, None, None),
        P(("req", "fsdp"), None),
        P(("req", "fsdp"), None),
        P(),
        P(),
        P(),
        P(),
        P(),
        P(),
        P(split, None, None),
        P(split, None, None),
        P(split),
        P(split),
        P(None, split),
    )
    out_specs = (P(None, split, None), P(split, None, None), P(split, None, None))
    return jax.shard_map(
        on_device, mesh=mesh, in_specs=in_specs, out_specs=out_specs, check_vma=False
    )
```
